32 devices in a mesh: wide: 16 (over z, y, core), narrow: 2 (over x).
Axes of the slice: x: 2, y: 2, z: 4, core: 2. Of those that a mesh axis runs over, the one named last changes fastest.
Arguments:
- tokens_short: bfloat16 [4096, 2048], P(('wide', 'narrow')), may hold values from -6 to 6
- tokens_long: bfloat16 [16384, 2048], P(('wide', 'narrow')), may hold values from -6 to 6
- cot_short: bfloat16 [4096, 2048], P(('wide', 'narrow')), may hold values from -6 to 6
- cot_long: bfloat16 [16384, 2048], P(('wide', 'narrow')), may hold values from -6 to 6
- seq_lengths: int32 [2, 32], P(None, ('wide', 'narrow')), may hold values from 64 to 512, as said below
- norm_gain: bfloat16 [2048], P(('wide', 'narrow')), may hold values from 0.25 to 1.75
- in_w: bfloat16 [2048, 8448], P(('wide', 'narrow')), may hold values from -0.125 to 0.125
- dt_w: bfloat16 [2048, 64], P(('wide', 'narrow')), may hold values from -0.125 to 0.125
- conv_w: bfloat16 [4, 4352], P(None, ('wide', 'narrow')), may hold values from -3 to 3
- conv_b: bfloat16 [4352], P(('wide', 'narrow')), may hold values from -3 to 3
- dt_bias: bfloat16 [64], replicated, may hold values from -8 to -3.5
- a_log: bfloat16 [64], replicated, may hold values from 0 to 2.796875
- d_skip: bfloat16 [64], replicated, may hold values from 0.5 to 1.5
- gate_gain: bfloat16 [4096], P(('wide', 'narrow')), may hold values from 0.25 to 1.75
- out_w: bfloat16 [4096, 2048], P(('wide', 'narrow')), may hold values from -0.09375 to 0.09375
Outputs:
- out_short: bfloat16 [4096, 2048], P(('wide', 'narrow'))
- out_long: bfloat16 [16384, 2048], P(('wide', 'narrow'))
- grad_short: float32 [4096, 2048], P(('wide', 'narrow'))
- grad_long: float32 [16384, 2048], P(('wide', 'narrow'))
- grad_norm_gain: float32 [2048], P(('wide', 'narrow'))
- grad_in_w: float32 [2048, 8448], P(('wide', 'narrow'))
- grad_dt_w: float32 [2048, 64], P(('wide', 'narrow'))
- grad_conv_w: float32 [4, 4352], P(None, ('wide', 'narrow'))
- grad_conv_b: float32 [4352], P(('wide', 'narrow'))
- grad_dt_bias: float32 [64], replicated
- grad_a_log: float32 [64], replicated
- grad_d_skip: float32 [64], replicated
- grad_gate_gain: float32 [4096], P(('wide', 'narrow'))
- grad_out_w: float32 [4096, 2048], P(('wide', 'narrow'))
The draws below stay inside these ranges and needn't reach their ends.
Inputs may be any that keep to these rules, and one draw needn't show every extreme that they name: `seq_lengths`: row 0 lies between 64 and 128, row 1 between 256 and 512; in each row some slot is full.
All inputs are finite; a program needn't handle non-finite values.
Results may differ from the reference program's by a relative error of at most 0.0085.
Values may be sent and summed in bfloat16 or wider, within the bound.
No kernel may reach another device: no remote copies, remote signals or barrier semaphores. Data moves between devices by JAX's collectives and lax.ppermute only.
A program may use at most 448 MiB of HBM per device.

```python
from functools import partial
import jax
import jax.numpy as jnp
from jax import lax

D = 2048
DI = 4096
HEADS = 64
HEAD_DIM = 64
STATE = 128
KERNEL = 4
SPAN = 256
SHORT = 128
LONG = 512
SEQS = 32


def draw_seq_lengths(key, part):
    key_short, key_long, key_full = jax.random.split(key, 3)
    short_len = jax.random.randint(key_short, (SEQS,), SHORT // 2, SHORT + 1)
    long_len = jax.random.randint(key_long, (SEQS,), LONG // 2, LONG + 1)
    fullest = jax.random.randint(key_full, (2,), 0, SEQS)
    places = jnp.arange(SEQS)
    short_len = jnp.where(places == fullest[0], SHORT, short_len)
    long_len = jnp.where(places == fullest[1], LONG, long_len)
    return jnp.stack([short_len, long_len]).astype(jnp.int32)


def shard_levels(key, extent, shards, smallest, top_value):
    def one(dim, blocks):
        draws = jax.random.uniform(jax.random.fold_in(jax.random.fold_in(key, 6), dim), (blocks,), jnp.float32, smallest / len(shards), top_value / len(shards))
        return jnp.repeat(jnp.exp(draws), extent[dim] // blocks).reshape((-1,) + (1,) * (len(extent) - dim - 1))

    loudness = one(*shards[0])
    for cut in shards[1:]:
        loudness = loudness * one(*cut)
    return loudness


def scatter_about(own_key, shape, scale, bound, cuts=(), dtype=jnp.bfloat16):
    drawn = scale * jax.random.normal(own_key, shape, jnp.float32)
    if cuts:
        drawn = drawn * shard_levels(own_key, shape, cuts, -0.22, 0.18)
    return jnp.clip(drawn, -bound, bound).astype(dtype)


def setup_inputs(seed: int = 0) -> dict:
    seeds = jax.random.split(jax.random.key(seed), 16)
    tokens_short = scatter_about(seeds[0], (SEQS * SHORT, D), 1.0, 6.0, ((0, 32),))
    tokens_long = scatter_about(seeds[1], (SEQS * LONG, D), 1.0, 6.0, ((0, 32),))
    cot_short = scatter_about(seeds[2], (SEQS * SHORT, D), 1.0, 6.0, ((0, 32),))
    cot_long = scatter_about(seeds[3], (SEQS * LONG, D), 1.0, 6.0, ((0, 32),))
    seq_lengths = draw_seq_lengths(jax.random.fold_in(seeds[15], 71), 0)
    norm_gain = jnp.clip(1.0 + 0.15 * jax.random.normal(seeds[5], (D,), jnp.float32), 0.25, 1.75).astype(jnp.bfloat16)
    in_w = scatter_about(seeds[6], (D, 2 * DI + 2 * STATE), D ** -0.5, 0.125, ((0, 32),))
    dt_w = scatter_about(seeds[7], (D, HEADS), D ** -0.5, 0.125, ((0, 32),))
    conv_w = scatter_about(seeds[8], (KERNEL, DI + 2 * STATE), KERNEL ** -0.5, 3.0, ((1, 32),))
    conv_b = scatter_about(seeds[9], (DI + 2 * STATE,), 0.5, 3.0, ((0, 32),))
    dt_bias = jnp.clip(jax.random.uniform(seeds[10], (HEADS,), jnp.float32, -8.0, -3.5), -8.0, -3.5).astype(jnp.bfloat16)
    a_log = jnp.clip(jax.random.uniform(seeds[11], (HEADS,), jnp.float32, 0.0, 2.796875), 0.0, 2.796875).astype(jnp.bfloat16)
    d_skip = jnp.clip(jax.random.uniform(seeds[12], (HEADS,), jnp.float32, 0.5, 1.5), 0.5, 1.5).astype(jnp.bfloat16)
    gate_gain = jnp.clip(1.0 + 0.15 * jax.random.normal(seeds[13], (DI,), jnp.float32), 0.25, 1.75).astype(jnp.bfloat16)
    out_w = scatter_about(seeds[14], (DI, D), DI ** -0.5, 0.09375, ((0, 32),))
    return dict(tokens_short=tokens_short, tokens_long=tokens_long, cot_short=cot_short, cot_long=cot_long, seq_lengths=seq_lengths, norm_gain=norm_gain, in_w=in_w, dt_w=dt_w, conv_w=conv_w, conv_b=conv_b, dt_bias=dt_bias, a_log=a_log, d_skip=d_skip, gate_gain=gate_gain, out_w=out_w)


EPS = 1e-05
HIGHEST = lax.Precision.HIGHEST

@jax.custom_vjp
def low(v):
    return lax.optimization_barrier(v.astype(jnp.bfloat16)).astype(jnp.float32)

@jax.custom_vjp
def low_back(v):
    return v

def low_keep(v):
    return (low(v), None)

def low_pass(kept, grad):
    return (grad,)

def back_keep(v):
    return (v, None)

def back_low(kept, grad):
    return (low(grad),)
low.defvjp(low_keep, low_pass)
low_back.defvjp(back_keep, back_low)

def silu_of(values):
    return values * jax.nn.sigmoid(values)

def causal_conv(values, kernel):
    kernel_len = kernel.shape[0]
    seq_len = values.shape[0]
    padded = jnp.concatenate([jnp.zeros((kernel_len - 1, values.shape[1]), jnp.float32), values], axis=0)
    return sum((kernel[offset] * padded[offset:offset + seq_len] for offset in range(kernel_len)))

def span_parts(b_block, c_block, dt_block, neg_rate):
    block_len = dt_block.shape[-1]
    places = jnp.arange(block_len)
    upper_ones = (places[:, None] <= places[None, :]).astype(jnp.float32)
    causal = places[:, None] >= places[None, :]
    cumulative = jnp.dot(dt_block * neg_rate[:, None], upper_ones, precision=HIGHEST)
    spread = cumulative[:, :, None] - cumulative[:, None, :]
    decays = jnp.where(causal[None], jnp.exp(jnp.where(causal[None], spread, 0.0)), 0.0)
    scores = jnp.dot(c_block, b_block.T, precision=HIGHEST)
    weights = jnp.exp(cumulative[:, -1:] - cumulative) * dt_block
    return (upper_ones, cumulative, decays, scores, weights)

def span_forward(state_in, inputs, neg_rate):
    x_block, b_block, c_block, dt_block = inputs
    upper_ones, cumulative, decays, scores, weights = span_parts(b_block, c_block, dt_block, neg_rate)
    mixing = scores[None] * decays * dt_block[:, None, :]
    inside = jnp.einsum('hij,hjp->hip', mixing, x_block, precision=HIGHEST)
    carried = jnp.exp(cumulative)[:, :, None] * jnp.einsum('in,hpn->hip', c_block, state_in, precision=HIGHEST)
    state_out = jnp.exp(cumulative[:, -1])[:, None, None] * state_in + jnp.einsum('hjp,jn->hpn', weights[:, :, None] * x_block, b_block, precision=HIGHEST)
    return (state_out, inside + carried)

def layer_seq(params, pair):
    norm_gain, in_w, dt_w, conv_w, conv_b, dt_bias, a_log, d_skip, gate_gain, out_w = params
    tokens, length = pair
    seq_len = tokens.shape[0]
    row_scale = lax.rsqrt(lax.optimization_barrier(jnp.mean(tokens * tokens, axis=-1, keepdims=True)) + EPS)
    normal_in = low(tokens * row_scale * norm_gain)
    projected = low_back(jnp.dot(normal_in, in_w, precision=HIGHEST, preferred_element_type=jnp.float32))
    dt_raw = low_back(jnp.dot(normal_in, dt_w, precision=HIGHEST, preferred_element_type=jnp.float32))
    gate_z = projected[:, :DI]
    conv_pre = causal_conv(projected[:, DI:], conv_w) + conv_b
    activated = silu_of(conv_pre)
    x_seq = low(activated[:, :DI])
    b_seq = low(activated[:, DI:DI + STATE])
    c_seq = low(activated[:, DI + STATE:])
    soft_dt = jax.nn.softplus(dt_raw + dt_bias)
    neg_rate = -jnp.exp(a_log)
    block_len = min(SPAN, seq_len)
    blocks = seq_len // block_len
    block_inputs = (x_seq.reshape(blocks, block_len, HEADS, HEAD_DIM).transpose(0, 2, 1, 3), b_seq.reshape(blocks, block_len, STATE), c_seq.reshape(blocks, block_len, STATE), soft_dt.reshape(blocks, block_len, HEADS).transpose(0, 2, 1))

    def block_step(state_in, inputs):
        return span_forward(state_in, inputs, neg_rate)
    final_state, y_blocks = lax.scan(jax.checkpoint(block_step), jnp.zeros((HEADS, HEAD_DIM, STATE), jnp.float32), block_inputs)
    y_total = y_blocks.transpose(0, 2, 1, 3).reshape(seq_len, DI) + jnp.repeat(d_skip, HEAD_DIM) * x_seq
    gated_y = y_total * silu_of(gate_z)
    gate_scale = lax.rsqrt(lax.optimization_barrier(jnp.mean(gated_y * gated_y, axis=-1, keepdims=True)) + EPS)
    normed = low(gated_y * gate_scale * gate_gain)
    branch = low_back(jnp.dot(normed, out_w, precision=HIGHEST, preferred_element_type=jnp.float32))
    live_rows = (jnp.arange(seq_len) < length).astype(jnp.float32)[:, None]
    return tokens + live_rows * branch

def reference(tokens_short, tokens_long, cot_short, cot_long, seq_lengths, norm_gain, in_w, dt_w, conv_w, conv_b, dt_bias, a_log, d_skip, gate_gain, out_w):
    params = (norm_gain.astype(jnp.float32), in_w.astype(jnp.float32), dt_w.astype(jnp.float32), conv_w.astype(jnp.float32), conv_b.astype(jnp.float32), dt_bias.astype(jnp.float32), a_log.astype(jnp.float32), d_skip.astype(jnp.float32), gate_gain.astype(jnp.float32), out_w.astype(jnp.float32))

    def forward(weight_set, short_rows, long_rows):
        one_seq = jax.checkpoint(partial(layer_seq, weight_set))
        out_first = lax.map(one_seq, (short_rows.reshape(-1, SHORT, D), seq_lengths[0]))
        out_second = lax.map(one_seq, (long_rows.reshape(-1, LONG, D), seq_lengths[1]))
        return (out_first.reshape(short_rows.shape), out_second.reshape(long_rows.shape))
    primal, pullback = jax.vjp(forward, params, tokens_short.astype(jnp.float32), tokens_long.astype(jnp.float32))
    weight_grads, grad_short, grad_long = pullback((cot_short.astype(jnp.float32), cot_long.astype(jnp.float32)))
    return (primal[0].astype(jnp.bfloat16), primal[1].astype(jnp.bfloat16), grad_short, grad_long, weight_grads[0], weight_grads[1], weight_grads[2], weight_grads[3], weight_grads[4], weight_grads[5], weight_grads[6], weight_grads[7], weight_grads[8], weight_grads[9])
```

```python
import functools

import jax
import jax.numpy as jnp
import numpy as np
from jax import lax
from jax.experimental import pallas as pl
from jax.experimental.pallas import tpu as pltpu
from jax.sharding import Mesh
from jax.sharding import PartitionSpec as P

D = 2048
DI = 4096
HEADS = 64
HEAD_DIM = 64
STATE = 128
KERNEL = 4
SPAN = 256
EPS = 1e-05
BF = jnp.bfloat16
F32 = jnp.float32

SLOTS = 4
AHEADS = 8
WIDTH = DI // SLOTS
LOCAL_HEADS = HEADS // SLOTS
XBC = WIDTH + 2 * STATE
XCOLS = XBC + 128
ALL = ("ra", "core", "rb", "x")
NEG = -1e30
TILE = 512

SWAP = [(0, 1), (1, 0)]
CYCLE = (0, 2, 4, 6, 7, 5, 3, 1)


def nt(a, b):
    return lax.dot_general(a, b, (((1,), (1,)), ((), ())), preferred_element_type=F32)


def nn(a, b):
    return lax.dot_general(a, b, (((1,), (0,)), ((), ())), preferred_element_type=F32)


def tn(a, b):
    return lax.dot_general(a, b, (((0,), (0,)), ((), ())), preferred_element_type=F32)


LOG2E = 1.4426950408889634
ROWS = 64


def sigmoid(v):
    return 0.5 * jnp.tanh(0.5 * v) + 0.5


def lane_index():
    return lax.broadcasted_iota(jnp.int32, (1, 128), 1)


def three_parts(values):
    values = jnp.where(lane_index() < LOCAL_HEADS, values, 0.0)
    high = values.astype(BF).astype(F32)
    rest = values - high
    mid = rest.astype(BF).astype(F32)
    low = rest - mid
    return (high + pltpu.roll(mid, LOCAL_HEADS, 1) + pltpu.roll(low, 2 * LOCAL_HEADS, 1)).astype(BF)


def add_parts(values):
    return values + pltpu.roll(values, 128 - LOCAL_HEADS, 1) + pltpu.roll(values, 128 - 2 * LOCAL_HEADS, 1)


def triangle(n, lower):
    i = lax.broadcasted_iota(jnp.int32, (n, n), 0)
    j = lax.broadcasted_iota(jnp.int32, (n, n), 1)
    return jnp.where(i >= j if lower else i <= j, 1.0, 0.0).astype(BF)


def running_sum(values, lower):
    return add_parts(nn(triangle(values.shape[0], lower), three_parts(values)))


def two_parts(values):
    values = jnp.where(lane_index() < LOCAL_HEADS, values, 0.0)
    high = values.astype(BF).astype(F32)
    return (high + pltpu.roll(values - high, LOCAL_HEADS, 1)).astype(BF)


def softplus(v):
    return jnp.maximum(v, 0.0) + jnp.log1p(jnp.exp(-jnp.abs(v)))


def conv_tile(p_ref, cw_ref, cb_ref, r0, seq, cols):
    starts = (r0 & (seq - 1)) == 0
    before = p_ref[pl.ds(pl.multiple_of(jnp.maximum(r0 - 8, 0), 8), 8), cols]
    before = jnp.where(starts, 0.0, before)
    here = p_ref[pl.ds(r0, ROWS), cols]
    both = jnp.concatenate([before, here], axis=0)
    back = [here] + [pltpu.roll(both, m, 0)[8:] for m in (1, 2, 3)]
    total = cb_ref[0:1, cols]
    for m in range(KERNEL):
        total = total + cw_ref[3 - m : 4 - m, cols] * back[m]
    return total, back


def fwd_kernel(
    steps_ref, p_ref, cw_ref, cb_ref, hp_ref, dsk_ref, seg_ref, bc_ref, *refs
):
    y_ref, act_ref, slope_ref, h_ref, dt_s, parts_s, grow_s, rt_s, g_s = refs[-9:]
    first = steps_ref[pl.program_id(0)] == 0
    seq = jnp.where(first, 128, 512)
    lane = lane_index()

    def conv_step(i, carry):
        r0 = pl.multiple_of(i * ROWS, ROWS)
        rows = pl.ds(r0, ROWS)
        for c in range(XBC // 128):
            cols = slice(c * 128, c * 128 + 128)
            conv, _ = conv_tile(p_ref, cw_ref, cb_ref, r0, seq, cols)
            gate = sigmoid(conv)
            act = conv * gate
            act_ref[rows, cols] = act.astype(BF)
            slope_ref[rows, cols] = (gate + act * (1.0 - gate)).astype(BF)
        dt_s[rows, :] = softplus(p_ref[rows, XBC:] + hp_ref[0:1])
        return carry

    lax.fori_loop(0, TILE // ROWS, conv_step, 0)
    rate = hp_ref[1:2]

    def block(off, q, read_state, make_state):
        rows = pl.ds(off, q)
        dt = dt_s[rows, :]
        cum2 = running_sum(dt * rate, True) * LOG2E
        parts_s[:q, :] = three_parts(cum2)
        turned = (cum2 - jnp.log2(dt)).T
        for h in range(LOCAL_HEADS):
            rt_s[h, :, :q] = turned[h : h + 1]
        b = act_ref[rows, WIDTH : WIDTH + STATE]
        c = act_ref[rows, WIDTH + STATE :]
        g_s[:q, :q] = nt(c, b)
        if read_state:
            grow_s[:q, :] = two_parts(jnp.exp2(cum2))
        if make_state:
            grow_s[:q, :] = two_parts(jnp.exp2(cum2[q - 1 : q] - cum2) * dt)
            b_turned = b.astype(F32).T.astype(BF)
        diagonal = lax.broadcasted_iota(jnp.int32, (128, 128), 0) >= lax.broadcasted_iota(
            jnp.int32, (128, 128), 1
        )

        def pair(p, carry):
            lanes = pl.ds(pl.multiple_of(p * 128, 128), 128)
            x2 = act_ref[rows, lanes]
            zero = jnp.zeros_like(x2)
            x_heads = [jnp.where(lane < HEAD_DIM, x2, zero), jnp.where(lane < HEAD_DIM, zero, x2)]
            cols = nn(parts_s[:q, :], bc_ref[:, pl.ds(pl.multiple_of(p * 256, 256), 256)])
            if read_state:
                carried = nn(grow_s[:q, :], seg_ref[:, lanes]) * nn(c, h_ref[0, :, lanes].astype(BF))
            for rt in range(q // 128):
                top = rt * 128
                mixes = []
                for j in range(2):
                    col = cols[top : top + 128, j * 128 : j * 128 + 128]
                    for ct in range(rt + 1):
                        lo = ct * 128
                        spread = col - rt_s[p * 2 + j, :, lo : lo + 128]
                        if ct == rt:
                            spread = jnp.where(diagonal, spread, NEG)
                        mixes.append((g_s[top : top + 128, lo : lo + 128] * jnp.exp2(spread)).astype(BF))
                x_both = jnp.concatenate([x[: top + 128] for x in x_heads], axis=0)
                out = nn(jnp.concatenate(mixes, axis=1), x_both)
                out = out + dsk_ref[0:1, lanes] * x2[top : top + 128].astype(F32)
                if read_state:
                    out = out + carried[top : top + 128]
                y_ref[pl.ds(off + top, 128), lanes] = out.astype(y_ref.dtype)
            if make_state:
                wide = nn(grow_s[:q, :], seg_ref[:, lanes])
                h_ref[0, :, lanes] = nn(b_turned, (wide * x2.astype(F32)).astype(BF))
            return carry

        lax.fori_loop(0, LOCAL_HEADS // 2, pair, 0)

    @pl.when(first)
    def _():
        def one(i, carry):
            block(pl.multiple_of(i * 128, 128), 128, False, False)
            return carry

        lax.fori_loop(0, TILE // 128, one, 0)

    @pl.when(jnp.logical_not(first))
    def _():
        block(0, SPAN, False, True)
        block(SPAN, SPAN, True, False)


def bwd_kernel(
    steps_ref, p_ref, act_ref, slope_ref, dy_ref, h_ref, cw_ref, hp_ref, dsk_ref, seg_ref, bc_ref, *refs
):
    dp_ref, acc_ref, hacc_ref = refs[-18:-15]
    dt_s, parts_s, grow_s, ct_s, gt_s, dgt_s, kc_s, kr_s, fold_s, dbc_s, ds_s, da_s, dst_s, after_s, sums_s = refs[-15:]
    first = steps_ref[pl.program_id(0)] == 0
    seq = jnp.where(first, 128, 512)
    lane = lane_index()
    head_row = lax.broadcasted_iota(jnp.int32, (LOCAL_HEADS, 1), 0)

    @pl.when(pl.program_id(0) == 0)
    def _():
        acc_ref[...] = jnp.zeros_like(acc_ref)
        hacc_ref[...] = jnp.zeros_like(hacc_ref)

    rate = hp_ref[1:2]
    dt_s[...] = softplus(p_ref[:, XBC:] + hp_ref[0:1])

    def block(off, q, state_in, state_out):
        rows = pl.ds(off, q)
        dt = dt_s[rows, :]
        cum2 = running_sum(dt * rate, True) * LOG2E
        parts_s[:q, :] = three_parts(cum2 - jnp.log2(dt))
        turned = cum2.T
        for h in range(LOCAL_HEADS):
            ct_s[h, :, :q] = turned[h : h + 1]
        b = act_ref[rows, WIDTH : WIDTH + STATE]
        c = act_ref[rows, WIDTH + STATE :]
        gt_s[:q, :q] = nt(b, c)
        dgt_s[:q, :q] = jnp.zeros((q, q), F32)
        kc_s[:q, :] = jnp.zeros((q, 128), F32)
        kr_s[:, :q] = jnp.zeros((LOCAL_HEADS, q), F32)
        if state_in or state_out:
            fold_s[:q, :] = jnp.zeros((q, 128), F32)
            dbc_s[:q, :] = jnp.zeros((q, 128), F32)
        if state_in:
            grow_s[:q, :] = two_parts(jnp.exp2(cum2))
            c_turned = c.astype(F32).T.astype(BF)
        if state_out:
            decay = jnp.exp2(cum2[q - 1 : q] - cum2)
            grow_s[:q, :] = two_parts(decay * dt)
        diagonal = lax.broadcasted_iota(jnp.int32, (128, 128), 1) >= lax.broadcasted_iota(
            jnp.int32, (128, 128), 0
        )
        tiles = q // 128

        def pair(p, carry):
            lanes = pl.ds(pl.multiple_of(p * 128, 128), 128)
            x2 = act_ref[rows, lanes]
            dy2 = dy_ref[rows, lanes]
            zero = jnp.zeros_like(dy2)
            dy_heads = [jnp.where(lane < HEAD_DIM, dy2, zero), jnp.where(lane < HEAD_DIM, zero, dy2)]
            cols = nn(parts_s[:q, :], bc_ref[:, pl.ds(pl.multiple_of(p * 256, 256), 256)])
            if state_in:
                hb = h_ref[0, :, lanes].astype(BF)
                dyc = dy2.astype(F32) * nn(grow_s[:q, :], seg_ref[:, lanes])
                dyb = dyc.astype(BF)
                fold_s[:q, :] += nt((dyc * nn(c, hb)).astype(BF), seg_ref[:, lanes])
                dbc_s[:q, :] += nt(dyb, hb)
                ds_s[:, lanes] = nn(c_turned, dyb).astype(BF)
            if state_out:
                sb = ds_s[:, lanes]
                wide = nn(grow_s[:q, :], seg_ref[:, lanes])
                bd = nn(b, sb)
                xf = x2.astype(F32)
                fold_s[:q, :] += nt((xf * bd).astype(BF), seg_ref[:, lanes])
                dbc_s[:q, :] += nt((wide * xf).astype(BF), sb)
                late = wide * bd
            picks = [jnp.where(lane == p * 2 + j, 1.0, 0.0).astype(BF) for j in range(2)]
            marks = [jnp.where(head_row == p * 2 + j, 1.0, 0.0).astype(BF) for j in range(2)]
            for jt in range(tiles):
                lo = jt * 128
                span = q - lo
                xj = x2[lo : lo + 128]
                mixes = []
                terms = []
                dgs = [None] * tiles
                for j in range(2):
                    col = cols[lo : lo + 128, j * 128 : j * 128 + 128]
                    for it in range(jt, tiles):
                        at = it * 128
                        spread = ct_s[p * 2 + j, :, at : at + 128] - col
                        if it == jt:
                            spread = jnp.where(diagonal, spread, NEG)
                        e = jnp.exp2(spread)
                        score = gt_s[lo : lo + 128, at : at + 128]
                        dme = nt(xj, dy_heads[j][at : at + 128]) * e
                        dgs[it] = dme if dgs[it] is None else dgs[it] + dme
                        terms.append((dme * score).astype(BF))
                        mixes.append((score * e).astype(BF))
                for it in range(jt, tiles):
                    dgt_s[lo : lo + 128, it * 128 : it * 128 + 128] += dgs[it]
                half = len(terms) // 2
                kc_s[lo : lo + 128, :] += nn(
                    jnp.concatenate(terms, axis=1),
                    jnp.concatenate([jnp.broadcast_to(v, (span, 128)) for v in picks], axis=0),
                )
                kr_s[:, lo:q] += nn(
                    jnp.concatenate([jnp.broadcast_to(v, (LOCAL_HEADS, 128)) for v in marks], axis=1),
                    jnp.concatenate(
                        [jnp.concatenate(terms[:half], axis=1), jnp.concatenate(terms[half:], axis=1)], axis=0
                    ),
                )
                dy_both = jnp.concatenate([d[lo:] for d in dy_heads], axis=0)
                out = nn(jnp.concatenate(mixes, axis=1), dy_both)
                dyj = dy2[lo : lo + 128].astype(F32)
                acc_ref[5:6, lanes] += jnp.sum(dyj * xj.astype(F32), axis=0, keepdims=True)
                out = out + dsk_ref[0:1, lanes] * dyj
                if state_out:
                    out = out + late[lo : lo + 128]
                da_s[pl.ds(off + lo, 128), lanes] = out
            return carry

        lax.fori_loop(0, LOCAL_HEADS // 2, pair, 0)

        dgt = dgt_s[:q, :q].astype(BF)
        db = nn(dgt, c)
        dc = tn(dgt, b)
        kcol = kc_s[:q, :]
        row_terms = jnp.concatenate([kr_s[:, :q], jnp.zeros((128 - LOCAL_HEADS, q), F32)], axis=0)
        d_cum = row_terms.T - kcol
        inverse = jnp.where(dt > 1e-30, 1.0 / jnp.maximum(dt, 1e-30), 0.0)
        d_dt = kcol * inverse
        if state_in:
            d_cum = d_cum + fold_s[:q, :]
            dc = dc + dbc_s[:q, :]
        if state_out:
            db = db + dbc_s[:q, :]
            d_weights = fold_s[:q, :]
            d_dt = d_dt + d_weights * decay
            w_term = d_weights * decay * dt
            last = lax.broadcasted_iota(jnp.int32, (q, 1), 0) == q - 1
            d_cum = d_cum - w_term + jnp.where(last, jnp.sum(w_term, axis=0, keepdims=True), 0.0)
        da_s[rows, WIDTH : WIDTH + STATE] = db
        da_s[rows, WIDTH + STATE :] = dc
        d_rate = running_sum(d_cum, False)
        dst_s[rows, :] = d_dt + d_rate * rate
        hacc_ref[1:2, :] += jnp.sum(d_rate * dt, axis=0, keepdims=True)

    @pl.when(first)
    def _():
        def one(i, carry):
            block(pl.multiple_of(i * 128, 128), 128, False, False)
            return carry

        lax.fori_loop(0, TILE // 128, one, 0)

    @pl.when(jnp.logical_not(first))
    def _():
        block(SPAN, SPAN, True, False)
        block(0, SPAN, False, True)

    d_soft = dst_s[...] * jax.nn.sigmoid(p_ref[:, XBC:] + hp_ref[0:1])
    d_soft = jnp.where(lane < LOCAL_HEADS, d_soft, 0.0)
    hacc_ref[0:1, :] += jnp.sum(d_soft, axis=0, keepdims=True)
    dp_ref[:, XBC:] = d_soft.astype(BF)
    sums_s[...] = jnp.zeros_like(sums_s)
    after_s[...] = jnp.zeros_like(after_s)

    def conv_step(i, carry):
        r0 = pl.multiple_of(TILE - ROWS - i * ROWS, ROWS)
        rows = pl.ds(r0, ROWS)
        ends = ((r0 + ROWS) & (seq - 1)) == 0
        fold = lambda v: jnp.sum(v.reshape(ROWS // 8, 8, 128), axis=0)
        for c in range(XBC // 128):
            cols = slice(c * 128, c * 128 + 128)
            here = p_ref[rows, cols]
            d_conv = da_s[rows, cols] * slope_ref[rows, cols].astype(F32)
            both = jnp.concatenate([d_conv, jnp.where(ends, 0.0, after_s[:, cols])], axis=0)
            after_s[:, cols] = d_conv[:8]
            total = cw_ref[3:4, cols] * d_conv
            sums_s[3, :, cols] += fold(d_conv * here)
            sums_s[4, :, cols] += fold(d_conv)
            for m in (1, 2, 3):
                ahead = pltpu.roll(both, ROWS + 8 - m, 0)[:ROWS]
                total = total + cw_ref[3 - m : 4 - m, cols] * ahead
                sums_s[3 - m, :, cols] += fold(ahead * here)
            dp_ref[rows, cols] = total.astype(BF)
        return carry

    lax.fori_loop(0, TILE // ROWS, conv_step, 0)
    for k in range(KERNEL + 1):
        acc_ref[k : k + 1, :] += jnp.sum(sums_s[k], axis=0, keepdims=True)


def stats_kernel(order_ref, y_ref, z_ref, dn_ref, gain_ref, st_ref, both_s):
    lane = lane_index()

    def step(i, carry):
        rows = pl.ds(pl.multiple_of(i * ROWS, ROWS), ROWS)
        p1 = jnp.zeros((ROWS, 128), F32)
        p2 = jnp.zeros((ROWS, 128), F32)
        for k in range(AHEADS):
            lanes = pl.ds(pl.multiple_of(order_ref[k] * 128, 128), 128)
            z = z_ref[rows, lanes].astype(F32)
            g = y_ref[rows, lanes].astype(F32) * (z * sigmoid(z))
            p1 = p1 + g * g
            p2 = p2 + g * (dn_ref[rows, k * 128 : k * 128 + 128].astype(F32) * gain_ref[0:1, lanes])
        both_s[rows, :] = jnp.where(
            lane == 0,
            jnp.sum(p1, axis=1, keepdims=True),
            jnp.where(lane == 1, jnp.sum(p2, axis=1, keepdims=True), 0.0),
        )
        return carry

    lax.fori_loop(0, y_ref.shape[0] // ROWS, step, 0)
    st_ref[...] = both_s[...].T[0:8]


def gate_kernel(order_ref, st_ref, y_ref, z_ref, dn_ref, gain_ref, n_ref, dy_ref, dz_ref, st_s):
    st_s[...] = jnp.concatenate([st_ref[...], jnp.zeros((120, y_ref.shape[0]), F32)], axis=0).T

    def step(i, carry):
        rows = pl.ds(pl.multiple_of(i * ROWS, ROWS), ROWS)
        st = st_s[rows, :]
        rg = lax.rsqrt(st[:, 0:1] * (1.0 / DI) + EPS)
        mean = rg * rg * st[:, 1:2] * (1.0 / DI)
        for k in range(AHEADS):
            lanes = pl.ds(pl.multiple_of(order_ref[k] * 128, 128), 128)
            fixed = slice(k * 128, k * 128 + 128)
            gain = gain_ref[0:1, lanes]
            z = z_ref[rows, lanes].astype(F32)
            y = y_ref[rows, lanes].astype(F32)
            sg = sigmoid(z)
            silu = z * sg
            ghat = y * silu * rg
            dg = rg * (dn_ref[rows, fixed].astype(F32) * gain) - ghat * mean
            n_ref[rows, fixed] = (ghat * gain).astype(BF)
            dy_ref[rows, lanes] = (dg * silu).astype(BF)
            dz_ref[rows, lanes] = (dg * y * (sg + silu * (1.0 - sg))).astype(BF)
        return carry

    lax.fori_loop(0, y_ref.shape[0] // ROWS, step, 0)


def norm_kernel(pieces, order_ref, *refs):
    gain_ref, u_ref = refs[pieces], refs[-1]
    at = 0
    for x_ref in refs[:pieces]:
        count = x_ref.shape[0] // ROWS

        def step(i, carry, x_ref=x_ref, at=at):
            rows = pl.ds(pl.multiple_of(i * ROWS, ROWS), ROWS)
            out = pl.ds(pl.multiple_of(at + i * ROWS, ROWS), ROWS)
            total = jnp.zeros((ROWS, 128), F32)
            for k in range(D // 128):
                v = x_ref[rows, k * 128 : k * 128 + 128].astype(F32)
                total = total + v * v
            scale = lax.rsqrt(jnp.sum(total, axis=1, keepdims=True) * (1.0 / D) + EPS)
            for k in range(AHEADS):
                lanes = pl.ds(pl.multiple_of(order_ref[k] * 256, 256), 256)
                u_ref[out, k * 256 : k * 256 + 256] = (
                    x_ref[rows, lanes].astype(F32) * scale * gain_ref[0:1, lanes]
                ).astype(BF)
            return carry

        lax.fori_loop(0, count, step, 0)
        at += x_ref.shape[0]


def whole(shape):
    return pl.BlockSpec(shape, lambda i, s: (0,) * len(shape))


def placed(cols):
    return pl.BlockSpec((TILE, cols), lambda i, s: (s[i], 0))


def params():
    return pltpu.CompilerParams(vmem_limit_bytes=56 * 1024 * 1024)


def onto(earlier, first_input):
    specs = [pl.BlockSpec(memory_space=pl.ANY)] * len(earlier)
    return list(earlier), specs, {first_input + i: i for i in range(len(earlier))}


STATES = pl.BlockSpec((1, STATE, WIDTH), lambda i, s: (s[i], 0, 0))


def ssd_forward(steps, proj, conv_w, conv_b, heads, skip, seg, spread, earlier=()):
    tokens = proj.shape[0]
    count = len(steps)
    more, more_specs, aliases = onto(earlier, 8)
    return pl.pallas_call(
        fwd_kernel,
        grid_spec=pltpu.PrefetchScalarGridSpec(
            num_scalar_prefetch=1,
            grid=(count,),
            in_specs=[
                placed(XCOLS), whole((8, XBC)), whole((8, XBC)), whole((8, 128)), whole((8, WIDTH)),
                whole((128, WIDTH)), whole((128, 128 * LOCAL_HEADS)), *more_specs,
            ],
            out_specs=[placed(WIDTH), placed(XBC), placed(XBC), STATES],
            scratch_shapes=[
                pltpu.VMEM((TILE, 128), F32),
                pltpu.VMEM((SPAN, 128), BF),
                pltpu.VMEM((SPAN, 128), BF),
                pltpu.VMEM((LOCAL_HEADS, 1, SPAN), F32),
                pltpu.VMEM((SPAN, SPAN), F32),
            ],
        ),
        out_shape=[
            jax.ShapeDtypeStruct((tokens, WIDTH), BF),
            jax.ShapeDtypeStruct((tokens, XBC), BF),
            jax.ShapeDtypeStruct((tokens, XBC), BF),
            jax.ShapeDtypeStruct((tokens // TILE, STATE, WIDTH), F32),
        ],
        input_output_aliases=aliases,
        compiler_params=params(),
        cost_estimate=pl.CostEstimate(
            flops=count * 4 * 10**9, bytes_accessed=count * 6 * 10**6, transcendentals=count * 2 * 10**6
        ),
        name="ssd_forward",
    )(jnp.asarray(steps, jnp.int32), proj, conv_w, conv_b, heads, skip, seg, spread, *more)


def ssd_backward(steps, proj, act, slope, dy, states, conv_w, conv_b, heads, skip, seg, spread, earlier=()):
    tokens = proj.shape[0]
    count = len(steps)
    more, more_specs, aliases = onto(earlier, 11)
    return pl.pallas_call(
        bwd_kernel,
        grid_spec=pltpu.PrefetchScalarGridSpec(
            num_scalar_prefetch=1,
            grid=(count,),
            in_specs=[
                placed(XCOLS), placed(XBC), placed(XBC), placed(WIDTH), STATES, whole((8, XBC)),
                whole((8, 128)), whole((8, WIDTH)), whole((128, WIDTH)), whole((128, 128 * LOCAL_HEADS)),
                *more_specs,
            ],
            out_specs=[placed(XCOLS), whole((8, XBC)), whole((8, 128))],
            scratch_shapes=[
                pltpu.VMEM((TILE, 128), F32),
                pltpu.VMEM((SPAN, 128), BF),
                pltpu.VMEM((SPAN, 128), BF),
                pltpu.VMEM((LOCAL_HEADS, 1, SPAN), F32),
                pltpu.VMEM((SPAN, SPAN), F32),
                pltpu.VMEM((SPAN, SPAN), F32),
                pltpu.VMEM((SPAN, 128), F32),
                pltpu.VMEM((LOCAL_HEADS, SPAN), F32),
                pltpu.VMEM((SPAN, 128), F32),
                pltpu.VMEM((SPAN, 128), F32),
                pltpu.VMEM((STATE, WIDTH), BF),
                pltpu.VMEM((TILE, XBC), F32),
                pltpu.VMEM((TILE, 128), F32),
                pltpu.VMEM((8, XBC), F32),
                pltpu.VMEM((KERNEL + 1, 8, XBC), F32),
            ],
        ),
        out_shape=[
            jax.ShapeDtypeStruct((tokens, XCOLS), BF),
            jax.ShapeDtypeStruct((8, XBC), F32),
            jax.ShapeDtypeStruct((8, 128), F32),
        ],
        input_output_aliases=aliases,
        compiler_params=params(),
        cost_estimate=pl.CostEstimate(
            flops=count * 10 * 10**9, bytes_accessed=count * 9 * 10**6, transcendentals=count * 4 * 10**6
        ),
        name="ssd_backward",
    )(jnp.asarray(steps, jnp.int32), proj, act, slope, dy, states, conv_w, heads, skip, seg, spread, *more)


def gate_stats(order, y, z, dn, gain):
    steps = y.shape[0] // TILE
    block = pl.BlockSpec((TILE, WIDTH), lambda i, o: (i, 0))
    return pl.pallas_call(
        stats_kernel,
        grid_spec=pltpu.PrefetchScalarGridSpec(
            num_scalar_prefetch=1,
            grid=(steps,),
            in_specs=[block, block, block, whole((8, WIDTH))],
            out_specs=pl.BlockSpec((8, TILE), lambda i, o: (0, i)),
            scratch_shapes=[pltpu.VMEM((TILE, 128), F32)],
        ),
        out_shape=jax.ShapeDtypeStruct((8, y.shape[0]), F32),
        compiler_params=params(),
        cost_estimate=pl.CostEstimate(flops=3 * 10**9, bytes_accessed=16 * 10**6, transcendentals=3 * 10**6),
        name="gate_stats",
    )(order, y, z, dn, gain)


def gate_backward(order, st, y, z, dn, gain):
    steps = y.shape[0] // TILE
    block = pl.BlockSpec((TILE, WIDTH), lambda i, o: (i, 0))
    return pl.pallas_call(
        gate_kernel,
        grid_spec=pltpu.PrefetchScalarGridSpec(
            num_scalar_prefetch=1,
            grid=(steps,),
            in_specs=[pl.BlockSpec((8, TILE), lambda i, o: (0, i)), block, block, block, whole((8, WIDTH))],
            out_specs=[block, block, block],
            scratch_shapes=[pltpu.VMEM((TILE, 128), F32)],
        ),
        out_shape=[jax.ShapeDtypeStruct(y.shape, BF)] * 3,
        compiler_params=params(),
        cost_estimate=pl.CostEstimate(flops=6 * 10**9, bytes_accessed=32 * 10**6, transcendentals=3 * 10**6),
        name="gate_backward",
    )(order, st, y, z, dn, gain)


def norm_tokens(order, values, gain, row, tokens, earlier=()):
    rows = sum(v.shape[0] for v in values)
    start = row // rows
    count = len(values)
    more, more_specs, aliases = onto(earlier, count + 2)
    return pl.pallas_call(
        functools.partial(norm_kernel, count),
        grid_spec=pltpu.PrefetchScalarGridSpec(
            num_scalar_prefetch=1,
            grid=(1,),
            in_specs=[*(whole(v.shape) for v in values), whole((8, D)), *more_specs],
            out_specs=[pl.BlockSpec((rows, D), lambda i, o: (start, 0))],
        ),
        out_shape=[jax.ShapeDtypeStruct((tokens, D), BF)],
        input_output_aliases=aliases,
        compiler_params=params(),
        cost_estimate=pl.CostEstimate(flops=rows * 10**6, bytes_accessed=rows * 8192, transcendentals=rows),
        name="norm_tokens",
    )(order, *values, gain, *more)[0]


def pack_kernel(at_ref, in_ref, dt_ref, xs_ref, xk_ref, zs_ref, zk_ref):
    rows = in_ref.shape[0]
    source = lax.broadcasted_iota(jnp.int32, (HEADS, 128), 0)
    lane = lax.broadcasted_iota(jnp.int32, (HEADS, 128), 1)
    for x_ref, z_ref, x in ((xs_ref, zs_ref, 1 - at_ref[0]), (xk_ref, zk_ref, at_ref[0])):
        for core in range(2):
            slot = 2 * core + x
            for k in range(AHEADS):
                cols = slice(k * 128, k * 128 + 128)
                at = (k * SLOTS + slot) * 128
                z_ref[core, :, cols] = in_ref[:, pl.ds(pl.multiple_of(at, 128), 128)]
                x_ref[core, :, cols] = in_ref[:, pl.ds(pl.multiple_of(DI + at, 128), 128)]
            x_ref[core, :, WIDTH:XBC] = in_ref[:, 2 * DI :]
            wanted = jnp.where(lane < LOCAL_HEADS, (lane // 2) * 8 + slot * 2 + lane % 2, -1)
            x_ref[core, :, XBC:] = nn(dt_ref[...], jnp.where(source == wanted, 1.0, 0.0).astype(BF)).astype(BF)


def pack_weights(xi, in_w, dt_w):
    rows = in_w.shape[0]
    shapes = [(2, rows, XCOLS)] * 2 + [(2, rows, WIDTH)] * 2
    return pl.pallas_call(
        pack_kernel,
        in_specs=[pl.BlockSpec(memory_space=pltpu.SMEM)] + [pl.BlockSpec(memory_space=pltpu.VMEM)] * 2,
        out_specs=[pl.BlockSpec(memory_space=pltpu.VMEM)] * 4,
        out_shape=[jax.ShapeDtypeStruct(shape, BF) for shape in shapes],
        cost_estimate=pl.CostEstimate(flops=10**8, bytes_accessed=3 * 10**6, transcendentals=0),
        name="pack_weights",
    )(xi[None].astype(jnp.int32), in_w, dt_w)


def pair_kernel(at_ref, keep_ref, got_ref, send_ref, stay_ref):
    rows = keep_ref.shape[1]
    mine = pl.ds(pl.multiple_of(at_ref[0] * rows, rows), rows)
    other = pl.ds(pl.multiple_of((1 - at_ref[0]) * rows, rows), rows)
    for out, core in ((send_ref, 1 - at_ref[1]), (stay_ref, at_ref[1])):
        out[mine, :] = keep_ref[core]
        out[other, :] = got_ref[core]


def pair_rows(xi, ci, keep, got):
    shape = (2 * keep.shape[1], keep.shape[2])
    return pl.pallas_call(
        pair_kernel,
        in_specs=[pl.BlockSpec(memory_space=pltpu.SMEM)] + [pl.BlockSpec(memory_space=pltpu.VMEM)] * 2,
        out_specs=[pl.BlockSpec(memory_space=pltpu.VMEM)] * 2,
        out_shape=[jax.ShapeDtypeStruct(shape, BF)] * 2,
        cost_estimate=pl.CostEstimate(flops=0, bytes_accessed=2 * 10**6, transcendentals=0),
        name="pair_rows",
    )(jnp.stack([xi, ci]).astype(jnp.int32), keep, got)


def place_kernel(at_ref, stay_ref, got_ref, out_ref):
    rows = stay_ref.shape[0]
    out_ref[pl.ds(pl.multiple_of(at_ref[0] * rows, rows), rows), :] = stay_ref[...]
    out_ref[pl.ds(pl.multiple_of((1 - at_ref[0]) * rows, rows), rows), :] = got_ref[...]


def place_rows(index, stay, got):
    return pl.pallas_call(
        place_kernel,
        in_specs=[pl.BlockSpec(memory_space=pltpu.SMEM)] + [pl.BlockSpec(memory_space=pltpu.VMEM)] * 2,
        out_specs=pl.BlockSpec(memory_space=pltpu.VMEM),
        out_shape=jax.ShapeDtypeStruct((2 * stay.shape[0], stay.shape[1]), BF),
        cost_estimate=pl.CostEstimate(flops=0, bytes_accessed=2 * 10**6, transcendentals=0),
        name="place_rows",
    )(index[None].astype(jnp.int32), stay, got)


def swap_x(v):
    return lax.ppermute(v, "x", SWAP)


def swap_core(v):
    return lax.ppermute(v, "core", SWAP)


def pick(v, index, axis=0):
    return lax.dynamic_index_in_dim(v, index, axis, keepdims=False)


def joined(index, mine, other, axis):
    return jnp.where(
        index == 0,
        jnp.concatenate([mine, other], axis=axis),
        jnp.concatenate([other, mine], axis=axis),
    )


def from_slots(v):
    slots, rows, cols = v.shape
    return (
        v.reshape(slots, rows, AHEADS, cols // AHEADS)
        .transpose(1, 2, 0, 3)
        .reshape(rows, slots * cols)
    )


class Return:
    def __init__(self, block):
        self.xi, self.ci = lax.axis_index("x"), lax.axis_index("core")
        self.rows = block.shape[0] // 4
        self.halves = block.astype(BF).reshape(2, 2 * self.rows, -1)
        self.flying = swap_core(pick(self.halves, 1 - self.ci))

    def turn(self, chain):
        got = chain.take(self.flying)
        pair = joined(self.ci, pick(self.halves, self.ci)[None], got[None], 0)
        self.pair = pair.reshape(2, 2, self.rows, -1)
        self.flying = swap_x(pick(self.pair, 1 - self.xi, 1))

    def land(self, chain):
        got = chain.take(self.flying)
        own = joined(self.xi, pick(self.pair, self.xi, 1)[:, None], got[:, None], 1)
        return own.reshape(4, self.rows, -1).astype(F32)


class Chain:
    def __init__(self):
        self.last = ()

    def tie(self, value):
        return lax.optimization_barrier((value, self.last))[0]

    def mark(self, value):
        self.last = value
        return value

    def take(self, value):
        return self.mark(self.tie(value))


class Ring:
    def __init__(self):
        self.size = len(CYCLE)
        place = [CYCLE.index(i) for i in range(self.size)]
        position = jnp.asarray(place, jnp.int32)[lax.axis_index("ra")]
        cycle = jnp.asarray(CYCLE, jnp.int32)
        steps = jnp.arange(self.size, dtype=jnp.int32)
        self.order = cycle[(position + steps) % self.size]
        self.inverse = (jnp.asarray(place, jnp.int32) - position) % self.size

    def pairs(self, d):
        return [(CYCLE[i], CYCLE[(i + d) % self.size]) for i in range(self.size)]

    def right(self, v):
        return lax.ppermute(v, "ra", self.pairs(1))

    def left(self, v):
        return lax.ppermute(v, "ra", self.pairs(-1))


class Gather:
    def __init__(self, ring, block):
        self.ring = ring
        self.rights, self.lefts = [block], [block]

    def start(self):
        r, l = self.rights[-1], self.lefts[-1]
        if len(self.rights) == 4:
            half = r.shape[0] // 2
            r, l = r[:half], l[half:]
        self.flying = self.ring.right(r), self.ring.left(l)

    def land(self, chain):
        r, l = chain.take(self.flying)
        self.rights.append(r)
        self.lefts.append(l)

    def blocks(self):
        r, l = self.rights, self.lefts
        return [r[0], l[1], l[2], l[3], jnp.concatenate([r[4], l[4]], axis=0), r[3], r[2], r[1]]


class Scatter:
    def __init__(self, ring, block):
        self.ring, self.block, self.count = ring, block, 0

    def start(self):
        block, ring, k = self.block, self.ring, self.count
        self.count += 1
        if k == 0:
            far = block(4)
            half = far.shape[0] // 2
            sends = far[:half], far[half:]
        elif k == 1:
            up, down = self.next
            half = up.shape[0] // 2
            r, l = self.right.astype(F32), self.left.astype(F32)
            sends = (
                jnp.concatenate([up[:half] + r, up[half:]], axis=0),
                jnp.concatenate([down[:half], down[half:] + l], axis=0),
            )
        else:
            sends = self.next[0] + self.right.astype(F32), self.next[1] + self.left.astype(F32)
        self.flying = ring.right(sends[0].astype(BF)), ring.left(sends[1].astype(BF))
        self.next = (block(3 - k), block(5 + k)) if k < 3 else (block(0),)

    def land(self, chain):
        self.right, self.left = chain.take(self.flying)

    def total(self):
        return self.next[0] + self.right.astype(F32) + self.left.astype(F32)


def flat_index(sizes):
    index = 0
    for name, size in zip(ALL, sizes):
        index = index * size + lax.axis_index(name)
    return index


class SmallSum:
    def __init__(self, v, sizes):
        self.value = v
        self.count = int(np.prod(sizes))
        self.bits = [2, 4, 8, 16, 1]

    def start(self):
        bit = self.bits.pop(0)
        self.flying = lax.ppermute(self.value, ALL, [(i, i ^ bit) for i in range(self.count)])

    def land(self, chain):
        self.value = self.value + chain.take(self.flying)


def permute_blocks(v, order, width):
    return jnp.concatenate(
        [
            lax.dynamic_slice(v, (0, order[k] * width), (v.shape[0], width))
            for k in range(v.shape[1] // width)
        ],
        axis=1,
    )


def reordered(v, order, short, long):
    parts = [v[:, k * short : (k + 1) * short] for k in order]
    base = 4 * short
    parts += [v[:, base + k * long : base + (k + 1) * long] for k in order]
    return jnp.concatenate(parts, axis=1)


def pad_rows(v, rows=8):
    return jnp.concatenate([v, jnp.zeros((rows - v.shape[0], v.shape[1]), v.dtype)], axis=0)


def pad_cols(v, cols):
    return jnp.concatenate([v, jnp.zeros(v.shape[:-1] + (cols - v.shape[-1],), v.dtype)], axis=-1)


def gather_small(v, sizes, chain):
    count = int(np.prod(sizes))
    if count != 32:
        return lax.all_gather(v[None], ALL, axis=0, tiled=True)
    me = flat_index(sizes)
    v = v[None]
    bit = 1
    while bit < count:
        got = chain.take(lax.ppermute(v, ALL, [(i, i ^ bit) for i in range(count)]))
        v = joined((me // bit) % 2, v, got, 0)
        bit *= 2
    return v


def per_device(
    sizes, tokens_short, tokens_long, cot_short, cot_long, seq_lengths,
    norm_gain, in_w, dt_w, conv_w, conv_b, dt_bias, a_log, d_skip, gate_gain, out_w,
):
    ringed = sizes == (8, 2, 1, 2)
    short, long = tokens_short.shape[0], tokens_long.shape[0]
    base = 4 * short
    tokens = base + 4 * long
    xi, ci = lax.axis_index("x"), lax.axis_index("core")
    slot = ci * 2 + xi
    feature = D // AHEADS
    mine_cols = lambda v: pick(v.reshape(v.shape[0], AHEADS, SLOTS, -1), slot, 2).reshape(v.shape[0], -1)
    chain = Chain()

    if ringed:
        ring = Ring()
        order, inverse = ring.order, ring.inverse
        from_ring = lambda v: permute_blocks(v, inverse, feature)
    else:
        order = jnp.arange(AHEADS, dtype=jnp.int32)
        from_ring = lambda v: v

    width = conv_w.shape[1]
    pieces = [conv_w.reshape(-1), conv_b, norm_gain, gate_gain]
    ends = np.cumsum([0] + [p.shape[0] for p in pieces])
    small = jnp.concatenate(pieces)
    half = long // 2

    part = long // 4
    long_parts = [tokens_long[k * part : (k + 1) * part] for k in range(4)]
    if ringed:
        x_send, x_keep, z_send, z_keep = chain.mark(pack_weights(xi, in_w, dt_w))
        x_got = swap_x(x_send)
        c_s, c_l = swap_core(chain.tie(tokens_short)), swap_core(chain.tie(tokens_long))
        send, stay = chain.mark(pair_rows(xi, ci, x_keep, chain.take(x_got)))
        got = swap_core(send)
        t_s = swap_x(chain.tie(tokens_short))
        gather_x = Gather(ring, chain.mark(place_rows(ci, stay, chain.take(got))))
        gather_x.start()
        pieces_l = [swap_x(chain.tie(long_parts[0]))]
    else:
        c_s, c_l = swap_core(tokens_short), swap_core(tokens_long)
        t_s = swap_x(tokens_short)
        pieces_l = [swap_x(v) for v in long_parts]

    small = chain.mark(gather_small(small, sizes, chain))
    norm_full = chain.mark(pad_rows(small[:, ends[2] : ends[3]].reshape(1, -1).astype(F32)))

    xh = ()

    def norm(values, row):
        nonlocal xh
        xh = (chain.mark(norm_tokens(order, values, norm_full, row, tokens, xh)),)

    t_s = chain.take(t_s)
    cx_s = swap_core(t_s)
    if ringed:
        pieces_l.append(swap_x(chain.tie(long_parts[1])))
        gather_x.land(chain)
        gather_x.start()
    norm([chain.tie(tokens_short)], 0)
    norm([chain.take(c_s)], 2 * short)
    norm([chain.tie(tokens_long)], base)
    if ringed:
        pieces_l[0] = chain.take(pieces_l[0])
        pieces_l.append(swap_x(chain.tie(long_parts[2])))
        gather_x.land(chain)
        gather_x.start()
    norm([chain.take(c_l)], base + 2 * long)
    norm([t_s], short)
    if ringed:
        pieces_l[1] = chain.take(pieces_l[1])
        pieces_l.append(swap_x(chain.tie(long_parts[3])))
        gather_x.land(chain)
        gather_x.start()
    pieces_c = [swap_core(pieces_l[0]), swap_core(pieces_l[1])]
    norm([chain.take(cx_s)], 3 * short)
    norm(pieces_l[:2], base + long)
    if ringed:
        gather_o = Gather(ring, chain.tie(out_w))
        gather_o.start()
        pieces_l[2] = chain.take(pieces_l[2])
        z_got = swap_x(chain.tie(z_send))
        gather_x.land(chain)
    pieces_c = chain.take(pieces_c)
    norm(pieces_c, base + 3 * long)

    small, dt_bias, a_log, d_skip, cot_s, cot_l = chain.mark(
        chain.tie((small, dt_bias, a_log, d_skip, cot_short, cot_long))
    )
    live_s = (jnp.arange(short) < seq_lengths[0, 0]).astype(F32)[:, None]
    live_l = (jnp.arange(long) < seq_lengths[1, 0]).astype(F32)[:, None]
    dv_s, dv_l = (live_s * cot_s).astype(BF), (live_l * cot_l).astype(BF)
    taps = small[:, : ends[2]].reshape(-1, KERNEL + 1, width)
    taps = taps.transpose(1, 0, 2).reshape(KERNEL + 1, -1).astype(F32)
    taps = jnp.concatenate([mine_cols(taps[:, :DI]), taps[:, DI:]], axis=1)
    conv_taps, conv_bias = pad_rows(taps[:KERNEL]), pad_rows(taps[KERNEL:])
    gate_mine = pad_rows(mine_cols(small[:, ends[3] :].reshape(1, -1).astype(F32)))
    neg_rate = -jnp.exp(a_log.astype(F32))
    heads = pad_rows(pad_cols(mine_cols(jnp.stack([dt_bias.astype(F32), neg_rate])), 128))
    skip = pad_rows(jnp.repeat(mine_cols(d_skip.astype(F32)[None]), HEAD_DIM, axis=1))
    head_rows = np.arange(128)[:, None]
    seg = jnp.asarray(
        (head_rows < 2 * LOCAL_HEADS) & (head_rows % LOCAL_HEADS == np.arange(WIDTH)[None, :] // HEAD_DIM), BF
    )
    spread = jnp.asarray(
        (head_rows < 3 * LOCAL_HEADS)
        & (head_rows % LOCAL_HEADS == np.arange(128 * LOCAL_HEADS)[None, :] // 128),
        BF,
    )
    seq_params = (conv_taps, conv_bias, heads, skip, seg, spread)

    pieces_l[3] = chain.take(pieces_l[3])
    pieces_c = [swap_core(pieces_l[2]), swap_core(pieces_l[3])]
    if ringed:
        w_x = chain.mark(jnp.concatenate(gather_x.blocks(), axis=0))
        gather_o.land(chain)
        gather_o.start()
    norm(pieces_l[2:], base + long + 2 * part)
    norm(chain.take(pieces_c), base + 3 * long + 2 * part)
    xh = xh[0]
    if ringed:
        send, stay = chain.mark(pair_rows(xi, ci, z_keep, chain.take(z_got)))
        dvx_s, dvx_a, dvx_b = swap_x(chain.tie(dv_s)), swap_x(chain.tie(dv_l[:half])), swap_x(chain.tie(dv_l[half:]))
        dvc_s, dvc_l = swap_core(chain.tie(dv_s)), swap_core(chain.tie(dv_l))
        got = chain.take(swap_core(send))
        gather_z = Gather(ring, chain.mark(place_rows(ci, stay, got)))
        gather_z.start()
        proj = chain.mark(nn(chain.tie(xh), w_x))
        for gather in (gather_o, gather_z):
            gather.land(chain)
            gather.start()
        dvx_s = chain.take(dvx_s)
        kept = chain.mark(ssd_forward((0, 1, 2), chain.tie(proj), *seq_params))
        for gather in (gather_o, gather_z):
            gather.land(chain)
            gather.start()
        dvx_a, dvx_b = chain.take(dvx_a), chain.take(dvx_b)
        dvcx_s, dvcx_a, dvcx_b = swap_core(dvx_s), swap_core(dvx_a), swap_core(dvx_b)
        y, act, slope, states = chain.mark(ssd_forward((3, 4), chain.tie(proj), *seq_params, earlier=kept))
        gather_o.land(chain)
        gather_z.land(chain)
        gather_z.start()
        w_o = chain.mark(jnp.concatenate(gather_o.blocks(), axis=0))
        dvcx_s, dvcx_a, dvcx_b, dvc_s, dvc_l = chain.take((dvcx_s, dvcx_a, dvcx_b, dvc_s, dvc_l))
        dv = chain.mark(
            jnp.concatenate([dv_s, dvx_s, dvc_s, dvcx_s, dv_l, dvx_a, dvx_b, dvc_l, dvcx_a, dvcx_b], axis=0)
        )
        dn = chain.mark(nt(dv, w_o).astype(BF))
        gather_z.land(chain)
        w_z = chain.mark(jnp.concatenate(gather_z.blocks(), axis=0))
        z = chain.mark(nn(chain.tie(xh), w_z).astype(BF))
    else:
        full = lax.all_gather(in_w, ALL, axis=0, tiled=True)
        full_dt = lax.all_gather(dt_w, ALL, axis=0, tiled=True)
        full_out = lax.all_gather(out_w, ALL, axis=0, tiled=True)
        w_z = mine_cols(full[:, :DI])
        w_x = jnp.concatenate(
            [mine_cols(full[:, DI : 2 * DI]), full[:, 2 * DI :], pad_cols(mine_cols(full_dt), 128)], axis=-1
        )
        w_o = pick(full_out.reshape(AHEADS, SLOTS, 128, D), slot, 1).reshape(WIDTH, D)
        dvx_s, dvx_l = swap_x(dv_s), swap_x(dv_l)
        dv = jnp.concatenate(
            [dv_s, dvx_s, swap_core(dv_s), swap_core(dvx_s), dv_l, dvx_l, swap_core(dv_l), swap_core(dvx_l)], axis=0
        )
        proj = nn(xh, w_x)
        y, act, slope, states = ssd_forward((0, 1, 2, 3, 4), proj, *seq_params)
        dn = nt(dv, w_o).astype(BF)
        z = nn(xh, w_z).astype(BF)

    st = chain.mark(gate_stats(order, y, chain.tie(z), dn, gate_mine))
    st = st + reordered(swap_core(st), (2, 3, 0, 1), short, long)
    st = st + reordered(swap_x(st), (1, 0, 3, 2), short, long)
    n, dy, dz = chain.mark(gate_backward(order, st, y, z, dn, gate_mine))

    far_s, far_l = slice(2 * short, base), slice(base + 2 * long, tokens)
    mid_s, mid_l = slice(short, 2 * short), slice(base + long, base + 2 * long)
    own_s, own_l = slice(0, short), slice(base, base + long)

    def send_far(product):
        values = chain.mark((product(far_s).astype(BF), product(far_l).astype(BF)))
        return swap_core(values[0]), swap_core(values[1])

    def send_mid(product, far):
        values = chain.mark(
            (
                (product(mid_s) + far[0][short:].astype(F32)).astype(BF),
                (product(mid_l) + far[1][long:].astype(F32)).astype(BF),
            )
        )
        return swap_x(values[0]), swap_x(values[1])

    def own_product(product):
        return chain.mark((product(own_s), product(own_l)))

    def with_own(own, far, mid):
        return (
            own[0] + far[0][:short].astype(F32) + mid[0].astype(F32),
            own[1] + far[1][:long].astype(F32) + mid[1].astype(F32),
        )

    def finish(product, far, mid):
        return with_own(own_product(product), far, mid)

    here = (jnp.arange(SLOTS) == slot).astype(F32)
    spread_cols = lambda v: (v.reshape(v.shape[0], AHEADS, 1, -1) * here[:, None]).reshape(v.shape[0], -1)

    def small_terms(acc, hacc):
        conv_part = jnp.concatenate([spread_cols(acc[:5, :WIDTH]), acc[:5, WIDTH:]], axis=1)
        skip_part = jnp.sum(acc[5, :WIDTH].reshape(LOCAL_HEADS, HEAD_DIM), axis=1)
        head_part = spread_cols(jnp.stack([hacc[0, :LOCAL_HEADS], hacc[1, :LOCAL_HEADS], skip_part]))
        return jnp.concatenate([conv_part.reshape(-1), head_part.reshape(-1)])

    def backward_call(steps, earlier):
        return chain.mark(
            ssd_backward(steps, chain.tie(proj), act, slope, dy, states, *seq_params, earlier=earlier)
        )

    def branch_product(part):
        return nn(chain.tie(n)[part], w_o)

    def unit_product(dx):
        return lambda part: nt(chain.tie(dx)[part], w_x) + nt(dz[part], w_z)

    g_out = chain.mark(tn(n, dv))
    if ringed:
        blocks_o = g_out.reshape(AHEADS, -1, D)
        scatter_o = Scatter(ring, lambda k: blocks_o[k])
        scatter_o.start()
        g_z = chain.mark(tn(chain.tie(xh), dz))
        blocks_z = g_z.reshape(AHEADS, -1, WIDTH)
        scatter_z = Scatter(ring, lambda k: blocks_z[k])
        scatter_z.start()
        scatter_o.land(chain)
        scatter_o.start()
        far_v = send_far(branch_product)
        scatter_z.land(chain)
        scatter_z.start()
        far_v = chain.take(far_v)
        mid_v = send_mid(branch_product, far_v)
        for scatter in (scatter_o, scatter_z):
            scatter.land(chain)
            scatter.start()
        dx, acc, hacc = backward_call((0, 3), ())
        for scatter in (scatter_o, scatter_z):
            scatter.land(chain)
            scatter.start()
        dx, acc2, hacc2 = backward_call((4,), (dx,))
        acc, hacc = acc + acc2, hacc + hacc2
        far_u = send_far(unit_product(dx))
        for scatter in (scatter_o, scatter_z):
            scatter.land(chain)
        own_out = chain.mark(scatter_o.total())
        back_z = Return(chain.mark(scatter_z.total()))
        mid_v = chain.take(mid_v)
        v_s, v_l = finish(branch_product, far_v, mid_v)
        back_z.turn(chain)
        dx, acc2, hacc2 = backward_call((2,), (chain.tie(dx),))
        acc, hacc = acc + acc2, hacc + hacc2
        far_u = chain.take(far_u)
        own_z = chain.mark(back_z.land(chain))
        mid_u = send_mid(unit_product(dx), far_u)
        dx, acc2, hacc2 = backward_call((1,), (chain.tie(dx),))
        acc, hacc = acc + acc2, hacc + hacc2
        scatter_x = Scatter(
            ring, lambda k: chain.mark(tn(xh[:, k * feature : (k + 1) * feature], chain.tie(dx)))
        )
        scatter_x.start()
        tally = SmallSum(small_terms(acc, hacc), sizes)
        tally.start()
        scatter_x.land(chain)
        scatter_x.start()
        tally.land(chain)
        tally.start()
        du_own = own_product(unit_product(dx))
        scatter_x.land(chain)
        scatter_x.start()
        tally.land(chain)
        tally.start()
        scatter_x.land(chain)
        scatter_x.start()
        tally.land(chain)
        tally.start()
        scatter_x.land(chain)
        back_x = Return(chain.mark(scatter_x.total()))
        tally.land(chain)
        tally.start()
        mid_u = chain.take(mid_u)
        du_s, du_l = chain.mark(with_own(du_own, far_u, mid_u))
        back_x.turn(chain)
        tally.land(chain)
        total = tally.value
    else:
        g_z = tn(xh, dz)
        far_v = send_far(branch_product)
        mid_v = send_mid(branch_product, far_v)
        v_s, v_l = finish(branch_product, far_v, mid_v)
        dx, acc, hacc = backward_call((0, 3, 4, 2, 1), ())
        far_u = send_far(unit_product(dx))
        mid_u = send_mid(unit_product(dx), far_u)
        du_s, du_l = finish(unit_product(dx), far_u, mid_u)
        g_x = tn(xh, dx)
        total = lax.psum(small_terms(acc, hacc), ALL)

    out_short = (tokens_short.astype(F32) + live_s * v_s).astype(BF)
    out_long = (tokens_long.astype(F32) + live_l * v_l).astype(BF)

    def token_grad(token, cot, d_u):
        residual = token.astype(F32)
        row_scale = lax.rsqrt(jnp.mean(residual * residual, axis=-1, keepdims=True) + EPS)
        unit = residual * row_scale
        d_norm = from_ring(d_u) * norm_full[0:1]
        return cot.astype(F32) + row_scale * (d_norm - unit * jnp.mean(d_norm * unit, axis=-1, keepdims=True))

    grad_short = token_grad(tokens_short, cot_short, du_s)
    grad_long = token_grad(tokens_long, cot_long, du_l)

    if ringed:
        own_x = back_x.land(chain)
        grad_in_w = jnp.concatenate(
            [
                from_slots(own_z),
                from_slots(own_x[:, :, :WIDTH]),
                jnp.sum(own_x[:, :, WIDTH:XBC], axis=0),
            ],
            axis=1,
        )
        grad_dt_w = from_slots(own_x[:, :, XBC : XBC + LOCAL_HEADS])
    else:
        here = (jnp.arange(SLOTS) == slot).astype(F32)
        widen = lambda v: (v.reshape(D, AHEADS, 1, -1) * here[:, None]).reshape(D, -1)
        reduce = lambda v: lax.psum_scatter(v, ALL, scatter_dimension=0, tiled=True)
        grad_in_w = reduce(
            jnp.concatenate([widen(g_z), widen(g_x[:, :WIDTH]), g_x[:, WIDTH:XBC]], axis=1)
        )
        grad_dt_w = reduce(widen(g_x[:, XBC : XBC + LOCAL_HEADS]))
        own_out = reduce((g_out.reshape(AHEADS, 1, 128, D) * here[:, None, None]).reshape(DI, D))

    grad_norm_gain = (
        jnp.sum(in_w.astype(F32) * grad_in_w, axis=1) + jnp.sum(dt_w.astype(F32) * grad_dt_w, axis=1)
    ) / norm_gain.astype(F32)
    grad_gate_gain = jnp.sum(out_w.astype(F32) * own_out, axis=1) / gate_gain.astype(F32)

    conv_total = total[: 5 * (DI + 2 * STATE)].reshape(5, -1)
    head_total = total[5 * (DI + 2 * STATE) :].reshape(3, HEADS)
    own_conv = lax.dynamic_slice(conv_total, (0, flat_index(sizes) * width), (5, width))
    return (
        out_short,
        out_long,
        grad_short,
        grad_long,
        grad_norm_gain,
        grad_in_w,
        grad_dt_w,
        own_conv[:KERNEL],
        own_conv[KERNEL],
        head_total[0],
        head_total[1] * neg_rate,
        head_total[2],
        grad_gate_gain,
        own_out,
    )


def solution(mesh):
    wide, narrow = mesh.shape["wide"], mesh.shape["narrow"]
    sizes = (wide // 2, 2, narrow // 2, 2)
    split = Mesh(mesh.devices.reshape(sizes), ALL)
    rows, vector, columns = P(ALL, None), P(ALL), P(None, ALL)
    return jax.shard_map(
        functools.partial(per_device, sizes),
        mesh=split,
        in_specs=(
            rows, rows, rows, rows, columns, vector, rows, rows, columns, vector, P(), P(), P(), vector, rows,
        ),
        out_specs=(
            rows, rows, rows, rows, vector, rows, rows, columns, vector, P(), P(), P(), vector, rows,
        ),
        check_vma=False,
    )
```

```python
import functools

import jax
import jax.numpy as jnp
import numpy as np
from jax import lax
from jax.experimental import pallas as pl
from jax.experimental.pallas import tpu as pltpu
from jax.sharding import Mesh
from jax.sharding import PartitionSpec as P

D = 2048
DI = 4096
HEADS = 64
HEAD_DIM = 64
STATE = 128
KERNEL = 4
SPAN = 256
EPS = 1e-05
BF = jnp.bfloat16
F32 = jnp.float32

SLOTS = 4
AHEADS = 8
WIDTH = DI // SLOTS
LOCAL_HEADS = HEADS // SLOTS
XBC = WIDTH + 2 * STATE
XCOLS = XBC + 128
ALL = ("ra", "core", "rb", "x")
NEG = -1e30
TILE = 640
HEAD = 128

SWAP = [(0, 1), (1, 0)]
CYCLE = (0, 2, 4, 6, 7, 5, 3, 1)


def nt(a, b):
    return lax.dot_general(a, b, (((1,), (1,)), ((), ())), preferred_element_type=F32)


def nn(a, b):
    return lax.dot_general(a, b, (((1,), (0,)), ((), ())), preferred_element_type=F32)


def tn(a, b):
    return lax.dot_general(a, b, (((0,), (0,)), ((), ())), preferred_element_type=F32)


LOG2E = 1.4426950408889634
ROWS = 64


def sigmoid(v):
    return 0.5 * jnp.tanh(0.5 * v) + 0.5


def lane_index():
    return lax.broadcasted_iota(jnp.int32, (1, 128), 1)


def three_parts(values):
    values = jnp.where(lane_index() < LOCAL_HEADS, values, 0.0)
    high = values.astype(BF).astype(F32)
    rest = values - high
    mid = rest.astype(BF).astype(F32)
    low = rest - mid
    return (high + pltpu.roll(mid, LOCAL_HEADS, 1) + pltpu.roll(low, 2 * LOCAL_HEADS, 1)).astype(BF)


def add_parts(values):
    return values + pltpu.roll(values, 128 - LOCAL_HEADS, 1) + pltpu.roll(values, 128 - 2 * LOCAL_HEADS, 1)


def triangle(n, lower):
    i = lax.broadcasted_iota(jnp.int32, (n, n), 0)
    j = lax.broadcasted_iota(jnp.int32, (n, n), 1)
    return jnp.where(i >= j if lower else i <= j, 1.0, 0.0).astype(BF)


def running_sum(values, lower):
    return add_parts(nn(triangle(values.shape[0], lower), three_parts(values)))


def two_parts(values):
    values = jnp.where(lane_index() < LOCAL_HEADS, values, 0.0)
    high = values.astype(BF).astype(F32)
    return (high + pltpu.roll(values - high, LOCAL_HEADS, 1)).astype(BF)


def softplus(v):
    return jnp.maximum(v, 0.0) + jnp.log1p(jnp.exp(-jnp.abs(v)))


def conv_tile(p_ref, cw_ref, cb_ref, r0, cols):
    starts = (r0 == 0) | (r0 == HEAD)
    before = p_ref[pl.ds(pl.multiple_of(jnp.maximum(r0 - 8, 0), 8), 8), cols]
    before = jnp.where(starts, 0.0, before)
    here = p_ref[pl.ds(r0, ROWS), cols]
    both = jnp.concatenate([before, here], axis=0)
    back = [here] + [pltpu.roll(both, m, 0)[8:] for m in (1, 2, 3)]
    total = cb_ref[0:1, cols]
    for m in range(KERNEL):
        total = total + cw_ref[3 - m : 4 - m, cols] * back[m]
    return total, back


def fwd_kernel(
    steps_ref, p_ref, cw_ref, cb_ref, hp_ref, dsk_ref, seg_ref, bc_ref, *refs
):
    y_ref, act_ref, slope_ref, h_ref, dt_s, parts_s, grow_s, rt_s, g_s = refs[-9:]
    lane = lane_index()

    def conv_step(i, carry):
        r0 = pl.multiple_of(i * ROWS, ROWS)
        rows = pl.ds(r0, ROWS)
        for c in range(XBC // 128):
            cols = slice(c * 128, c * 128 + 128)
            conv, _ = conv_tile(p_ref, cw_ref, cb_ref, r0, cols)
            gate = sigmoid(conv)
            act = conv * gate
            act_ref[rows, cols] = act.astype(BF)
            slope_ref[rows, cols] = (gate + act * (1.0 - gate)).astype(BF)
        dt_s[rows, :] = softplus(p_ref[rows, XBC:] + hp_ref[0:1])
        return carry

    lax.fori_loop(0, TILE // ROWS, conv_step, 0)
    rate = hp_ref[1:2]

    def block(off, q, read_state, make_state):
        rows = pl.ds(off, q)
        dt = dt_s[rows, :]
        cum2 = running_sum(dt * rate, True) * LOG2E
        parts_s[:q, :] = three_parts(cum2)
        turned = (cum2 - jnp.log2(dt)).T
        for h in range(LOCAL_HEADS):
            rt_s[h, :, :q] = turned[h : h + 1]
        b = act_ref[rows, WIDTH : WIDTH + STATE]
        c = act_ref[rows, WIDTH + STATE :]
        g_s[:q, :q] = nt(c, b)
        if read_state:
            grow_s[:q, :] = two_parts(jnp.exp2(cum2))
        if make_state:
            grow_s[:q, :] = two_parts(jnp.exp2(cum2[q - 1 : q] - cum2) * dt)
            b_turned = b.astype(F32).T.astype(BF)
        diagonal = lax.broadcasted_iota(jnp.int32, (128, 128), 0) >= lax.broadcasted_iota(
            jnp.int32, (128, 128), 1
        )

        def pair(p, carry):
            lanes = pl.ds(pl.multiple_of(p * 128, 128), 128)
            x2 = act_ref[rows, lanes]
            zero = jnp.zeros_like(x2)
            x_heads = [jnp.where(lane < HEAD_DIM, x2, zero), jnp.where(lane < HEAD_DIM, zero, x2)]
            cols = nn(parts_s[:q, :], bc_ref[:, pl.ds(pl.multiple_of(p * 256, 256), 256)])
            if read_state:
                carried = nn(grow_s[:q, :], seg_ref[:, lanes]) * nn(c, h_ref[0, :, lanes].astype(BF))
            for rt in range(q // 128):
                top = rt * 128
                mixes = []
                for j in range(2):
                    col = cols[top : top + 128, j * 128 : j * 128 + 128]
                    for ct in range(rt + 1):
                        lo = ct * 128
                        spread = col - rt_s[p * 2 + j, :, lo : lo + 128]
                        if ct == rt:
                            spread = jnp.where(diagonal, spread, NEG)
                        mixes.append((g_s[top : top + 128, lo : lo + 128] * jnp.exp2(spread)).astype(BF))
                x_both = jnp.concatenate([x[: top + 128] for x in x_heads], axis=0)
                out = nn(jnp.concatenate(mixes, axis=1), x_both)
                out = out + dsk_ref[0:1, lanes] * x2[top : top + 128].astype(F32)
                if read_state:
                    out = out + carried[top : top + 128]
                y_ref[pl.ds(off + top, 128), lanes] = out.astype(y_ref.dtype)
            if make_state:
                wide = nn(grow_s[:q, :], seg_ref[:, lanes])
                h_ref[0, :, lanes] = nn(b_turned, (wide * x2.astype(F32)).astype(BF))
            return carry

        lax.fori_loop(0, LOCAL_HEADS // 2, pair, 0, unroll=True)

    block(0, HEAD, False, False)
    block(HEAD, SPAN, False, True)
    block(HEAD + SPAN, SPAN, True, False)


def bwd_kernel(
    steps_ref, p_ref, act_ref, slope_ref, dy_ref, dz_ref, h_ref, cw_ref, hp_ref, dsk_ref, seg_ref, bc_ref, *refs
):
    dp_ref, acc_ref, hacc_ref = refs[-18:-15]
    dt_s, parts_s, grow_s, ct_s, gt_s, dgt_s, kc_s, kr_s, fold_s, dbc_s, ds_s, da_s, dst_s, after_s, sums_s = refs[-15:]
    lane = lane_index()
    head_row = lax.broadcasted_iota(jnp.int32, (LOCAL_HEADS, 1), 0)

    @pl.when(pl.program_id(0) == 0)
    def _():
        acc_ref[...] = jnp.zeros_like(acc_ref)
        hacc_ref[...] = jnp.zeros_like(hacc_ref)

    rate = hp_ref[1:2]
    dt_s[...] = softplus(p_ref[:, XBC:] + hp_ref[0:1])

    def block(off, q, state_in, state_out):
        rows = pl.ds(off, q)
        dt = dt_s[rows, :]
        cum2 = running_sum(dt * rate, True) * LOG2E
        parts_s[:q, :] = three_parts(cum2 - jnp.log2(dt))
        turned = cum2.T
        for h in range(LOCAL_HEADS):
            ct_s[h, :, :q] = turned[h : h + 1]
        b = act_ref[rows, WIDTH : WIDTH + STATE]
        c = act_ref[rows, WIDTH + STATE :]
        gt_s[:q, :q] = nt(b, c)
        dgt_s[:q, :q] = jnp.zeros((q, q), F32)
        kc_s[:q, :] = jnp.zeros((q, 128), F32)
        kr_s[:, :q] = jnp.zeros((LOCAL_HEADS, q), F32)
        if state_in or state_out:
            fold_s[:q, :] = jnp.zeros((q, 128), F32)
            dbc_s[:q, :] = jnp.zeros((q, 128), F32)
        if state_in:
            grow_s[:q, :] = two_parts(jnp.exp2(cum2))
            c_turned = c.astype(F32).T.astype(BF)
        if state_out:
            decay = jnp.exp2(cum2[q - 1 : q] - cum2)
            grow_s[:q, :] = two_parts(decay * dt)
        diagonal = lax.broadcasted_iota(jnp.int32, (128, 128), 1) >= lax.broadcasted_iota(
            jnp.int32, (128, 128), 0
        )
        tiles = q // 128

        def pair(p, carry):
            lanes = pl.ds(pl.multiple_of(p * 128, 128), 128)
            x2 = act_ref[rows, lanes]
            dy2 = dy_ref[rows, lanes]
            zero = jnp.zeros_like(dy2)
            dy_heads = [jnp.where(lane < HEAD_DIM, dy2, zero), jnp.where(lane < HEAD_DIM, zero, dy2)]
            cols = nn(parts_s[:q, :], bc_ref[:, pl.ds(pl.multiple_of(p * 256, 256), 256)])
            if state_in:
                hb = h_ref[0, :, lanes].astype(BF)
                dyc = dy2.astype(F32) * nn(grow_s[:q, :], seg_ref[:, lanes])
                dyb = dyc.astype(BF)
                fold_s[:q, :] += nt((dyc * nn(c, hb)).astype(BF), seg_ref[:, lanes])
                dbc_s[:q, :] += nt(dyb, hb)
                ds_s[:, lanes] = nn(c_turned, dyb).astype(BF)
            if state_out:
                sb = ds_s[:, lanes]
                wide = nn(grow_s[:q, :], seg_ref[:, lanes])
                bd = nn(b, sb)
                xf = x2.astype(F32)
                fold_s[:q, :] += nt((xf * bd).astype(BF), seg_ref[:, lanes])
                dbc_s[:q, :] += nt((wide * xf).astype(BF), sb)
                late = wide * bd
            picks = [jnp.where(lane == p * 2 + j, 1.0, 0.0).astype(BF) for j in range(2)]
            marks = [jnp.where(head_row == p * 2 + j, 1.0, 0.0).astype(BF) for j in range(2)]
            for jt in range(tiles):
                lo = jt * 128
                span = q - lo
                xj = x2[lo : lo + 128]
                mixes = []
                terms = []
                dgs = [None] * tiles
                for j in range(2):
                    col = cols[lo : lo + 128, j * 128 : j * 128 + 128]
                    for it in range(jt, tiles):
                        at = it * 128
                        spread = ct_s[p * 2 + j, :, at : at + 128] - col
                        if it == jt:
                            spread = jnp.where(diagonal, spread, NEG)
                        e = jnp.exp2(spread)
                        score = gt_s[lo : lo + 128, at : at + 128]
                        dme = nt(xj, dy_heads[j][at : at + 128]) * e
                        dgs[it] = dme if dgs[it] is None else dgs[it] + dme
                        terms.append((dme * score).astype(BF))
                        mixes.append((score * e).astype(BF))
                for it in range(jt, tiles):
                    dgt_s[lo : lo + 128, it * 128 : it * 128 + 128] += dgs[it]
                half = len(terms) // 2
                kc_s[lo : lo + 128, :] += nn(
                    jnp.concatenate(terms, axis=1),
                    jnp.concatenate([jnp.broadcast_to(v, (span, 128)) for v in picks], axis=0),
                )
                kr_s[:, lo:q] += nn(
                    jnp.concatenate([jnp.broadcast_to(v, (LOCAL_HEADS, 128)) for v in marks], axis=1),
                    jnp.concatenate(
                        [jnp.concatenate(terms[:half], axis=1), jnp.concatenate(terms[half:], axis=1)], axis=0
                    ),
                )
                dy_both = jnp.concatenate([d[lo:] for d in dy_heads], axis=0)
                out = nn(jnp.concatenate(mixes, axis=1), dy_both)
                dyj = dy2[lo : lo + 128].astype(F32)
                acc_ref[5:6, lanes] += jnp.sum(dyj * xj.astype(F32), axis=0, keepdims=True)
                out = out + dsk_ref[0:1, lanes] * dyj
                if state_out:
                    out = out + late[lo : lo + 128]
                da_s[pl.ds(off + lo, 128), lanes] = out
            return carry

        lax.fori_loop(0, LOCAL_HEADS // 2, pair, 0, unroll=True)

        dgt = dgt_s[:q, :q].astype(BF)
        db = nn(dgt, c)
        dc = tn(dgt, b)
        kcol = kc_s[:q, :]
        row_terms = jnp.concatenate([kr_s[:, :q], jnp.zeros((128 - LOCAL_HEADS, q), F32)], axis=0)
        d_cum = row_terms.T - kcol
        inverse = jnp.where(dt > 1e-30, 1.0 / jnp.maximum(dt, 1e-30), 0.0)
        d_dt = kcol * inverse
        if state_in:
            d_cum = d_cum + fold_s[:q, :]
            dc = dc + dbc_s[:q, :]
        if state_out:
            db = db + dbc_s[:q, :]
            d_weights = fold_s[:q, :]
            d_dt = d_dt + d_weights * decay
            w_term = d_weights * decay * dt
            last = lax.broadcasted_iota(jnp.int32, (q, 1), 0) == q - 1
            d_cum = d_cum - w_term + jnp.where(last, jnp.sum(w_term, axis=0, keepdims=True), 0.0)
        da_s[rows, WIDTH : WIDTH + STATE] = db
        da_s[rows, WIDTH + STATE :] = dc
        d_rate = running_sum(d_cum, False)
        dst_s[rows, :] = d_dt + d_rate * rate
        hacc_ref[1:2, :] += jnp.sum(d_rate * dt, axis=0, keepdims=True)

    block(0, HEAD, False, False)
    block(HEAD + SPAN, SPAN, True, False)
    block(HEAD, SPAN, False, True)

    d_soft = dst_s[...] * jax.nn.sigmoid(p_ref[:, XBC:] + hp_ref[0:1])
    d_soft = jnp.where(lane < LOCAL_HEADS, d_soft, 0.0)
    hacc_ref[0:1, :] += jnp.sum(d_soft, axis=0, keepdims=True)
    dp_ref[:, XBC:XCOLS] = d_soft.astype(BF)
    dp_ref[:, XCOLS:] = dz_ref[...]
    sums_s[...] = jnp.zeros_like(sums_s)
    after_s[...] = jnp.zeros_like(after_s)

    def conv_step(i, carry):
        r0 = pl.multiple_of(TILE - ROWS - i * ROWS, ROWS)
        rows = pl.ds(r0, ROWS)
        ends = (r0 + ROWS == HEAD) | (r0 + ROWS == TILE)
        fold = lambda v: jnp.sum(v.reshape(ROWS // 8, 8, 128), axis=0)
        for c in range(XBC // 128):
            cols = slice(c * 128, c * 128 + 128)
            here = p_ref[rows, cols]
            d_conv = da_s[rows, cols] * slope_ref[rows, cols].astype(F32)
            both = jnp.concatenate([d_conv, jnp.where(ends, 0.0, after_s[:, cols])], axis=0)
            after_s[:, cols] = d_conv[:8]
            total = cw_ref[3:4, cols] * d_conv
            sums_s[3, :, cols] += fold(d_conv * here)
            sums_s[4, :, cols] += fold(d_conv)
            for m in (1, 2, 3):
                ahead = pltpu.roll(both, ROWS + 8 - m, 0)[:ROWS]
                total = total + cw_ref[3 - m : 4 - m, cols] * ahead
                sums_s[3 - m, :, cols] += fold(ahead * here)
            dp_ref[rows, cols] = total.astype(BF)
        return carry

    lax.fori_loop(0, TILE // ROWS, conv_step, 0)
    for k in range(KERNEL + 1):
        acc_ref[k : k + 1, :] += jnp.sum(sums_s[k], axis=0, keepdims=True)


def stats_kernel(order_ref, y_ref, z_ref, dn_ref, gain_ref, st_ref, both_s):
    lane = lane_index()

    def step(i, carry):
        rows = pl.ds(pl.multiple_of(i * ROWS, ROWS), ROWS)
        p1 = jnp.zeros((ROWS, 128), F32)
        p2 = jnp.zeros((ROWS, 128), F32)
        for k in range(AHEADS):
            lanes = pl.ds(pl.multiple_of(order_ref[k] * 128, 128), 128)
            z = z_ref[rows, lanes].astype(F32)
            g = y_ref[rows, lanes].astype(F32) * (z * sigmoid(z))
            p1 = p1 + g * g
            p2 = p2 + g * (dn_ref[rows, k * 128 : k * 128 + 128].astype(F32) * gain_ref[0:1, lanes])
        both_s[rows, :] = jnp.where(
            lane == 0,
            jnp.sum(p1, axis=1, keepdims=True),
            jnp.where(lane == 1, jnp.sum(p2, axis=1, keepdims=True), 0.0),
        )
        return carry

    lax.fori_loop(0, y_ref.shape[0] // ROWS, step, 0)
    st_ref[...] = both_s[...].T[0:8]


def gate_kernel(order_ref, st_ref, y_ref, z_ref, dn_ref, gain_ref, n_ref, dy_ref, dz_ref, st_s):
    st_s[...] = jnp.concatenate([st_ref[...], jnp.zeros((120, y_ref.shape[0]), F32)], axis=0).T

    def step(i, carry):
        rows = pl.ds(pl.multiple_of(i * ROWS, ROWS), ROWS)
        st = st_s[rows, :]
        rg = lax.rsqrt(st[:, 0:1] * (1.0 / DI) + EPS)
        mean = rg * rg * st[:, 1:2] * (1.0 / DI)
        for k in range(AHEADS):
            lanes = pl.ds(pl.multiple_of(order_ref[k] * 128, 128), 128)
            fixed = slice(k * 128, k * 128 + 128)
            gain = gain_ref[0:1, lanes]
            z = z_ref[rows, lanes].astype(F32)
            y = y_ref[rows, lanes].astype(F32)
            sg = sigmoid(z)
            silu = z * sg
            ghat = y * silu * rg
            dg = rg * (dn_ref[rows, fixed].astype(F32) * gain) - ghat * mean
            n_ref[rows, fixed] = (ghat * gain).astype(BF)
            dy_ref[rows, lanes] = (dg * silu).astype(BF)
            dz_ref[rows, lanes] = (dg * y * (sg + silu * (1.0 - sg))).astype(BF)
        return carry

    lax.fori_loop(0, y_ref.shape[0] // ROWS, step, 0)


def norm_kernel(pieces, order_ref, *refs):
    gain_ref, u_ref = refs[pieces], refs[-1]
    at = 0
    for x_ref in refs[:pieces]:
        count = x_ref.shape[0] // ROWS

        def step(i, carry, x_ref=x_ref, at=at):
            rows = pl.ds(pl.multiple_of(i * ROWS, ROWS), ROWS)
            out = pl.ds(pl.multiple_of(at + i * ROWS, ROWS), ROWS)
            total = jnp.zeros((ROWS, 128), F32)
            for k in range(D // 128):
                v = x_ref[rows, k * 128 : k * 128 + 128].astype(F32)
                total = total + v * v
            scale = lax.rsqrt(jnp.sum(total, axis=1, keepdims=True) * (1.0 / D) + EPS)
            for k in range(AHEADS):
                lanes = pl.ds(pl.multiple_of(order_ref[k] * 256, 256), 256)
                u_ref[out, k * 256 : k * 256 + 256] = (
                    x_ref[rows, lanes].astype(F32) * scale * gain_ref[0:1, lanes]
                ).astype(BF)
            return carry

        lax.fori_loop(0, count, step, 0)
        at += x_ref.shape[0]


def whole(shape):
    return pl.BlockSpec(shape, lambda i, s: (0,) * len(shape))


def placed(cols):
    return pl.BlockSpec((TILE, cols), lambda i, s: (s[i], 0))


def params():
    return pltpu.CompilerParams(vmem_limit_bytes=56 * 1024 * 1024)


def onto(earlier, first_input):
    specs = [pl.BlockSpec(memory_space=pl.ANY)] * len(earlier)
    return list(earlier), specs, {first_input + i: i for i in range(len(earlier))}


STATES = pl.BlockSpec((1, STATE, WIDTH), lambda i, s: (s[i], 0, 0))


def ssd_forward(steps, proj, conv_w, conv_b, heads, skip, seg, spread, earlier=()):
    tokens = proj.shape[0]
    count = len(steps)
    more, more_specs, aliases = onto(earlier, 8)
    return pl.pallas_call(
        fwd_kernel,
        grid_spec=pltpu.PrefetchScalarGridSpec(
            num_scalar_prefetch=1,
            grid=(count,),
            in_specs=[
                placed(XCOLS), whole((8, XBC)), whole((8, XBC)), whole((8, 128)), whole((8, WIDTH)),
                whole((128, WIDTH)), whole((128, 128 * LOCAL_HEADS)), *more_specs,
            ],
            out_specs=[placed(WIDTH), placed(XBC), placed(XBC), STATES],
            scratch_shapes=[
                pltpu.VMEM((TILE, 128), F32),
                pltpu.VMEM((SPAN, 128), BF),
                pltpu.VMEM((SPAN, 128), BF),
                pltpu.VMEM((LOCAL_HEADS, 1, SPAN), F32),
                pltpu.VMEM((SPAN, SPAN), F32),
            ],
        ),
        out_shape=[
            jax.ShapeDtypeStruct((tokens, WIDTH), BF),
            jax.ShapeDtypeStruct((tokens, XBC), BF),
            jax.ShapeDtypeStruct((tokens, XBC), BF),
            jax.ShapeDtypeStruct((tokens // TILE, STATE, WIDTH), F32),
        ],
        input_output_aliases=aliases,
        compiler_params=params(),
        cost_estimate=pl.CostEstimate(
            flops=count * 4 * 10**9, bytes_accessed=count * 6 * 10**6, transcendentals=count * 2 * 10**6
        ),
        name="ssd_forward",
    )(jnp.stack(steps).astype(jnp.int32), proj, conv_w, conv_b, heads, skip, seg, spread, *more)


def ssd_backward(steps, proj, act, slope, dy, dz, states, conv_w, conv_b, heads, skip, seg, spread, earlier=()):
    tokens = proj.shape[0]
    count = len(steps)
    more, more_specs, aliases = onto(earlier, 12)
    return pl.pallas_call(
        bwd_kernel,
        grid_spec=pltpu.PrefetchScalarGridSpec(
            num_scalar_prefetch=1,
            grid=(count,),
            in_specs=[
                placed(XCOLS), placed(XBC), placed(XBC), placed(WIDTH), placed(WIDTH), STATES, whole((8, XBC)),
                whole((8, 128)), whole((8, WIDTH)), whole((128, WIDTH)), whole((128, 128 * LOCAL_HEADS)),
                *more_specs,
            ],
            out_specs=[placed(XCOLS + WIDTH), whole((8, XBC)), whole((8, 128))],
            scratch_shapes=[
                pltpu.VMEM((TILE, 128), F32),
                pltpu.VMEM((SPAN, 128), BF),
                pltpu.VMEM((SPAN, 128), BF),
                pltpu.VMEM((LOCAL_HEADS, 1, SPAN), F32),
                pltpu.VMEM((SPAN, SPAN), F32),
                pltpu.VMEM((SPAN, SPAN), F32),
                pltpu.VMEM((SPAN, 128), F32),
                pltpu.VMEM((LOCAL_HEADS, SPAN), F32),
                pltpu.VMEM((SPAN, 128), F32),
                pltpu.VMEM((SPAN, 128), F32),
                pltpu.VMEM((STATE, WIDTH), BF),
                pltpu.VMEM((TILE, XBC), F32),
                pltpu.VMEM((TILE, 128), F32),
                pltpu.VMEM((8, XBC), F32),
                pltpu.VMEM((KERNEL + 1, 8, XBC), F32),
            ],
        ),
        out_shape=[
            jax.ShapeDtypeStruct((tokens, XCOLS + WIDTH), BF),
            jax.ShapeDtypeStruct((8, XBC), F32),
            jax.ShapeDtypeStruct((8, 128), F32),
        ],
        input_output_aliases=aliases,
        compiler_params=params(),
        cost_estimate=pl.CostEstimate(
            flops=count * 10 * 10**9, bytes_accessed=count * 9 * 10**6, transcendentals=count * 4 * 10**6
        ),
        name="ssd_backward",
    )(jnp.stack(steps).astype(jnp.int32), proj, act, slope, dy, dz, states, conv_w, heads, skip, seg, spread, *more)


def gate_stats(order, y, z, dn, gain):
    steps = y.shape[0] // TILE
    block = pl.BlockSpec((TILE, WIDTH), lambda i, o: (i, 0))
    return pl.pallas_call(
        stats_kernel,
        grid_spec=pltpu.PrefetchScalarGridSpec(
            num_scalar_prefetch=1,
            grid=(steps,),
            in_specs=[block, block, block, whole((8, WIDTH))],
            out_specs=pl.BlockSpec((8, TILE), lambda i, o: (0, i)),
            scratch_shapes=[pltpu.VMEM((TILE, 128), F32)],
        ),
        out_shape=jax.ShapeDtypeStruct((8, y.shape[0]), F32),
        compiler_params=params(),
        cost_estimate=pl.CostEstimate(flops=3 * 10**9, bytes_accessed=16 * 10**6, transcendentals=3 * 10**6),
        name="gate_stats",
    )(order, y, z, dn, gain)


def gate_backward(order, st, y, z, dn, gain):
    steps = y.shape[0] // TILE
    block = pl.BlockSpec((TILE, WIDTH), lambda i, o: (i, 0))
    return pl.pallas_call(
        gate_kernel,
        grid_spec=pltpu.PrefetchScalarGridSpec(
            num_scalar_prefetch=1,
            grid=(steps,),
            in_specs=[pl.BlockSpec((8, TILE), lambda i, o: (0, i)), block, block, block, whole((8, WIDTH))],
            out_specs=[block, block, block],
            scratch_shapes=[pltpu.VMEM((TILE, 128), F32)],
        ),
        out_shape=[jax.ShapeDtypeStruct(y.shape, BF)] * 3,
        compiler_params=params(),
        cost_estimate=pl.CostEstimate(flops=6 * 10**9, bytes_accessed=32 * 10**6, transcendentals=3 * 10**6),
        name="gate_backward",
    )(order, st, y, z, dn, gain)


def norm_tokens(order, values, gain):
    rows = sum(v.shape[0] for v in values)
    return pl.pallas_call(
        functools.partial(norm_kernel, len(values)),
        grid_spec=pltpu.PrefetchScalarGridSpec(
            num_scalar_prefetch=1,
            grid=(1,),
            in_specs=[*(whole(v.shape) for v in values), whole((8, D))],
            out_specs=[whole((rows, D))],
        ),
        out_shape=[jax.ShapeDtypeStruct((rows, D), BF)],
        compiler_params=params(),
        cost_estimate=pl.CostEstimate(flops=rows * 10**6, bytes_accessed=rows * 8192, transcendentals=rows),
        name="norm_tokens",
    )(order, *values, gain)[0]


def pack_kernel(at_ref, in_ref, dt_ref, small_ref, send_ref, keep_ref):
    rows = in_ref.shape[0]
    send_ref[:, rows:, :] = jnp.zeros((2, 8, XCOLS + WIDTH), BF)
    send_ref[0, rows:, :] = small_ref[...]
    source = lax.broadcasted_iota(jnp.int32, (HEADS, 128), 0)
    lane = lax.broadcasted_iota(jnp.int32, (HEADS, 128), 1)
    for out_ref, x in ((send_ref, 1 - at_ref[0]), (keep_ref, at_ref[0])):
        for core in range(2):
            slot = 2 * core + x
            for k in range(AHEADS):
                at = (k * SLOTS + slot) * 128
                out_ref[core, :rows, XCOLS + k * 128 : XCOLS + k * 128 + 128] = in_ref[
                    :, pl.ds(pl.multiple_of(at, 128), 128)
                ]
                out_ref[core, :rows, k * 128 : k * 128 + 128] = in_ref[
                    :, pl.ds(pl.multiple_of(DI + at, 128), 128)
                ]
            out_ref[core, :rows, WIDTH:XBC] = in_ref[:, 2 * DI :]
            wanted = jnp.where(lane < LOCAL_HEADS, (lane // 2) * 8 + slot * 2 + lane % 2, -1)
            out_ref[core, :rows, XBC:XCOLS] = nn(
                dt_ref[...], jnp.where(source == wanted, 1.0, 0.0).astype(BF)
            ).astype(BF)


def pack_weights(xi, in_w, dt_w, small):
    rows = in_w.shape[0]
    small = pad_rows(pad_cols(small[None], XCOLS + WIDTH))
    return pl.pallas_call(
        pack_kernel,
        in_specs=[pl.BlockSpec(memory_space=pltpu.SMEM)] + [pl.BlockSpec(memory_space=pltpu.VMEM)] * 3,
        out_specs=[pl.BlockSpec(memory_space=pltpu.VMEM)] * 2,
        out_shape=[jax.ShapeDtypeStruct((2, r, XCOLS + WIDTH), BF) for r in (rows + 8, rows)],
        cost_estimate=pl.CostEstimate(flops=10**8, bytes_accessed=3 * 10**6, transcendentals=0),
        name="pack_weights",
    )(xi[None].astype(jnp.int32), in_w, dt_w, small)


def pair_kernel(at_ref, keep_ref, got_ref, send_ref, stay_ref):
    rows = keep_ref.shape[1]
    mine = pl.ds(pl.multiple_of(at_ref[0] * rows, rows), rows)
    other = pl.ds(pl.multiple_of((1 - at_ref[0]) * rows, rows), rows)
    for out, core in ((send_ref, 1 - at_ref[1]), (stay_ref, at_ref[1])):
        out[mine, :] = keep_ref[core]
        out[other, :] = got_ref[core, :rows]


def pair_rows(xi, ci, keep, got):
    shape = (2 * keep.shape[1], keep.shape[2])
    return pl.pallas_call(
        pair_kernel,
        in_specs=[pl.BlockSpec(memory_space=pltpu.SMEM)] + [pl.BlockSpec(memory_space=pltpu.VMEM)] * 2,
        out_specs=[pl.BlockSpec(memory_space=pltpu.VMEM)] * 2,
        out_shape=[jax.ShapeDtypeStruct(shape, BF)] * 2,
        cost_estimate=pl.CostEstimate(flops=0, bytes_accessed=2 * 10**6, transcendentals=0),
        name="pair_rows",
    )(jnp.stack([xi, ci]).astype(jnp.int32), keep, got)


def place_kernel(at_ref, stay_ref, got_ref, x_ref, z_ref):
    rows = stay_ref.shape[0]
    for index, ref in ((at_ref[0], stay_ref), (1 - at_ref[0], got_ref)):
        at = pl.ds(pl.multiple_of(index * rows, rows), rows)
        x_ref[at, :] = ref[:, :XCOLS]
        z_ref[at, :] = ref[:, XCOLS:]


def place_rows(index, stay, got):
    rows = 2 * stay.shape[0]
    return pl.pallas_call(
        place_kernel,
        in_specs=[pl.BlockSpec(memory_space=pltpu.SMEM)] + [pl.BlockSpec(memory_space=pltpu.VMEM)] * 2,
        out_specs=[pl.BlockSpec(memory_space=pltpu.VMEM)] * 2,
        out_shape=[jax.ShapeDtypeStruct((rows, XCOLS), BF), jax.ShapeDtypeStruct((rows, WIDTH), BF)],
        cost_estimate=pl.CostEstimate(flops=0, bytes_accessed=2 * 10**6, transcendentals=0),
        name="place_rows",
    )(index[None].astype(jnp.int32), stay, got)


def assemble_kernel(at_ref, pz_ref, gz_ref, px_ref, gx_ref, in_ref, dt_ref, out_ref, dt_out_ref, sum_ref):
    rows = in_ref.shape[0]
    total = jnp.zeros((rows, 128), F32)
    shared = [jnp.zeros((rows, 128), F32), jnp.zeros((rows, 128), F32)]
    dt_total = jnp.zeros((rows, HEADS), F32)
    lane = lax.broadcasted_iota(jnp.int32, (128, HEADS), 0)
    place = lax.broadcasted_iota(jnp.int32, (128, HEADS), 1)
    for core in range(2):
        for mine in (True, False):
            x = at_ref[0] if mine else 1 - at_ref[0]
            slot = 2 * core + x
            z_of = (lambda cols: pz_ref[core, x, :, cols]) if mine else (lambda cols: gz_ref[core, :, cols])
            x_of = (lambda cols: px_ref[core, x, :, cols]) if mine else (lambda cols: gx_ref[core, :, cols])
            for k in range(AHEADS):
                cols = slice(k * 128, k * 128 + 128)
                at = (k * SLOTS + slot) * 128
                for value, start in ((z_of(cols), at), (x_of(cols), DI + at)):
                    lanes = pl.ds(pl.multiple_of(start, 128), 128)
                    value = value.astype(F32)
                    out_ref[:, lanes] = value
                    total = total + value * in_ref[:, lanes].astype(F32)
            for k in range(2):
                shared[k] = shared[k] + x_of(slice(WIDTH + k * 128, WIDTH + k * 128 + 128)).astype(F32)
            wanted = jnp.where(lane < LOCAL_HEADS, (lane // 2) * 8 + slot * 2 + lane % 2, -1)
            dt_total = dt_total + nn(x_of(slice(XBC, XCOLS)), jnp.where(place == wanted, 1.0, 0.0).astype(BF))
    for k in range(2):
        cols = slice(2 * DI + k * 128, 2 * DI + k * 128 + 128)
        out_ref[:, cols] = shared[k]
        total = total + shared[k] * in_ref[:, cols].astype(F32)
    dt_out_ref[...] = dt_total
    rows_sum = jnp.sum(total, axis=1, keepdims=True) + jnp.sum(
        dt_total * dt_ref[...].astype(F32), axis=1, keepdims=True
    )
    sum_ref[...] = jnp.broadcast_to(rows_sum, (rows, 128))


def assemble_rows(xi, z_pair, z_got, x_pair, x_got, in_w, dt_w):
    rows = in_w.shape[0]
    return pl.pallas_call(
        assemble_kernel,
        in_specs=[pl.BlockSpec(memory_space=pltpu.SMEM)] + [pl.BlockSpec(memory_space=pltpu.VMEM)] * 6,
        out_specs=[pl.BlockSpec(memory_space=pltpu.VMEM)] * 3,
        out_shape=[
            jax.ShapeDtypeStruct(in_w.shape, F32),
            jax.ShapeDtypeStruct(dt_w.shape, F32),
            jax.ShapeDtypeStruct((rows, 128), F32),
        ],
        cost_estimate=pl.CostEstimate(flops=10**7, bytes_accessed=5 * 10**6, transcendentals=0),
        name="assemble_rows",
    )(xi[None].astype(jnp.int32), z_pair, z_got, x_pair, x_got, in_w, dt_w)


def swap_x(v):
    return lax.ppermute(v, "x", SWAP)


def swap_core(v):
    return lax.ppermute(v, "core", SWAP)


def pick(v, index, axis=0):
    return lax.dynamic_index_in_dim(v, index, axis, keepdims=False)


def joined(index, mine, other, axis):
    return jnp.where(
        index == 0,
        jnp.concatenate([mine, other], axis=axis),
        jnp.concatenate([other, mine], axis=axis),
    )


def from_slots(v):
    slots, rows, cols = v.shape
    return (
        v.reshape(slots, rows, AHEADS, cols // AHEADS)
        .transpose(1, 2, 0, 3)
        .reshape(rows, slots * cols)
    )


class Return:
    def __init__(self, block):
        self.xi, self.ci = lax.axis_index("x"), lax.axis_index("core")
        self.rows = block.shape[0] // 4
        self.halves = block.astype(BF).reshape(2, 2 * self.rows, -1)
        self.flying = swap_core(pick(self.halves, 1 - self.ci))

    def turn(self, chain):
        got = chain.take(self.flying)
        pair = joined(self.ci, pick(self.halves, self.ci)[None], got[None], 0)
        self.pair = pair.reshape(2, 2, self.rows, -1)
        self.flying = swap_x(pick(self.pair, 1 - self.xi, 1))

    def land(self, chain):
        self.got = chain.take(self.flying)


class Chain:
    def __init__(self):
        self.last = ()

    def tie(self, value):
        return lax.optimization_barrier((value, self.last))[0]

    def mark(self, value):
        self.last = value
        return value

    def take(self, value):
        return self.mark(self.tie(value))


class Ring:
    def __init__(self):
        self.size = len(CYCLE)
        place = [CYCLE.index(i) for i in range(self.size)]
        position = jnp.asarray(place, jnp.int32)[lax.axis_index("ra")]
        cycle = jnp.asarray(CYCLE, jnp.int32)
        steps = jnp.arange(self.size, dtype=jnp.int32)
        self.order = cycle[(position + steps) % self.size]
        self.inverse = (jnp.asarray(place, jnp.int32) - position) % self.size

    def pairs(self, d):
        return [(CYCLE[i], CYCLE[(i + d) % self.size]) for i in range(self.size)]

    def right(self, v):
        return lax.ppermute(v, "ra", self.pairs(1))

    def left(self, v):
        return lax.ppermute(v, "ra", self.pairs(-1))


class Gather:
    def __init__(self, ring, block):
        self.ring = ring
        self.rights, self.lefts = [block], [block]

    def start(self):
        r, l = self.rights[-1], self.lefts[-1]
        if len(self.rights) == 4:
            half = r.shape[0] // 2
            r, l = r[:half], l[half:]
        self.flying = self.ring.right(r), self.ring.left(l)

    def land(self, chain):
        r, l = chain.take(self.flying)
        self.rights.append(r)
        self.lefts.append(l)

    def blocks(self):
        r, l = self.rights, self.lefts
        return [r[0], l[1], l[2], l[3], jnp.concatenate([r[4], l[4]], axis=0), r[3], r[2], r[1]]


class Scatter:
    def __init__(self, ring, block):
        self.ring, self.block, self.count = ring, block, 0

    def start(self):
        block, ring, k = self.block, self.ring, self.count
        self.count += 1
        if k == 0:
            far = block(4)
            half = far.shape[0] // 2
            sends = far[:half], far[half:]
        elif k == 1:
            up, down = self.next
            half = up.shape[0] // 2
            r, l = self.right.astype(F32), self.left.astype(F32)
            sends = (
                jnp.concatenate([up[:half] + r, up[half:]], axis=0),
                jnp.concatenate([down[:half], down[half:] + l], axis=0),
            )
        else:
            sends = self.next[0] + self.right.astype(F32), self.next[1] + self.left.astype(F32)
        self.flying = ring.right(sends[0].astype(BF)), ring.left(sends[1].astype(BF))
        self.next = (block(3 - k), block(5 + k)) if k < 3 else (block(0),)

    def land(self, chain):
        self.right, self.left = chain.take(self.flying)

    def total(self):
        return self.next[0] + self.right.astype(F32) + self.left.astype(F32)


def flat_index(sizes):
    index = 0
    for name, size in zip(ALL, sizes):
        index = index * size + lax.axis_index(name)
    return index


class SmallSum:
    def __init__(self, v, sizes):
        self.value = v
        self.count = int(np.prod(sizes))
        self.bits = [2, 4, 8, 16, 1]

    def start(self):
        bit = self.bits.pop(0)
        self.flying = lax.ppermute(self.value, ALL, [(i, i ^ bit) for i in range(self.count)])

    def land(self, chain):
        self.value = self.value + chain.take(self.flying)


def permute_blocks(v, order, width):
    return jnp.concatenate(
        [
            lax.dynamic_slice(v, (0, order[k] * width), (v.shape[0], width))
            for k in range(v.shape[1] // width)
        ],
        axis=1,
    )


def pad_rows(v, rows=8):
    return jnp.concatenate([v, jnp.zeros((rows - v.shape[0], v.shape[1]), v.dtype)], axis=0)


def pad_cols(v, cols):
    return jnp.concatenate([v, jnp.zeros(v.shape[:-1] + (cols - v.shape[-1],), v.dtype)], axis=-1)


def per_device(
    sizes, tokens_short, tokens_long, cot_short, cot_long, seq_lengths,
    norm_gain, in_w, dt_w, conv_w, conv_b, dt_bias, a_log, d_skip, gate_gain, out_w,
):
    ringed = sizes == (8, 2, 1, 2)
    short, long = tokens_short.shape[0], tokens_long.shape[0]
    xi, ci = lax.axis_index("x"), lax.axis_index("core")
    slot = ci * 2 + xi
    feature = D // AHEADS
    mine_cols = lambda v: pick(v.reshape(v.shape[0], AHEADS, SLOTS, -1), slot, 2).reshape(v.shape[0], -1)
    chain = Chain()

    if ringed:
        ring = Ring()
        order, inverse = ring.order, ring.inverse
        from_ring = lambda v: permute_blocks(v, inverse, feature)
    else:
        order = jnp.arange(AHEADS, dtype=jnp.int32)
        from_ring = lambda v: v

    width = conv_w.shape[1]
    pieces = [conv_w.reshape(-1), conv_b, norm_gain, gate_gain]
    ends = np.cumsum([0] + [p.shape[0] for p in pieces])
    small = jnp.concatenate(pieces)
    group = ("core", "x")
    everyone = lambda v: lax.all_gather(v, group, axis=0, tiled=True)

    def stage(v, bit):
        count = int(np.prod(sizes))
        return lax.ppermute(v, ALL, [(i, i ^ bit) for i in range(count)])

    def widen(v, got, bit):
        return joined((flat_index(sizes) // bit) % 2, v, got, 0)

    if ringed:
        rows, n = in_w.shape[0], small.shape[0]
        x_send, x_keep = chain.mark(pack_weights(xi, in_w, dt_w, small))
        x_got = chain.take(swap_x(x_send))
        small = widen(small[None], x_got[0, rows : rows + 1, :n], 1)
        passing = stage(small, 2)
        send, stay = chain.mark(pair_rows(xi, ci, x_keep, x_got))
        got = swap_core(send)
        small = widen(small, chain.take(passing), 2)
        passing = stage(small, 4)
        got = chain.take(got)
        small = widen(small, chain.take(passing), 4)
        passing = stage(small, 8)
        x_block, z_block = chain.mark(place_rows(ci, stay, got))
        small = widen(small, chain.take(passing), 8)
        small = widen(small, chain.take(stage(small, 16)), 16)
        gather_x = Gather(ring, chain.tie(x_block))
        gather_x.start()
    else:
        small = lax.all_gather(small[None], ALL, axis=0, tiled=True)
    norm_full = pad_rows(small[:, ends[2] : ends[3]].reshape(1, -1).astype(F32))
    u_own = chain.mark(norm_tokens(order, [chain.tie(tokens_short), tokens_long], norm_full))
    xh = everyone(u_own)
    if ringed:
        gather_x.land(chain)
        gather_x.start()

    small, dt_bias, a_log, d_skip, cot_s, cot_l = chain.mark(
        chain.tie((small, dt_bias, a_log, d_skip, cot_short, cot_long))
    )
    live_s = (jnp.arange(short) < seq_lengths[0, 0]).astype(F32)[:, None]
    live_l = (jnp.arange(long) < seq_lengths[1, 0]).astype(F32)[:, None]
    dv_own = chain.mark(jnp.concatenate([(live_s * cot_s).astype(BF), (live_l * cot_l).astype(BF)], axis=0))
    taps = small[:, : ends[2]].reshape(-1, KERNEL + 1, width)
    taps = taps.transpose(1, 0, 2).reshape(KERNEL + 1, -1).astype(F32)
    taps = jnp.concatenate([mine_cols(taps[:, :DI]), taps[:, DI:]], axis=1)
    conv_taps, conv_bias = pad_rows(taps[:KERNEL]), pad_rows(taps[KERNEL:])
    gate_mine = pad_rows(mine_cols(small[:, ends[3] :].reshape(1, -1).astype(F32)))
    neg_rate = -jnp.exp(a_log.astype(F32))
    heads = pad_rows(pad_cols(mine_cols(jnp.stack([dt_bias.astype(F32), neg_rate])), 128))
    skip = pad_rows(jnp.repeat(mine_cols(d_skip.astype(F32)[None]), HEAD_DIM, axis=1))
    head_rows = np.arange(128)[:, None]
    seg = jnp.asarray(
        (head_rows < 2 * LOCAL_HEADS) & (head_rows % LOCAL_HEADS == np.arange(WIDTH)[None, :] // HEAD_DIM), BF
    )
    spread = jnp.asarray(
        (head_rows < 3 * LOCAL_HEADS)
        & (head_rows % LOCAL_HEADS == np.arange(128 * LOCAL_HEADS)[None, :] // 128),
        BF,
    )
    seq_params = (conv_taps, conv_bias, heads, skip, seg, spread)
    slots = [jnp.int32(k) for k in range(SLOTS)]

    if ringed:
        gather_x.land(chain)
        gather_x.start()
        gather_x.land(chain)
        gather_x.start()
        gather_x.land(chain)
        o_block, z_block = chain.tie((out_w, z_block))
        gather_o, gather_z = Gather(ring, o_block), Gather(ring, z_block)
        both = gather_o, gather_z
        gather_o.start()
        gather_z.start()
        w_x = chain.mark(jnp.concatenate(gather_x.blocks(), axis=0))
        xh = chain.take(xh)
        dv = everyone(chain.tie(dv_own))
        for gather in both:
            gather.land(chain)
            gather.start()
        proj = chain.mark(nn(chain.tie(xh), w_x))
        for gather in both:
            gather.land(chain)
            gather.start()
        kept = chain.mark(ssd_forward(slots[:2], chain.tie(proj), *seq_params))
        for gather in both:
            gather.land(chain)
            gather.start()
        y, act, slope, states = chain.mark(ssd_forward(slots[2:], chain.tie(proj), *seq_params, earlier=kept))
        for gather in both:
            gather.land(chain)
        w_all = chain.mark(jnp.concatenate([w_x, jnp.concatenate(gather_z.blocks(), axis=0)], axis=1))
        z = chain.mark(nn(chain.tie(xh), w_all[:, XCOLS:]).astype(BF))
        w_o = jnp.zeros((WIDTH, D), BF)
        for k, block in enumerate(gather_o.blocks()):
            w_o = lax.dynamic_update_slice(w_o, chain.tie(block), (order[k] * (WIDTH // AHEADS), 0))
        w_o = chain.mark(w_o)
        dv = chain.take(dv)
        dn = chain.mark(nt(dv, w_o).astype(BF))
    else:
        full = lax.all_gather(in_w, ALL, axis=0, tiled=True)
        full_dt = lax.all_gather(dt_w, ALL, axis=0, tiled=True)
        full_out = lax.all_gather(out_w, ALL, axis=0, tiled=True)
        w_z = mine_cols(full[:, :DI])
        w_x = jnp.concatenate(
            [mine_cols(full[:, DI : 2 * DI]), full[:, 2 * DI :], pad_cols(mine_cols(full_dt), 128)], axis=-1
        )
        w_o = pick(full_out.reshape(AHEADS, SLOTS, 128, D), slot, 1).reshape(WIDTH, D)
        dv = everyone(dv_own)
        proj = nn(xh, w_x)
        y, act, slope, states = ssd_forward(slots, proj, *seq_params)
        dn = nt(dv, w_o).astype(BF)
        z = nn(xh, w_z).astype(BF)
        w_all = jnp.concatenate([w_x, w_z], axis=1)

    straight = jnp.arange(AHEADS, dtype=jnp.int32)
    st = chain.mark(gate_stats(straight, y, chain.tie(z), dn, gate_mine))
    st = st + swap_core(st)
    st = st + swap_x(st)
    n, dy, dz = chain.mark(gate_backward(straight, st, y, z, dn, gate_mine))

    own = short + long
    rows_of = lambda v, start, count: lax.dynamic_slice(v, (start * own, 0), (count * own, v.shape[1]))

    def unit_product(dx, start, count):
        dx = chain.tie(dx)
        return nt(rows_of(dx, start, count), w_all)

    here = (jnp.arange(SLOTS) == slot).astype(F32)
    spread_cols = lambda v: (v.reshape(v.shape[0], AHEADS, 1, -1) * here[:, None]).reshape(v.shape[0], -1)

    def small_terms(acc, hacc):
        conv_part = jnp.concatenate([spread_cols(acc[:5, :WIDTH]), acc[:5, WIDTH:]], axis=1)
        skip_part = jnp.sum(acc[5, :WIDTH].reshape(LOCAL_HEADS, HEAD_DIM), axis=1)
        head_part = spread_cols(jnp.stack([hacc[0, :LOCAL_HEADS], hacc[1, :LOCAL_HEADS], skip_part]))
        return jnp.concatenate([conv_part.reshape(-1), head_part.reshape(-1)])

    def backward_call(steps, earlier):
        return chain.mark(
            ssd_backward(steps, chain.tie(proj), act, slope, dy, dz, states, *seq_params, earlier=earlier)
        )

    far, mid = 2 * (1 - ci), 2 * ci + 1 - xi
    g_out = chain.mark(tn(n, dv).astype(BF))
    reduced = lambda v, axes: lax.psum_scatter(v, axes, scatter_dimension=0, tiled=True)
    if ringed:
        own_out = reduced(g_out, "ra").astype(F32)
        g_z = chain.mark(tn(chain.tie(xh), dz))
        blocks_z = g_z.reshape(AHEADS, -1, WIDTH)
        scatter_z = Scatter(ring, lambda k: blocks_z[k])
        scatter_z.start()
    else:
        g_z = tn(xh, dz)
    branch = chain.mark(nn(chain.tie(n), w_o).astype(BF))
    branch = reduced(branch, group)
    if ringed:
        scatter_z.land(chain)
        scatter_z.start()
        dx, acc, hacc = backward_call([far, far + 1], ())
        scatter_z.land(chain)
        scatter_z.start()
        far_u = swap_core(chain.mark(unit_product(dx, far, 2).astype(BF)))
        scatter_z.land(chain)
        scatter_z.start()
        dx, acc2, hacc2 = backward_call([mid], (chain.tie(dx),))
        acc, hacc = acc + acc2, hacc + hacc2
        far_u = chain.take(far_u)
        mid_u = chain.mark(
            (unit_product(dx, mid, 1) + rows_of(far_u, 1 - xi, 1).astype(F32)).astype(BF)
        )
        mid_u = swap_x(mid_u)
        scatter_z.land(chain)
        back_z = Return(chain.mark(scatter_z.total()))
        dx, acc2, hacc2 = backward_call([slot], (chain.tie(dx),))
        acc, hacc = acc + acc2, hacc + hacc2
        scatter_x = Scatter(
            ring, lambda k: chain.mark(tn(xh[:, k * feature : (k + 1) * feature], chain.tie(dx)[:, :XCOLS]))
        )
        scatter_x.start()
        scatter_x.land(chain)
        scatter_x.start()
        back_z.turn(chain)
        tally = SmallSum(small_terms(*chain.tie((acc, hacc))), sizes)
        tally.start()
        scatter_x.land(chain)
        scatter_x.start()
        tally.land(chain)
        tally.start()
        du_own = chain.mark(unit_product(dx, slot, 1) + rows_of(far_u, xi, 1).astype(F32))
        scatter_x.land(chain)
        scatter_x.start()
        tally.land(chain)
        tally.start()
        back_z.land(chain)
        mid_u = chain.take(mid_u)
        du = du_own + mid_u.astype(F32)
        scatter_x.land(chain)
        back_x = Return(chain.mark(scatter_x.total()))
        tally.land(chain)
        tally.start()
        back_x.turn(chain)
        tally.land(chain)
        tally.start()
    else:
        dx, acc, hacc = backward_call(slots, ())
        du = reduced(nt(dx, w_all), group)
        g_x = tn(xh, dx[:, :XCOLS])
        total = lax.psum(small_terms(acc, hacc), ALL)
    v_s, v_l = branch[:short].astype(F32), branch[short:].astype(F32)
    du_s, du_l = du[:short], du[short:]

    out_short = (tokens_short.astype(F32) + live_s * v_s).astype(BF)
    out_long = (tokens_long.astype(F32) + live_l * v_l).astype(BF)

    def token_grad(token, cot, d_u):
        residual = token.astype(F32)
        row_scale = lax.rsqrt(jnp.mean(residual * residual, axis=-1, keepdims=True) + EPS)
        unit = residual * row_scale
        d_norm = from_ring(d_u) * norm_full[0:1]
        return cot.astype(F32) + row_scale * (d_norm - unit * jnp.mean(d_norm * unit, axis=-1, keepdims=True))

    grad_short, grad_long = chain.mark(
        (token_grad(tokens_short, cot_short, du_s), token_grad(tokens_long, cot_long, du_l))
    )

    if ringed:
        back_x.land(chain)
        grad_in_w, grad_dt_w, norm_sum = chain.mark(
            assemble_rows(xi, back_z.pair, back_z.got, back_x.pair, back_x.got, in_w, dt_w)
        )
        norm_sum = norm_sum[:, 0]
        tally.land(chain)
        total = tally.value
    else:
        here = (jnp.arange(SLOTS) == slot).astype(F32)
        wider = lambda v: (v.reshape(D, AHEADS, 1, -1) * here[:, None]).reshape(D, -1)
        reduce = lambda v: lax.psum_scatter(v, ALL, scatter_dimension=0, tiled=True)
        grad_in_w = reduce(
            jnp.concatenate([wider(g_z), wider(g_x[:, :WIDTH]), g_x[:, WIDTH:XBC]], axis=1)
        )
        grad_dt_w = reduce(wider(g_x[:, XBC : XBC + LOCAL_HEADS]))
        own_out = reduce(
            (g_out.astype(F32).reshape(AHEADS, 1, 128, D) * here[:, None, None]).reshape(DI, D)
        )

        norm_sum = jnp.sum(in_w.astype(F32) * grad_in_w, axis=1) + jnp.sum(dt_w.astype(F32) * grad_dt_w, axis=1)

    grad_norm_gain = norm_sum / norm_gain.astype(F32)
    grad_gate_gain = jnp.sum(out_w.astype(F32) * own_out, axis=1) / gate_gain.astype(F32)

    conv_total = total[: 5 * (DI + 2 * STATE)].reshape(5, -1)
    head_total = total[5 * (DI + 2 * STATE) :].reshape(3, HEADS)
    own_conv = lax.dynamic_slice(conv_total, (0, flat_index(sizes) * width), (5, width))
    return (
        out_short,
        out_long,
        grad_short,
        grad_long,
        grad_norm_gain,
        grad_in_w,
        grad_dt_w,
        own_conv[:KERNEL],
        own_conv[KERNEL],
        head_total[0],
        head_total[1] * neg_rate,
        head_total[2],
        grad_gate_gain,
        own_out,
    )


def solution(mesh):
    wide, narrow = mesh.shape["wide"], mesh.shape["narrow"]
    sizes = (wide // 2, 2, narrow // 2, 2)
    split = Mesh(mesh.devices.reshape(sizes), ALL)
    rows, vector, columns = P(ALL, None), P(ALL), P(None, ALL)
    return jax.shard_map(
        functools.partial(per_device, sizes),
        mesh=split,
        in_specs=(
            rows, rows, rows, rows, columns, vector, rows, rows, columns, vector, P(), P(), P(), vector, rows,
        ),
        out_specs=(
            rows, rows, rows, rows, vector, rows, rows, columns, vector, P(), P(), P(), vector, rows,
        ),
        check_vma=False,
    )
```

```python
import functools

import jax
import jax.numpy as jnp
import numpy as np
from jax import lax
from jax.experimental import pallas as pl
from jax.experimental.pallas import tpu as pltpu
from jax.sharding import Mesh
from jax.sharding import PartitionSpec as P

D = 2048
DI = 4096
HEADS = 64
HEAD_DIM = 64
STATE = 128
KERNEL = 4
SPAN = 256
EPS = 1e-05
BF = jnp.bfloat16
F32 = jnp.float32

SLOTS = 4
AHEADS = 8
WIDTH = DI // SLOTS
LOCAL_HEADS = HEADS // SLOTS
XBC = WIDTH + 2 * STATE
XCOLS = XBC + 128
ALL = ("ra", "core", "rb", "x")
NEG = -1e30
TILE = 640
HEAD = 128

SWAP = [(0, 1), (1, 0)]
CYCLE = (0, 2, 4, 6, 7, 5, 3, 1)


def nt(a, b):
    return lax.dot_general(a, b, (((1,), (1,)), ((), ())), preferred_element_type=F32)


def nn(a, b):
    return lax.dot_general(a, b, (((1,), (0,)), ((), ())), preferred_element_type=F32)


def tn(a, b):
    return lax.dot_general(a, b, (((0,), (0,)), ((), ())), preferred_element_type=F32)


LOG2E = 1.4426950408889634
ROWS = 64


def sigmoid(v):
    return 0.5 * jnp.tanh(0.5 * v) + 0.5


def lane_index():
    return lax.broadcasted_iota(jnp.int32, (1, 128), 1)


def three_parts(values):
    values = jnp.where(lane_index() < LOCAL_HEADS, values, 0.0)
    high = values.astype(BF).astype(F32)
    rest = values - high
    mid = rest.astype(BF).astype(F32)
    low = rest - mid
    return (high + pltpu.roll(mid, LOCAL_HEADS, 1) + pltpu.roll(low, 2 * LOCAL_HEADS, 1)).astype(BF)


def add_parts(values):
    return values + pltpu.roll(values, 128 - LOCAL_HEADS, 1) + pltpu.roll(values, 128 - 2 * LOCAL_HEADS, 1)


def triangle(n, lower):
    i = lax.broadcasted_iota(jnp.int32, (n, n), 0)
    j = lax.broadcasted_iota(jnp.int32, (n, n), 1)
    return jnp.where(i >= j if lower else i <= j, 1.0, 0.0).astype(BF)


def running_sum(values, lower):
    return add_parts(nn(triangle(values.shape[0], lower), three_parts(values)))


def two_parts(values):
    values = jnp.where(lane_index() < LOCAL_HEADS, values, 0.0)
    high = values.astype(BF).astype(F32)
    return (high + pltpu.roll(values - high, LOCAL_HEADS, 1)).astype(BF)


def softplus(v):
    return jnp.maximum(v, 0.0) + jnp.log1p(jnp.exp(-jnp.abs(v)))


def conv_tile(p_ref, cw_ref, cb_ref, r0, cols):
    starts = (r0 == 0) | (r0 == HEAD)
    before = p_ref[pl.ds(pl.multiple_of(jnp.maximum(r0 - 8, 0), 8), 8), cols]
    before = jnp.where(starts, 0.0, before)
    here = p_ref[pl.ds(r0, ROWS), cols]
    both = jnp.concatenate([before, here], axis=0)
    back = [here] + [pltpu.roll(both, m, 0)[8:] for m in (1, 2, 3)]
    total = cb_ref[0:1, cols]
    for m in range(KERNEL):
        total = total + cw_ref[3 - m : 4 - m, cols] * back[m]
    return total, back


def fwd_kernel(
    steps_ref, p_ref, cw_ref, cb_ref, hp_ref, dsk_ref, seg_ref, bc_ref, *refs
):
    y_ref, act_ref, slope_ref, h_ref, dt_s, parts_s, grow_s, rt_s, g_s = refs[-9:]
    lane = lane_index()

    def conv_step(i, carry):
        r0 = pl.multiple_of(i * ROWS, ROWS)
        rows = pl.ds(r0, ROWS)
        for c in range(XBC // 128):
            cols = slice(c * 128, c * 128 + 128)
            conv, _ = conv_tile(p_ref, cw_ref, cb_ref, r0, cols)
            gate = sigmoid(conv)
            act = conv * gate
            act_ref[rows, cols] = act.astype(BF)
            slope_ref[rows, cols] = (gate + act * (1.0 - gate)).astype(BF)
        dt_s[rows, :] = softplus(p_ref[rows, XBC:] + hp_ref[0:1])
        return carry

    lax.fori_loop(0, TILE // ROWS, conv_step, 0)
    rate = hp_ref[1:2]

    def block(off, q, read_state, make_state):
        rows = pl.ds(off, q)
        dt = dt_s[rows, :]
        cum2 = running_sum(dt * rate, True) * LOG2E
        parts_s[:q, :] = three_parts(cum2)
        turned = (cum2 - jnp.log2(dt)).T
        for h in range(LOCAL_HEADS):
            rt_s[h, :, :q] = turned[h : h + 1]
        b = act_ref[rows, WIDTH : WIDTH + STATE]
        c = act_ref[rows, WIDTH + STATE :]
        g_s[:q, :q] = nt(c, b)
        if read_state:
            grow_s[:q, :] = two_parts(jnp.exp2(cum2))
        if make_state:
            grow_s[:q, :] = two_parts(jnp.exp2(cum2[q - 1 : q] - cum2) * dt)
            b_turned = b.astype(F32).T.astype(BF)
        diagonal = lax.broadcasted_iota(jnp.int32, (128, 128), 0) >= lax.broadcasted_iota(
            jnp.int32, (128, 128), 1
        )

        def pair(p, carry):
            lanes = pl.ds(pl.multiple_of(p * 128, 128), 128)
            x2 = act_ref[rows, lanes]
            zero = jnp.zeros_like(x2)
            x_heads = [jnp.where(lane < HEAD_DIM, x2, zero), jnp.where(lane < HEAD_DIM, zero, x2)]
            cols = nn(parts_s[:q, :], bc_ref[:, pl.ds(pl.multiple_of(p * 256, 256), 256)])
            if read_state:
                carried = nn(grow_s[:q, :], seg_ref[:, lanes]) * nn(c, h_ref[0, :, lanes].astype(BF))
            for rt in range(q // 128):
                top = rt * 128
                mixes = []
                for j in range(2):
                    col = cols[top : top + 128, j * 128 : j * 128 + 128]
                    for ct in range(rt + 1):
                        lo = ct * 128
                        spread = col - rt_s[p * 2 + j, :, lo : lo + 128]
                        if ct == rt:
                            spread = jnp.where(diagonal, spread, NEG)
                        mixes.append((g_s[top : top + 128, lo : lo + 128] * jnp.exp2(spread)).astype(BF))
                x_both = jnp.concatenate([x[: top + 128] for x in x_heads], axis=0)
                out = nn(jnp.concatenate(mixes, axis=1), x_both)
                out = out + dsk_ref[0:1, lanes] * x2[top : top + 128].astype(F32)
                if read_state:
                    out = out + carried[top : top + 128]
                y_ref[pl.ds(off + top, 128), lanes] = out.astype(y_ref.dtype)
            if make_state:
                wide = nn(grow_s[:q, :], seg_ref[:, lanes])
                h_ref[0, :, lanes] = nn(b_turned, (wide * x2.astype(F32)).astype(BF))
            return carry

        lax.fori_loop(0, LOCAL_HEADS // 2, pair, 0, unroll=True)

    block(0, HEAD, False, False)
    block(HEAD, SPAN, False, True)
    block(HEAD + SPAN, SPAN, True, False)


def bwd_kernel(
    steps_ref, p_ref, act_ref, slope_ref, dy_ref, dz_ref, h_ref, cw_ref, hp_ref, dsk_ref, seg_ref, bc_ref, sofar_ref, *refs
):
    dp_ref, acc_ref = refs[-17:-15]
    heads_at = slice(XBC, XCOLS)
    dt_s, parts_s, grow_s, ct_s, gt_s, dgt_s, kc_s, kr_s, fold_s, dbc_s, ds_s, da_s, dst_s, after_s, sums_s = refs[-15:]
    lane = lane_index()
    head_row = lax.broadcasted_iota(jnp.int32, (LOCAL_HEADS, 1), 0)

    @pl.when(pl.program_id(0) == 0)
    def _():
        acc_ref[...] = sofar_ref[...]

    rate = hp_ref[1:2]
    dt_s[...] = softplus(p_ref[:, XBC:] + hp_ref[0:1])

    def block(off, q, state_in, state_out):
        rows = pl.ds(off, q)
        dt = dt_s[rows, :]
        cum2 = running_sum(dt * rate, True) * LOG2E
        parts_s[:q, :] = three_parts(cum2 - jnp.log2(dt))
        turned = cum2.T
        for h in range(LOCAL_HEADS):
            ct_s[h, :, :q] = turned[h : h + 1]
        b = act_ref[rows, WIDTH : WIDTH + STATE]
        c = act_ref[rows, WIDTH + STATE :]
        gt_s[:q, :q] = nt(b, c)
        dgt_s[:q, :q] = jnp.zeros((q, q), F32)
        kc_s[:q, :] = jnp.zeros((q, 128), F32)
        kr_s[:, :q] = jnp.zeros((LOCAL_HEADS, q), F32)
        if state_in or state_out:
            fold_s[:q, :] = jnp.zeros((q, 128), F32)
            dbc_s[:q, :] = jnp.zeros((q, 128), F32)
        if state_in:
            grow_s[:q, :] = two_parts(jnp.exp2(cum2))
            c_turned = c.astype(F32).T.astype(BF)
        if state_out:
            decay = jnp.exp2(cum2[q - 1 : q] - cum2)
            grow_s[:q, :] = two_parts(decay * dt)
        diagonal = lax.broadcasted_iota(jnp.int32, (128, 128), 1) >= lax.broadcasted_iota(
            jnp.int32, (128, 128), 0
        )
        tiles = q // 128

        def pair(p, carry):
            lanes = pl.ds(pl.multiple_of(p * 128, 128), 128)
            x2 = act_ref[rows, lanes]
            dy2 = dy_ref[rows, lanes]
            zero = jnp.zeros_like(dy2)
            dy_heads = [jnp.where(lane < HEAD_DIM, dy2, zero), jnp.where(lane < HEAD_DIM, zero, dy2)]
            cols = nn(parts_s[:q, :], bc_ref[:, pl.ds(pl.multiple_of(p * 256, 256), 256)])
            if state_in:
                hb = h_ref[0, :, lanes].astype(BF)
                dyc = dy2.astype(F32) * nn(grow_s[:q, :], seg_ref[:, lanes])
                dyb = dyc.astype(BF)
                fold_s[:q, :] += nt((dyc * nn(c, hb)).astype(BF), seg_ref[:, lanes])
                dbc_s[:q, :] += nt(dyb, hb)
                ds_s[:, lanes] = nn(c_turned, dyb).astype(BF)
            if state_out:
                sb = ds_s[:, lanes]
                wide = nn(grow_s[:q, :], seg_ref[:, lanes])
                bd = nn(b, sb)
                xf = x2.astype(F32)
                fold_s[:q, :] += nt((xf * bd).astype(BF), seg_ref[:, lanes])
                dbc_s[:q, :] += nt((wide * xf).astype(BF), sb)
                late = wide * bd
            picks = [jnp.where(lane == p * 2 + j, 1.0, 0.0).astype(BF) for j in range(2)]
            marks = [jnp.where(head_row == p * 2 + j, 1.0, 0.0).astype(BF) for j in range(2)]
            for jt in range(tiles):
                lo = jt * 128
                span = q - lo
                xj = x2[lo : lo + 128]
                mixes = []
                terms = []
                dgs = [None] * tiles
                for j in range(2):
                    col = cols[lo : lo + 128, j * 128 : j * 128 + 128]
                    for it in range(jt, tiles):
                        at = it * 128
                        spread = ct_s[p * 2 + j, :, at : at + 128] - col
                        if it == jt:
                            spread = jnp.where(diagonal, spread, NEG)
                        e = jnp.exp2(spread)
                        score = gt_s[lo : lo + 128, at : at + 128]
                        dme = nt(xj, dy_heads[j][at : at + 128]) * e
                        dgs[it] = dme if dgs[it] is None else dgs[it] + dme
                        terms.append((dme * score).astype(BF))
                        mixes.append((score * e).astype(BF))
                for it in range(jt, tiles):
                    dgt_s[lo : lo + 128, it * 128 : it * 128 + 128] += dgs[it]
                half = len(terms) // 2
                kc_s[lo : lo + 128, :] += nn(
                    jnp.concatenate(terms, axis=1),
                    jnp.concatenate([jnp.broadcast_to(v, (span, 128)) for v in picks], axis=0),
                )
                kr_s[:, lo:q] += nn(
                    jnp.concatenate([jnp.broadcast_to(v, (LOCAL_HEADS, 128)) for v in marks], axis=1),
                    jnp.concatenate(
                        [jnp.concatenate(terms[:half], axis=1), jnp.concatenate(terms[half:], axis=1)], axis=0
                    ),
                )
                dy_both = jnp.concatenate([d[lo:] for d in dy_heads], axis=0)
                out = nn(jnp.concatenate(mixes, axis=1), dy_both)
                dyj = dy2[lo : lo + 128].astype(F32)
                acc_ref[5:6, lanes] += jnp.sum(dyj * xj.astype(F32), axis=0, keepdims=True)
                out = out + dsk_ref[0:1, lanes] * dyj
                if state_out:
                    out = out + late[lo : lo + 128]
                da_s[pl.ds(off + lo, 128), lanes] = out
            return carry

        lax.fori_loop(0, LOCAL_HEADS // 2, pair, 0, unroll=True)

        dgt = dgt_s[:q, :q].astype(BF)
        db = nn(dgt, c)
        dc = tn(dgt, b)
        kcol = kc_s[:q, :]
        row_terms = jnp.concatenate([kr_s[:, :q], jnp.zeros((128 - LOCAL_HEADS, q), F32)], axis=0)
        d_cum = row_terms.T - kcol
        inverse = jnp.where(dt > 1e-30, 1.0 / jnp.maximum(dt, 1e-30), 0.0)
        d_dt = kcol * inverse
        if state_in:
            d_cum = d_cum + fold_s[:q, :]
            dc = dc + dbc_s[:q, :]
        if state_out:
            db = db + dbc_s[:q, :]
            d_weights = fold_s[:q, :]
            d_dt = d_dt + d_weights * decay
            w_term = d_weights * decay * dt
            last = lax.broadcasted_iota(jnp.int32, (q, 1), 0) == q - 1
            d_cum = d_cum - w_term + jnp.where(last, jnp.sum(w_term, axis=0, keepdims=True), 0.0)
        da_s[rows, WIDTH : WIDTH + STATE] = db
        da_s[rows, WIDTH + STATE :] = dc
        d_rate = running_sum(d_cum, False)
        dst_s[rows, :] = d_dt + d_rate * rate
        acc_ref[1:2, heads_at] += jnp.sum(d_rate * dt, axis=0, keepdims=True)

    block(0, HEAD, False, False)
    block(HEAD + SPAN, SPAN, True, False)
    block(HEAD, SPAN, False, True)

    d_soft = dst_s[...] * jax.nn.sigmoid(p_ref[:, XBC:] + hp_ref[0:1])
    d_soft = jnp.where(lane < LOCAL_HEADS, d_soft, 0.0)
    acc_ref[0:1, heads_at] += jnp.sum(d_soft, axis=0, keepdims=True)
    dp_ref[:, XBC:XCOLS] = d_soft.astype(BF)
    dp_ref[:, XCOLS:] = dz_ref[...]
    sums_s[...] = jnp.zeros_like(sums_s)
    after_s[...] = jnp.zeros_like(after_s)

    def conv_step(i, carry):
        r0 = pl.multiple_of(TILE - ROWS - i * ROWS, ROWS)
        rows = pl.ds(r0, ROWS)
        ends = (r0 + ROWS == HEAD) | (r0 + ROWS == TILE)
        fold = lambda v: jnp.sum(v.reshape(ROWS // 8, 8, 128), axis=0)
        for c in range(XBC // 128):
            cols = slice(c * 128, c * 128 + 128)
            here = p_ref[rows, cols]
            d_conv = da_s[rows, cols] * slope_ref[rows, cols].astype(F32)
            both = jnp.concatenate([d_conv, jnp.where(ends, 0.0, after_s[:, cols])], axis=0)
            after_s[:, cols] = d_conv[:8]
            total = cw_ref[3:4, cols] * d_conv
            sums_s[3, :, cols] += fold(d_conv * here)
            sums_s[4, :, cols] += fold(d_conv)
            for m in (1, 2, 3):
                ahead = pltpu.roll(both, ROWS + 8 - m, 0)[:ROWS]
                total = total + cw_ref[3 - m : 4 - m, cols] * ahead
                sums_s[3 - m, :, cols] += fold(ahead * here)
            dp_ref[rows, cols] = total.astype(BF)
        return carry

    lax.fori_loop(0, TILE // ROWS, conv_step, 0)
    for k in range(KERNEL + 1):
        acc_ref[k : k + 1, :XBC] += jnp.sum(sums_s[k], axis=0, keepdims=True)


def stats_kernel(order_ref, y_ref, z_ref, dn_ref, gain_ref, st_ref, both_s):
    lane = lane_index()

    def step(i, carry):
        rows = pl.ds(pl.multiple_of(i * ROWS, ROWS), ROWS)
        p1 = jnp.zeros((ROWS, 128), F32)
        p2 = jnp.zeros((ROWS, 128), F32)
        for k in range(AHEADS):
            lanes = pl.ds(pl.multiple_of(order_ref[k] * 128, 128), 128)
            z = z_ref[rows, lanes].astype(F32)
            g = y_ref[rows, lanes].astype(F32) * (z * sigmoid(z))
            p1 = p1 + g * g
            p2 = p2 + g * (dn_ref[rows, k * 128 : k * 128 + 128].astype(F32) * gain_ref[0:1, lanes])
        both_s[rows, :] = jnp.where(
            lane == 0,
            jnp.sum(p1, axis=1, keepdims=True),
            jnp.where(lane == 1, jnp.sum(p2, axis=1, keepdims=True), 0.0),
        )
        return carry

    lax.fori_loop(0, y_ref.shape[0] // ROWS, step, 0)
    st_ref[...] = both_s[...].T[0:8]


def gate_kernel(order_ref, st_ref, y_ref, z_ref, dn_ref, gain_ref, n_ref, dy_ref, dz_ref, st_s):
    st_s[...] = jnp.concatenate([st_ref[...], jnp.zeros((120, y_ref.shape[0]), F32)], axis=0).T

    def step(i, carry):
        rows = pl.ds(pl.multiple_of(i * ROWS, ROWS), ROWS)
        st = st_s[rows, :]
        rg = lax.rsqrt(st[:, 0:1] * (1.0 / DI) + EPS)
        mean = rg * rg * st[:, 1:2] * (1.0 / DI)
        for k in range(AHEADS):
            lanes = pl.ds(pl.multiple_of(order_ref[k] * 128, 128), 128)
            fixed = slice(k * 128, k * 128 + 128)
            gain = gain_ref[0:1, lanes]
            z = z_ref[rows, lanes].astype(F32)
            y = y_ref[rows, lanes].astype(F32)
            sg = sigmoid(z)
            silu = z * sg
            ghat = y * silu * rg
            dg = rg * (dn_ref[rows, fixed].astype(F32) * gain) - ghat * mean
            n_ref[rows, fixed] = (ghat * gain).astype(BF)
            dy_ref[rows, lanes] = (dg * silu).astype(BF)
            dz_ref[rows, lanes] = (dg * y * (sg + silu * (1.0 - sg))).astype(BF)
        return carry

    lax.fori_loop(0, y_ref.shape[0] // ROWS, step, 0)


def norm_kernel(pieces, order_ref, *refs):
    gain_ref, u_ref = refs[pieces], refs[-1]
    at = 0
    for x_ref in refs[:pieces]:
        count = x_ref.shape[0] // ROWS

        def step(i, carry, x_ref=x_ref, at=at):
            rows = pl.ds(pl.multiple_of(i * ROWS, ROWS), ROWS)
            out = pl.ds(pl.multiple_of(at + i * ROWS, ROWS), ROWS)
            total = jnp.zeros((ROWS, 128), F32)
            for k in range(D // 128):
                v = x_ref[rows, k * 128 : k * 128 + 128].astype(F32)
                total = total + v * v
            scale = lax.rsqrt(jnp.sum(total, axis=1, keepdims=True) * (1.0 / D) + EPS)
            for k in range(AHEADS):
                lanes = pl.ds(pl.multiple_of(order_ref[k] * 256, 256), 256)
                u_ref[out, k * 256 : k * 256 + 256] = (
                    x_ref[rows, lanes].astype(F32) * scale * gain_ref[0:1, lanes]
                ).astype(BF)
            return carry

        lax.fori_loop(0, count, step, 0)
        at += x_ref.shape[0]


def whole(shape):
    return pl.BlockSpec(shape, lambda i, s: (0,) * len(shape))


def placed(cols):
    return pl.BlockSpec((TILE, cols), lambda i, s: (s[i], 0))


def params():
    return pltpu.CompilerParams(vmem_limit_bytes=56 * 1024 * 1024)


def onto(earlier, first_input):
    specs = [pl.BlockSpec(memory_space=pl.ANY)] * len(earlier)
    return list(earlier), specs, {first_input + i: i for i in range(len(earlier))}


STATES = pl.BlockSpec((1, STATE, WIDTH), lambda i, s: (s[i], 0, 0))


def ssd_forward(steps, proj, conv_w, conv_b, heads, skip, seg, spread, earlier=()):
    tokens = proj.shape[0]
    count = len(steps)
    more, more_specs, aliases = onto(earlier, 8)
    return pl.pallas_call(
        fwd_kernel,
        grid_spec=pltpu.PrefetchScalarGridSpec(
            num_scalar_prefetch=1,
            grid=(count,),
            in_specs=[
                placed(XCOLS), whole((8, XBC)), whole((8, XBC)), whole((8, 128)), whole((8, WIDTH)),
                whole((128, WIDTH)), whole((128, 128 * LOCAL_HEADS)), *more_specs,
            ],
            out_specs=[placed(WIDTH), placed(XBC), placed(XBC), STATES],
            scratch_shapes=[
                pltpu.VMEM((TILE, 128), F32),
                pltpu.VMEM((SPAN, 128), BF),
                pltpu.VMEM((SPAN, 128), BF),
                pltpu.VMEM((LOCAL_HEADS, 1, SPAN), F32),
                pltpu.VMEM((SPAN, SPAN), F32),
            ],
        ),
        out_shape=[
            jax.ShapeDtypeStruct((tokens, WIDTH), BF),
            jax.ShapeDtypeStruct((tokens, XBC), BF),
            jax.ShapeDtypeStruct((tokens, XBC), BF),
            jax.ShapeDtypeStruct((tokens // TILE, STATE, WIDTH), F32),
        ],
        input_output_aliases=aliases,
        compiler_params=params(),
        cost_estimate=pl.CostEstimate(
            flops=count * 4 * 10**9, bytes_accessed=count * 6 * 10**6, transcendentals=count * 2 * 10**6
        ),
        name="ssd_forward",
    )(jnp.stack(steps).astype(jnp.int32), proj, conv_w, conv_b, heads, skip, seg, spread, *more)


def ssd_backward(steps, proj, act, slope, dy, dz, states, conv_w, conv_b, heads, skip, seg, spread, sofar, earlier=()):
    tokens = proj.shape[0]
    count = len(steps)
    more, more_specs, aliases = onto(earlier, 13)
    return pl.pallas_call(
        bwd_kernel,
        grid_spec=pltpu.PrefetchScalarGridSpec(
            num_scalar_prefetch=1,
            grid=(count,),
            in_specs=[
                placed(XCOLS), placed(XBC), placed(XBC), placed(WIDTH), placed(WIDTH), STATES, whole((8, XBC)),
                whole((8, 128)), whole((8, WIDTH)), whole((128, WIDTH)), whole((128, 128 * LOCAL_HEADS)),
                whole((8, XCOLS)), *more_specs,
            ],
            out_specs=[placed(XCOLS + WIDTH), whole((8, XCOLS))],
            scratch_shapes=[
                pltpu.VMEM((TILE, 128), F32),
                pltpu.VMEM((SPAN, 128), BF),
                pltpu.VMEM((SPAN, 128), BF),
                pltpu.VMEM((LOCAL_HEADS, 1, SPAN), F32),
                pltpu.VMEM((SPAN, SPAN), F32),
                pltpu.VMEM((SPAN, SPAN), F32),
                pltpu.VMEM((SPAN, 128), F32),
                pltpu.VMEM((LOCAL_HEADS, SPAN), F32),
                pltpu.VMEM((SPAN, 128), F32),
                pltpu.VMEM((SPAN, 128), F32),
                pltpu.VMEM((STATE, WIDTH), BF),
                pltpu.VMEM((TILE, XBC), F32),
                pltpu.VMEM((TILE, 128), F32),
                pltpu.VMEM((8, XBC), F32),
                pltpu.VMEM((KERNEL + 1, 8, XBC), F32),
            ],
        ),
        out_shape=[
            jax.ShapeDtypeStruct((tokens, XCOLS + WIDTH), BF),
            jax.ShapeDtypeStruct((8, XCOLS), F32),
        ],
        input_output_aliases=aliases,
        compiler_params=params(),
        cost_estimate=pl.CostEstimate(
            flops=count * 10 * 10**9, bytes_accessed=count * 9 * 10**6, transcendentals=count * 4 * 10**6
        ),
        name="ssd_backward",
    )(jnp.stack(steps).astype(jnp.int32), proj, act, slope, dy, dz, states, conv_w, heads, skip, seg, spread, sofar, *more)


def gate_stats(order, y, z, dn, gain):
    steps = y.shape[0] // TILE
    block = pl.BlockSpec((TILE, WIDTH), lambda i, o: (i, 0))
    return pl.pallas_call(
        stats_kernel,
        grid_spec=pltpu.PrefetchScalarGridSpec(
            num_scalar_prefetch=1,
            grid=(steps,),
            in_specs=[block, block, block, whole((8, WIDTH))],
            out_specs=pl.BlockSpec((8, TILE), lambda i, o: (0, i)),
            scratch_shapes=[pltpu.VMEM((TILE, 128), F32)],
        ),
        out_shape=jax.ShapeDtypeStruct((8, y.shape[0]), F32),
        compiler_params=params(),
        cost_estimate=pl.CostEstimate(flops=3 * 10**9, bytes_accessed=16 * 10**6, transcendentals=3 * 10**6),
        name="gate_stats",
    )(order, y, z, dn, gain)


def gate_backward(order, st, y, z, dn, gain):
    steps = y.shape[0] // TILE
    block = pl.BlockSpec((TILE, WIDTH), lambda i, o: (i, 0))
    return pl.pallas_call(
        gate_kernel,
        grid_spec=pltpu.PrefetchScalarGridSpec(
            num_scalar_prefetch=1,
            grid=(steps,),
            in_specs=[pl.BlockSpec((8, TILE), lambda i, o: (0, i)), block, block, block, whole((8, WIDTH))],
            out_specs=[block, block, block],
            scratch_shapes=[pltpu.VMEM((TILE, 128), F32)],
        ),
        out_shape=[jax.ShapeDtypeStruct(y.shape, BF)] * 3,
        compiler_params=params(),
        cost_estimate=pl.CostEstimate(flops=6 * 10**9, bytes_accessed=32 * 10**6, transcendentals=3 * 10**6),
        name="gate_backward",
    )(order, st, y, z, dn, gain)


def norm_tokens(order, values, gain):
    rows = sum(v.shape[0] for v in values)
    return pl.pallas_call(
        functools.partial(norm_kernel, len(values)),
        grid_spec=pltpu.PrefetchScalarGridSpec(
            num_scalar_prefetch=1,
            grid=(1,),
            in_specs=[*(whole(v.shape) for v in values), whole((8, D))],
            out_specs=[whole((rows, D))],
        ),
        out_shape=[jax.ShapeDtypeStruct((rows, D), BF)],
        compiler_params=params(),
        cost_estimate=pl.CostEstimate(flops=rows * 10**6, bytes_accessed=rows * 8192, transcendentals=rows),
        name="norm_tokens",
    )(order, *values, gain)[0]


def pack_kernel(at_ref, in_ref, dt_ref, small_ref, send_ref, keep_ref, z_send_ref, z_keep_ref):
    rows = in_ref.shape[0]
    send_ref[:, rows:, :] = jnp.zeros((2, 8, XCOLS), BF)
    send_ref[0, rows:, :] = small_ref[...]
    source = lax.broadcasted_iota(jnp.int32, (HEADS, 128), 0)
    lane = lax.broadcasted_iota(jnp.int32, (HEADS, 128), 1)
    for x_ref, z_ref, x in ((send_ref, z_send_ref, 1 - at_ref[0]), (keep_ref, z_keep_ref, at_ref[0])):
        for core in range(2):
            slot = 2 * core + x
            for k in range(AHEADS):
                cols = slice(k * 128, k * 128 + 128)
                at = (k * SLOTS + slot) * 128
                z_ref[core, :, cols] = in_ref[:, pl.ds(pl.multiple_of(at, 128), 128)]
                x_ref[core, :rows, cols] = in_ref[:, pl.ds(pl.multiple_of(DI + at, 128), 128)]
            x_ref[core, :rows, WIDTH:XBC] = in_ref[:, 2 * DI :]
            wanted = jnp.where(lane < LOCAL_HEADS, (lane // 2) * 8 + slot * 2 + lane % 2, -1)
            x_ref[core, :rows, XBC:XCOLS] = nn(
                dt_ref[...], jnp.where(source == wanted, 1.0, 0.0).astype(BF)
            ).astype(BF)


def pack_weights(xi, in_w, dt_w, small):
    rows = in_w.shape[0]
    small = pad_rows(pad_cols(small[None], XCOLS))
    shapes = [(2, rows + 8, XCOLS), (2, rows, XCOLS), (2, rows, WIDTH), (2, rows, WIDTH)]
    return pl.pallas_call(
        pack_kernel,
        in_specs=[pl.BlockSpec(memory_space=pltpu.SMEM)] + [pl.BlockSpec(memory_space=pltpu.VMEM)] * 3,
        out_specs=[pl.BlockSpec(memory_space=pltpu.VMEM)] * 4,
        out_shape=[jax.ShapeDtypeStruct(shape, BF) for shape in shapes],
        cost_estimate=pl.CostEstimate(flops=10**8, bytes_accessed=3 * 10**6, transcendentals=0),
        name="pack_weights",
    )(xi[None].astype(jnp.int32), in_w, dt_w, small)


def pair_kernel(at_ref, keep_ref, got_ref, send_ref, stay_ref):
    rows = keep_ref.shape[1]
    mine = pl.ds(pl.multiple_of(at_ref[0] * rows, rows), rows)
    other = pl.ds(pl.multiple_of((1 - at_ref[0]) * rows, rows), rows)
    for out, core in ((send_ref, 1 - at_ref[1]), (stay_ref, at_ref[1])):
        out[mine, :] = keep_ref[core]
        out[other, :] = got_ref[core, :rows]


def pair_rows(xi, ci, keep, got):
    shape = (2 * keep.shape[1], keep.shape[2])
    return pl.pallas_call(
        pair_kernel,
        in_specs=[pl.BlockSpec(memory_space=pltpu.SMEM)] + [pl.BlockSpec(memory_space=pltpu.VMEM)] * 2,
        out_specs=[pl.BlockSpec(memory_space=pltpu.VMEM)] * 2,
        out_shape=[jax.ShapeDtypeStruct(shape, BF)] * 2,
        cost_estimate=pl.CostEstimate(flops=0, bytes_accessed=2 * 10**6, transcendentals=0),
        name="pair_rows",
    )(jnp.stack([xi, ci]).astype(jnp.int32), keep, got)


def place_kernel(at_ref, stay_ref, got_ref, out_ref):
    rows = stay_ref.shape[0]
    for index, ref in ((at_ref[0], stay_ref), (1 - at_ref[0], got_ref)):
        out_ref[pl.ds(pl.multiple_of(index * rows, rows), rows), :] = ref[...]


def place_rows(index, stay, got):
    return pl.pallas_call(
        place_kernel,
        in_specs=[pl.BlockSpec(memory_space=pltpu.SMEM)] + [pl.BlockSpec(memory_space=pltpu.VMEM)] * 2,
        out_specs=pl.BlockSpec(memory_space=pltpu.VMEM),
        out_shape=jax.ShapeDtypeStruct((2 * stay.shape[0], stay.shape[1]), BF),
        cost_estimate=pl.CostEstimate(flops=0, bytes_accessed=2 * 10**6, transcendentals=0),
        name="place_rows",
    )(index[None].astype(jnp.int32), stay, got)


def assemble_kernel(at_ref, pz_ref, gz_ref, px_ref, gx_ref, in_ref, dt_ref, out_ref, dt_out_ref, sum_ref):
    rows = in_ref.shape[0]
    total = jnp.zeros((rows, 128), F32)
    shared = [jnp.zeros((rows, 128), F32), jnp.zeros((rows, 128), F32)]
    dt_total = jnp.zeros((rows, HEADS), F32)
    lane = lax.broadcasted_iota(jnp.int32, (128, HEADS), 0)
    place = lax.broadcasted_iota(jnp.int32, (128, HEADS), 1)
    for core in range(2):
        for mine in (True, False):
            x = at_ref[0] if mine else 1 - at_ref[0]
            slot = 2 * core + x
            z_of = (lambda cols: pz_ref[core, x, :, cols]) if mine else (lambda cols: gz_ref[core, :, cols])
            x_of = (lambda cols: px_ref[core, x, :, cols]) if mine else (lambda cols: gx_ref[core, :, cols])
            for k in range(AHEADS):
                cols = slice(k * 128, k * 128 + 128)
                at = (k * SLOTS + slot) * 128
                for value, start in ((z_of(cols), at), (x_of(cols), DI + at)):
                    lanes = pl.ds(pl.multiple_of(start, 128), 128)
                    value = value.astype(F32)
                    out_ref[:, lanes] = value
                    total = total + value * in_ref[:, lanes].astype(F32)
            for k in range(2):
                shared[k] = shared[k] + x_of(slice(WIDTH + k * 128, WIDTH + k * 128 + 128)).astype(F32)
            wanted = jnp.where(lane < LOCAL_HEADS, (lane // 2) * 8 + slot * 2 + lane % 2, -1)
            dt_total = dt_total + nn(x_of(slice(XBC, XCOLS)), jnp.where(place == wanted, 1.0, 0.0).astype(BF))
    for k in range(2):
        cols = slice(2 * DI + k * 128, 2 * DI + k * 128 + 128)
        out_ref[:, cols] = shared[k]
        total = total + shared[k] * in_ref[:, cols].astype(F32)
    dt_out_ref[...] = dt_total
    rows_sum = jnp.sum(total, axis=1, keepdims=True) + jnp.sum(
        dt_total * dt_ref[...].astype(F32), axis=1, keepdims=True
    )
    sum_ref[...] = jnp.broadcast_to(rows_sum, (rows, 128))


def assemble_rows(xi, z_pair, z_got, x_pair, x_got, in_w, dt_w):
    rows = in_w.shape[0]
    return pl.pallas_call(
        assemble_kernel,
        in_specs=[pl.BlockSpec(memory_space=pltpu.SMEM)] + [pl.BlockSpec(memory_space=pltpu.VMEM)] * 6,
        out_specs=[pl.BlockSpec(memory_space=pltpu.VMEM)] * 3,
        out_shape=[
            jax.ShapeDtypeStruct(in_w.shape, F32),
            jax.ShapeDtypeStruct(dt_w.shape, F32),
            jax.ShapeDtypeStruct((rows, 128), F32),
        ],
        cost_estimate=pl.CostEstimate(flops=10**7, bytes_accessed=5 * 10**6, transcendentals=0),
        name="assemble_rows",
    )(xi[None].astype(jnp.int32), z_pair, z_got, x_pair, x_got, in_w, dt_w)


def small_kernel(at_ref, own_ref, x_ref, far_ref, taps_ref, heads_ref):
    xi, ci = at_ref[0], at_ref[1]
    terms = (
        (2 * ci + xi, own_ref), (2 * ci + 1 - xi, x_ref),
        (2 - 2 * ci + xi, far_ref.at[0]), (3 - 2 * ci - xi, far_ref.at[1]),
    )
    shared = jnp.zeros((8, 2 * STATE), F32)
    heads = jnp.zeros((8, HEADS), F32)
    source = lax.broadcasted_iota(jnp.int32, (128, HEADS), 0)
    place = lax.broadcasted_iota(jnp.int32, (128, HEADS), 1)
    row = lax.broadcasted_iota(jnp.int32, (8, 1), 0)
    exact = functools.partial(
        lax.dot_general,
        dimension_numbers=(((1,), (0,)), ((), ())),
        precision=lax.Precision.HIGHEST,
        preferred_element_type=F32,
    )
    for slot, ref in terms:
        for k in range(AHEADS):
            cols = ref[:, k * 128 : k * 128 + 128]
            taps_ref[:, pl.ds(pl.multiple_of((k * SLOTS + slot) * 128, 128), 128)] = cols
            wanted = jnp.where(place == k * 8 + slot * 2 + source // HEAD_DIM, 1.0, 0.0)
            heads = heads + exact(jnp.where(row == 5, cols, 0.0), wanted)
        shared = shared + ref[:, WIDTH:XBC]
        wanted = jnp.where(
            (source < LOCAL_HEADS) & (place == (source // 2) * 8 + slot * 2 + source % 2), 1.0, 0.0
        )
        heads = heads + exact(jnp.where(row < 2, ref[:, XBC:], 0.0), wanted)
    taps_ref[:, DI:] = shared
    heads_ref[...] = heads


def assemble_small(xi, ci, own, x, far):
    return pl.pallas_call(
        small_kernel,
        in_specs=[pl.BlockSpec(memory_space=pltpu.SMEM)] + [pl.BlockSpec(memory_space=pltpu.VMEM)] * 3,
        out_specs=[pl.BlockSpec(memory_space=pltpu.VMEM)] * 2,
        out_shape=[jax.ShapeDtypeStruct((8, DI + 2 * STATE), F32), jax.ShapeDtypeStruct((8, HEADS), F32)],
        cost_estimate=pl.CostEstimate(flops=10**7, bytes_accessed=10**6, transcendentals=0),
        name="assemble_small",
    )(jnp.stack([xi, ci]).astype(jnp.int32), own, x, far)


def rows_kernel(order_ref, *refs):
    rows = refs[0].shape[0]
    out_ref = refs[-1]
    for k, (ref, shift) in enumerate(zip(refs[:-1], (0, 0, 0, 0, 0, rows // 2, 0, 0, 0))):
        at = order_ref[k if k < 5 else k - 1] * rows + shift
        out_ref[pl.ds(pl.multiple_of(at, rows // 2), ref.shape[0]), :] = ref[...]


def ordered_rows(order, blocks):
    rows, cols = blocks[0].shape
    return pl.pallas_call(
        rows_kernel,
        in_specs=[pl.BlockSpec(memory_space=pltpu.SMEM)] + [pl.BlockSpec(memory_space=pltpu.VMEM)] * len(blocks),
        out_specs=pl.BlockSpec(memory_space=pltpu.VMEM),
        out_shape=jax.ShapeDtypeStruct((AHEADS * rows, cols), BF),
        compiler_params=params(),
        cost_estimate=pl.CostEstimate(flops=0, bytes_accessed=8 * 10**6, transcendentals=0),
        name="ordered_rows",
    )(order, *blocks)


def swap_x(v):
    return lax.ppermute(v, "x", SWAP)


def swap_core(v):
    return lax.ppermute(v, "core", SWAP)


def pick(v, index, axis=0):
    return lax.dynamic_index_in_dim(v, index, axis, keepdims=False)


def joined(index, mine, other, axis):
    return jnp.where(
        index == 0,
        jnp.concatenate([mine, other], axis=axis),
        jnp.concatenate([other, mine], axis=axis),
    )


def from_slots(v):
    slots, rows, cols = v.shape
    return (
        v.reshape(slots, rows, AHEADS, cols // AHEADS)
        .transpose(1, 2, 0, 3)
        .reshape(rows, slots * cols)
    )


class Return:
    def __init__(self, block):
        self.xi, self.ci = lax.axis_index("x"), lax.axis_index("core")
        self.rows = block.shape[0] // 4
        self.halves = block.astype(BF).reshape(2, 2 * self.rows, -1)
        self.flying = swap_core(pick(self.halves, 1 - self.ci))

    def turn(self, chain):
        got = chain.take(self.flying)
        pair = joined(self.ci, pick(self.halves, self.ci)[None], got[None], 0)
        self.pair = pair.reshape(2, 2, self.rows, -1)
        self.flying = swap_x(pick(self.pair, 1 - self.xi, 1))

    def land(self, chain):
        self.got = chain.take(self.flying)


class Chain:
    def __init__(self):
        self.last = ()

    def tie(self, value):
        return lax.optimization_barrier((value, self.last))[0]

    def mark(self, value):
        self.last = value
        return value

    def take(self, value):
        return self.mark(self.tie(value))


class Ring:
    def __init__(self):
        self.size = len(CYCLE)
        place = [CYCLE.index(i) for i in range(self.size)]
        position = jnp.asarray(place, jnp.int32)[lax.axis_index("ra")]
        cycle = jnp.asarray(CYCLE, jnp.int32)
        steps = jnp.arange(self.size, dtype=jnp.int32)
        self.order = cycle[(position + steps) % self.size]
        self.inverse = (jnp.asarray(place, jnp.int32) - position) % self.size

    def pairs(self, d):
        return [(CYCLE[i], CYCLE[(i + d) % self.size]) for i in range(self.size)]

    def right(self, v):
        return lax.ppermute(v, "ra", self.pairs(1))

    def left(self, v):
        return lax.ppermute(v, "ra", self.pairs(-1))


class Gather:
    def __init__(self, ring, block):
        self.ring = ring
        self.rights, self.lefts = [block], [block]

    def start(self):
        r, l = self.rights[-1], self.lefts[-1]
        if len(self.rights) == 4:
            half = r.shape[0] // 2
            r, l = r[:half], l[half:]
        self.flying = self.ring.right(r), self.ring.left(l)

    def land(self, chain):
        r, l = chain.take(self.flying)
        self.rights.append(r)
        self.lefts.append(l)

    def pieces(self):
        r, l = self.rights, self.lefts
        return [r[0], l[1], l[2], l[3], r[4], l[4], r[3], r[2], r[1]]


class Scatter:
    def __init__(self, ring, block, chain):
        self.ring, self.block, self.chain, self.count = ring, block, chain, 0

    def start(self):
        block, ring, k = self.block, self.ring, self.count
        self.count += 1
        if k == 0:
            far = block(4)
            half = far.shape[0] // 2
            sends = far[:half], far[half:]
        elif k == 1:
            up, down = block(3), block(5)
            half = up.shape[0] // 2
            r, l = self.right.astype(F32), self.left.astype(F32)
            sends = (
                jnp.concatenate([up[:half] + r, up[half:]], axis=0),
                jnp.concatenate([down[:half], down[half:] + l], axis=0),
            )
        else:
            sends = block(4 - k) + self.right.astype(F32), block(4 + k) + self.left.astype(F32)
        sends = self.chain.mark((sends[0].astype(BF), sends[1].astype(BF)))
        self.flying = ring.right(sends[0]), ring.left(sends[1])

    def land(self, chain):
        self.right, self.left = chain.take(self.flying)

    def total(self):
        return self.block(0) + self.right.astype(F32) + self.left.astype(F32)


def flat_index(sizes):
    index = 0
    for name, size in zip(ALL, sizes):
        index = index * size + lax.axis_index(name)
    return index


class SmallSum:
    def __init__(self, v):
        self.value = v
        self.bits = [1, 2, 4]

    def start(self):
        bit = self.bits.pop(0)
        self.flying = lax.ppermute(self.value, "ra", [(i, i ^ bit) for i in range(len(CYCLE))])

    def land(self, chain):
        self.value = chain.mark(self.value + chain.take(self.flying))


def permute_blocks(v, order, width):
    return jnp.concatenate(
        [
            lax.dynamic_slice(v, (0, order[k] * width), (v.shape[0], width))
            for k in range(v.shape[1] // width)
        ],
        axis=1,
    )


def pad_rows(v, rows=8):
    return jnp.concatenate([v, jnp.zeros((rows - v.shape[0], v.shape[1]), v.dtype)], axis=0)


def pad_cols(v, cols):
    return jnp.concatenate([v, jnp.zeros(v.shape[:-1] + (cols - v.shape[-1],), v.dtype)], axis=-1)


def per_device(
    sizes, tokens_short, tokens_long, cot_short, cot_long, seq_lengths,
    norm_gain, in_w, dt_w, conv_w, conv_b, dt_bias, a_log, d_skip, gate_gain, out_w,
):
    ringed = sizes == (8, 2, 1, 2)
    short, long = tokens_short.shape[0], tokens_long.shape[0]
    xi, ci = lax.axis_index("x"), lax.axis_index("core")
    slot = ci * 2 + xi
    feature = D // AHEADS
    mine_cols = lambda v: pick(v.reshape(v.shape[0], AHEADS, SLOTS, -1), slot, 2).reshape(v.shape[0], -1)
    chain = Chain()

    if ringed:
        ring = Ring()
        order, inverse = ring.order, ring.inverse
        from_ring = lambda v: permute_blocks(v, inverse, feature)
    else:
        order = jnp.arange(AHEADS, dtype=jnp.int32)
        from_ring = lambda v: v

    width = conv_w.shape[1]
    pieces = [conv_w.reshape(-1), conv_b, norm_gain, gate_gain]
    ends = np.cumsum([0] + [p.shape[0] for p in pieces])
    small = jnp.concatenate(pieces)
    group = ("core", "x")
    everyone = lambda v: lax.all_gather(v, group, axis=0, tiled=True)

    def stage(v, bit):
        count = int(np.prod(sizes))
        return lax.ppermute(v, ALL, [(i, i ^ bit) for i in range(count)])

    def widen(v, got, bit):
        return joined((flat_index(sizes) // bit) % 2, v, got, 0)

    if ringed:
        rows, n = in_w.shape[0], small.shape[0]
        x_send, x_keep, z_send, z_keep = chain.mark(pack_weights(xi, in_w, dt_w, small))
        x_got = chain.take(swap_x(x_send))
        small = widen(small[None], x_got[0, rows : rows + 1, :n], 1)
        passing = stage(small, 2)
        send, stay = chain.mark(pair_rows(xi, ci, x_keep, x_got))
        got = swap_core(send)
        small = widen(small, chain.take(passing), 2)
        passing = stage(small, 4)
        got = chain.take(got)
        small = widen(small, chain.take(passing), 4)
        passing = stage(small, 8)
        x_block = chain.mark(place_rows(ci, stay, got))
        small = widen(small, chain.take(passing), 8)
        small = widen(small, chain.take(stage(small, 16)), 16)
        gather_x = Gather(ring, chain.tie(x_block))
        gather_x.start()
        z_got = swap_x(chain.tie(z_send))
    else:
        small = lax.all_gather(small[None], ALL, axis=0, tiled=True)
    norm_full = pad_rows(small[:, ends[2] : ends[3]].reshape(1, -1).astype(F32))
    u_own = chain.mark(norm_tokens(order, [chain.tie(tokens_short), tokens_long], norm_full))
    xh = everyone(u_own)
    if ringed:
        gather_x.land(chain)
        gather_x.start()

    small, dt_bias, a_log, d_skip, cot_s, cot_l = chain.mark(
        chain.tie((small, dt_bias, a_log, d_skip, cot_short, cot_long))
    )
    live_s = (jnp.arange(short) < seq_lengths[0, 0]).astype(F32)[:, None]
    live_l = (jnp.arange(long) < seq_lengths[1, 0]).astype(F32)[:, None]
    dv_own = chain.mark(jnp.concatenate([(live_s * cot_s).astype(BF), (live_l * cot_l).astype(BF)], axis=0))
    taps = small[:, : ends[2]].reshape(-1, KERNEL + 1, width)
    taps = taps.transpose(1, 0, 2).reshape(KERNEL + 1, -1).astype(F32)
    taps = jnp.concatenate([mine_cols(taps[:, :DI]), taps[:, DI:]], axis=1)
    conv_taps, conv_bias = pad_rows(taps[:KERNEL]), pad_rows(taps[KERNEL:])
    gate_mine = pad_rows(mine_cols(small[:, ends[3] :].reshape(1, -1).astype(F32)))
    neg_rate = -jnp.exp(a_log.astype(F32))
    heads = pad_rows(pad_cols(mine_cols(jnp.stack([dt_bias.astype(F32), neg_rate])), 128))
    skip = pad_rows(jnp.repeat(mine_cols(d_skip.astype(F32)[None]), HEAD_DIM, axis=1))
    head_rows = np.arange(128)[:, None]
    seg = jnp.asarray(
        (head_rows < 2 * LOCAL_HEADS) & (head_rows % LOCAL_HEADS == np.arange(WIDTH)[None, :] // HEAD_DIM), BF
    )
    spread = jnp.asarray(
        (head_rows < 3 * LOCAL_HEADS)
        & (head_rows % LOCAL_HEADS == np.arange(128 * LOCAL_HEADS)[None, :] // 128),
        BF,
    )
    gate_mine, *seq_params = chain.mark((gate_mine, conv_taps, conv_bias, heads, skip, seg, spread))
    if ringed:
        send, stay = chain.mark(pair_rows(xi, ci, z_keep, chain.take(z_got)))
        z_block = chain.mark(place_rows(ci, stay, chain.take(swap_core(send))))
    slots = [jnp.int32(k) for k in range(SLOTS)]

    if ringed:
        gather_x.land(chain)
        gather_x.start()
        gather_x.land(chain)
        gather_x.start()
        gather_z = Gather(ring, z_block)
        gather_z.start()
        gather_z.land(chain)
        gather_x.land(chain)
        w_x = chain.mark(jnp.concatenate(gather_x.pieces(), axis=0))
        xh = chain.take(xh)
        dv = everyone(chain.tie(dv_own))
        gather_z.start()
        gather_o = Gather(ring, chain.tie(out_w))
        gather_o.start()
        both = gather_o, gather_z
        proj = chain.mark(nn(chain.tie(xh), w_x))
        for gather in both:
            gather.land(chain)
            gather.start()
        kept = chain.mark(ssd_forward(slots[:2], chain.tie(proj), *seq_params))
        for gather in both:
            gather.land(chain)
            gather.start()
        y, act, slope, states = chain.mark(ssd_forward(slots[2:], chain.tie(proj), *seq_params, earlier=kept))
        for gather in both:
            gather.land(chain)
        gather_o.start()
        w_all = chain.mark(jnp.concatenate([w_x, jnp.concatenate(gather_z.pieces(), axis=0)], axis=1))
        z = chain.mark(nn(chain.tie(xh), w_all[:, XCOLS:]).astype(BF))
        gather_o.land(chain)
        w_o = chain.mark(ordered_rows(order, chain.tie(gather_o.pieces())))
        dv = chain.take(dv)
        dn = chain.mark(nt(dv, w_o).astype(BF))
    else:
        full = lax.all_gather(in_w, ALL, axis=0, tiled=True)
        full_dt = lax.all_gather(dt_w, ALL, axis=0, tiled=True)
        full_out = lax.all_gather(out_w, ALL, axis=0, tiled=True)
        w_z = mine_cols(full[:, :DI])
        w_x = jnp.concatenate(
            [mine_cols(full[:, DI : 2 * DI]), full[:, 2 * DI :], pad_cols(mine_cols(full_dt), 128)], axis=-1
        )
        w_o = pick(full_out.reshape(AHEADS, SLOTS, 128, D), slot, 1).reshape(WIDTH, D)
        dv = everyone(dv_own)
        proj = nn(xh, w_x)
        y, act, slope, states = ssd_forward(slots, proj, *seq_params)
        dn = nt(dv, w_o).astype(BF)
        z = nn(xh, w_z).astype(BF)
        w_all = jnp.concatenate([w_x, w_z], axis=1)

    straight = jnp.arange(AHEADS, dtype=jnp.int32)
    st = chain.mark(gate_stats(straight, y, chain.tie(z), dn, gate_mine))
    st = st + swap_core(st)
    st = st + swap_x(st)
    n, dy, dz = chain.mark(gate_backward(straight, st, y, z, dn, gate_mine))

    own = short + long
    rows_of = lambda v, start, count: lax.dynamic_slice(v, (start * own, 0), (count * own, v.shape[1]))

    def unit_product(dx, start, count):
        dx = chain.tie(dx)
        return nt(rows_of(dx, start, count), w_all)

    def backward_call(steps, sofar, earlier):
        return chain.mark(
            ssd_backward(steps, chain.tie(proj), act, slope, dy, dz, states, *seq_params, sofar, earlier=earlier)
        )

    none_yet = jnp.zeros((8, XCOLS), F32)

    far, mid = 2 * (1 - ci), 2 * ci + 1 - xi
    g_out = chain.mark(tn(n, dv).astype(BF))
    reduced = lambda v, axes: lax.psum_scatter(v, axes, scatter_dimension=0, tiled=True)
    if ringed:
        own_out = reduced(g_out, "ra").astype(F32)
        g_z = chain.mark(tn(chain.tie(xh), dz))
        blocks_z = g_z.reshape(AHEADS, -1, WIDTH)
        scatter_z = Scatter(ring, lambda k: blocks_z[k], chain)
        scatter_z.start()
    else:
        g_z = tn(xh, dz)
    branch = chain.mark(nn(chain.tie(n), w_o).astype(BF))
    branch = reduced(branch, group)
    if ringed:
        scatter_z.land(chain)
        scatter_z.start()
        dx, acc = backward_call([far, far + 1], none_yet, ())
        scatter_z.land(chain)
        scatter_z.start()
        far_u = swap_core(chain.mark(unit_product(dx, far, 2).astype(BF)))
        dx, acc = backward_call([mid], acc, (chain.tie(dx),))
        scatter_z.land(chain)
        scatter_z.start()
        far_u = chain.take(far_u)
        mid_u = chain.mark(
            (unit_product(dx, mid, 1) + rows_of(far_u, 1 - xi, 1).astype(F32)).astype(BF)
        )
        mid_u = swap_x(mid_u)
        dx, acc = backward_call([slot], acc, (chain.tie(dx),))
        scatter_z.land(chain)
        back_z = Return(chain.mark(scatter_z.total()))

        def blocks_x(first, last):
            part = tn(xh[:, first * feature : last * feature], chain.tie(dx)[:, :XCOLS])
            return dict(enumerate(chain.mark(part).reshape(last - first, feature, XCOLS), first))

        made = blocks_x(3, 6)
        scatter_x = Scatter(ring, lambda k: made[k], chain)
        scatter_x.start()
        made.update(blocks_x(0, 3))
        scatter_x.land(chain)
        scatter_x.start()
        made.update(blocks_x(6, 8))
        du_own = chain.mark(unit_product(dx, slot, 1) + rows_of(far_u, xi, 1).astype(F32))
        scatter_x.land(chain)
        scatter_x.start()
        back_z.turn(chain)
        tally = SmallSum(chain.tie(acc))
        tally.start()
        scatter_x.land(chain)
        scatter_x.start()
        tally.land(chain)
        tally.start()
        mid_u = chain.take(mid_u)
        du = chain.mark(du_own + mid_u.astype(F32))
        scatter_x.land(chain)
        back_x = Return(chain.mark(scatter_x.total()))
        tally.land(chain)
        tally.start()
        back_z.land(chain)
        back_x.turn(chain)
        tally.land(chain)
        acc = tally.value
        acc_x = chain.take(swap_x(acc))
        acc_far = swap_core(jnp.stack([acc, acc_x]))
    else:
        dx, acc = backward_call(slots, none_yet, ())
        du = reduced(nt(dx, w_all), group)
        g_x = tn(xh, dx[:, :XCOLS])
        acc = lax.psum(acc, ("ra", "rb"))
        acc_x = swap_x(acc)
        acc_far = swap_core(jnp.stack([acc, acc_x]))
        taps_total, head_total = assemble_small(xi, ci, acc, acc_x, acc_far)
    v_s, v_l = branch[:short].astype(F32), branch[short:].astype(F32)
    du_s, du_l = du[:short], du[short:]

    out_short = (tokens_short.astype(F32) + live_s * v_s).astype(BF)
    out_long = (tokens_long.astype(F32) + live_l * v_l).astype(BF)

    def token_grad(token, cot, d_u):
        residual = token.astype(F32)
        row_scale = lax.rsqrt(jnp.mean(residual * residual, axis=-1, keepdims=True) + EPS)
        unit = residual * row_scale
        d_norm = from_ring(d_u) * norm_full[0:1]
        return cot.astype(F32) + row_scale * (d_norm - unit * jnp.mean(d_norm * unit, axis=-1, keepdims=True))

    grad_short, grad_long = chain.mark(
        (token_grad(tokens_short, cot_short, du_s), token_grad(tokens_long, cot_long, du_l))
    )

    if ringed:
        back_x.land(chain)
        grad_in_w, grad_dt_w, norm_sum = chain.mark(
            assemble_rows(xi, back_z.pair, back_z.got, back_x.pair, back_x.got, in_w, dt_w)
        )
        norm_sum = norm_sum[:, 0]
        taps_total, head_total = assemble_small(xi, ci, acc, acc_x, chain.take(acc_far))
    else:
        here = (jnp.arange(SLOTS) == slot).astype(F32)
        wider = lambda v: (v.reshape(D, AHEADS, 1, -1) * here[:, None]).reshape(D, -1)
        reduce = lambda v: lax.psum_scatter(v, ALL, scatter_dimension=0, tiled=True)
        grad_in_w = reduce(
            jnp.concatenate([wider(g_z), wider(g_x[:, :WIDTH]), g_x[:, WIDTH:XBC]], axis=1)
        )
        grad_dt_w = reduce(wider(g_x[:, XBC : XBC + LOCAL_HEADS]))
        own_out = reduce(
            (g_out.astype(F32).reshape(AHEADS, 1, 128, D) * here[:, None, None]).reshape(DI, D)
        )

        norm_sum = jnp.sum(in_w.astype(F32) * grad_in_w, axis=1) + jnp.sum(dt_w.astype(F32) * grad_dt_w, axis=1)

    grad_norm_gain = norm_sum / norm_gain.astype(F32)
    grad_gate_gain = jnp.sum(out_w.astype(F32) * own_out, axis=1) / gate_gain.astype(F32)

    own_conv = lax.dynamic_slice(taps_total, (0, flat_index(sizes) * width), (KERNEL + 1, width))
    return (
        out_short,
        out_long,
        grad_short,
        grad_long,
        grad_norm_gain,
        grad_in_w,
        grad_dt_w,
        own_conv[:KERNEL],
        own_conv[KERNEL],
        head_total[0],
        head_total[1] * neg_rate,
        head_total[5],
        grad_gate_gain,
        own_out,
    )


def solution(mesh):
    wide, narrow = mesh.shape["wide"], mesh.shape["narrow"]
    sizes = (wide // 2, 2, narrow // 2, 2)
    split = Mesh(mesh.devices.reshape(sizes), ALL)
    rows, vector, columns = P(ALL, None), P(ALL), P(None, ALL)
    return jax.shard_map(
        functools.partial(per_device, sizes),
        mesh=split,
        in_specs=(
            rows, rows, rows, rows, columns, vector, rows, rows, columns, vector, P(), P(), P(), vector, rows,
        ),
        out_specs=(
            rows, rows, rows, rows, vector, rows, rows, columns, vector, P(), P(), P(), vector, rows,
        ),
        check_vma=False,
    )
```

```python
import functools

import jax
import jax.numpy as jnp
import numpy as np
from jax import lax
from jax.experimental import pallas as pl
from jax.experimental.pallas import tpu as pltpu
from jax.sharding import Mesh
from jax.sharding import PartitionSpec as P

D = 2048
DI = 4096
HEADS = 64
HEAD_DIM = 64
STATE = 128
KERNEL = 4
SPAN = 256
EPS = 1e-05
BF = jnp.bfloat16
F32 = jnp.float32

SLOTS = 4
AHEADS = 8
WIDTH = DI // SLOTS
LOCAL_HEADS = HEADS // SLOTS
XBC = WIDTH + 2 * STATE
XCOLS = XBC + 128
ALL = ("ra", "core", "rb", "x")
NEG = -1e30
TILE = 640
HEAD = 128

SWAP = [(0, 1), (1, 0)]
CYCLE = (0, 2, 4, 6, 7, 5, 3, 1)


def nt(a, b):
    return lax.dot_general(a, b, (((1,), (1,)), ((), ())), preferred_element_type=F32)


def nn(a, b):
    return lax.dot_general(a, b, (((1,), (0,)), ((), ())), preferred_element_type=F32)


def tn(a, b):
    return lax.dot_general(a, b, (((0,), (0,)), ((), ())), preferred_element_type=F32)


LOG2E = 1.4426950408889634
ROWS = 64


def sigmoid(v):
    return 0.5 * jnp.tanh(0.5 * v) + 0.5


def lane_index():
    return lax.broadcasted_iota(jnp.int32, (1, 128), 1)


def three_parts(values):
    values = jnp.where(lane_index() < LOCAL_HEADS, values, 0.0)
    high = values.astype(BF).astype(F32)
    rest = values - high
    mid = rest.astype(BF).astype(F32)
    low = rest - mid
    return (high + pltpu.roll(mid, LOCAL_HEADS, 1) + pltpu.roll(low, 2 * LOCAL_HEADS, 1)).astype(BF)


def add_parts(values):
    return values + pltpu.roll(values, 128 - LOCAL_HEADS, 1) + pltpu.roll(values, 128 - 2 * LOCAL_HEADS, 1)


def triangle(n, lower):
    i = lax.broadcasted_iota(jnp.int32, (n, n), 0)
    j = lax.broadcasted_iota(jnp.int32, (n, n), 1)
    return jnp.where(i >= j if lower else i <= j, 1.0, 0.0).astype(BF)


def running_sum(values, lower):
    return add_parts(nn(triangle(values.shape[0], lower), three_parts(values)))


def two_parts(values):
    values = jnp.where(lane_index() < LOCAL_HEADS, values, 0.0)
    high = values.astype(BF).astype(F32)
    return (high + pltpu.roll(values - high, LOCAL_HEADS, 1)).astype(BF)


def softplus(v):
    return jnp.maximum(v, 0.0) + jnp.log1p(jnp.exp(-jnp.abs(v)))


def conv_tile(p_ref, cw_ref, cb_ref, r0, cols):
    starts = (r0 == 0) | (r0 == HEAD)
    before = p_ref[pl.ds(pl.multiple_of(jnp.maximum(r0 - 8, 0), 8), 8), cols]
    before = jnp.where(starts, 0.0, before)
    here = p_ref[pl.ds(r0, ROWS), cols]
    both = jnp.concatenate([before, here], axis=0)
    back = [here] + [pltpu.roll(both, m, 0)[8:] for m in (1, 2, 3)]
    total = cb_ref[0:1, cols]
    for m in range(KERNEL):
        total = total + cw_ref[3 - m : 4 - m, cols] * back[m]
    return total, back


def fwd_kernel(
    steps_ref, p_ref, cw_ref, cb_ref, hp_ref, dsk_ref, seg_ref, bc_ref, *refs
):
    y_ref, act_ref, slope_ref, h_ref, dt_s, parts_s, grow_s, rt_s, g_s = refs[-9:]
    lane = lane_index()

    def conv_step(i, carry):
        r0 = pl.multiple_of(i * ROWS, ROWS)
        rows = pl.ds(r0, ROWS)
        for c in range(XBC // 128):
            cols = slice(c * 128, c * 128 + 128)
            conv, _ = conv_tile(p_ref, cw_ref, cb_ref, r0, cols)
            gate = sigmoid(conv)
            act = conv * gate
            act_ref[rows, cols] = act.astype(BF)
            slope_ref[rows, cols] = (gate + act * (1.0 - gate)).astype(BF)
        dt_s[rows, :] = softplus(p_ref[rows, XBC:] + hp_ref[0:1])
        return carry

    lax.fori_loop(0, TILE // ROWS, conv_step, 0)
    rate = hp_ref[1:2]

    def block(off, q, read_state, make_state):
        rows = pl.ds(off, q)
        dt = dt_s[rows, :]
        cum2 = running_sum(dt * rate, True) * LOG2E
        parts_s[:q, :] = three_parts(cum2)
        turned = (cum2 - jnp.log2(dt)).T
        for h in range(LOCAL_HEADS):
            rt_s[h, :, :q] = turned[h : h + 1]
        b = act_ref[rows, WIDTH : WIDTH + STATE]
        c = act_ref[rows, WIDTH + STATE :]
        g_s[:q, :q] = nt(c, b)
        if read_state:
            grow_s[:q, :] = two_parts(jnp.exp2(cum2))
        if make_state:
            grow_s[:q, :] = two_parts(jnp.exp2(cum2[q - 1 : q] - cum2) * dt)
            b_turned = b.astype(F32).T.astype(BF)
        diagonal = lax.broadcasted_iota(jnp.int32, (128, 128), 0) >= lax.broadcasted_iota(
            jnp.int32, (128, 128), 1
        )

        def pair(p, carry):
            lanes = pl.ds(pl.multiple_of(p * 128, 128), 128)
            x2 = act_ref[rows, lanes]
            zero = jnp.zeros_like(x2)
            x_heads = [jnp.where(lane < HEAD_DIM, x2, zero), jnp.where(lane < HEAD_DIM, zero, x2)]
            cols = nn(parts_s[:q, :], bc_ref[:, pl.ds(pl.multiple_of(p * 256, 256), 256)])
            if read_state:
                carried = nn(grow_s[:q, :], seg_ref[:, lanes]) * nn(c, h_ref[0, :, lanes].astype(BF))
            for rt in range(q // 128):
                top = rt * 128
                mixes = []
                for j in range(2):
                    col = cols[top : top + 128, j * 128 : j * 128 + 128]
                    for ct in range(rt + 1):
                        lo = ct * 128
                        spread = col - rt_s[p * 2 + j, :, lo : lo + 128]
                        if ct == rt:
                            spread = jnp.where(diagonal, spread, NEG)
                        mixes.append((g_s[top : top + 128, lo : lo + 128] * jnp.exp2(spread)).astype(BF))
                x_both = jnp.concatenate([x[: top + 128] for x in x_heads], axis=0)
                out = nn(jnp.concatenate(mixes, axis=1), x_both)
                out = out + dsk_ref[0:1, lanes] * x2[top : top + 128].astype(F32)
                if read_state:
                    out = out + carried[top : top + 128]
                y_ref[pl.ds(off + top, 128), lanes] = out.astype(y_ref.dtype)
            if make_state:
                wide = nn(grow_s[:q, :], seg_ref[:, lanes])
                h_ref[0, :, lanes] = nn(b_turned, (wide * x2.astype(F32)).astype(BF))
            return carry

        lax.fori_loop(0, LOCAL_HEADS // 2, pair, 0, unroll=True)

    block(0, HEAD, False, False)
    block(HEAD, SPAN, False, True)
    block(HEAD + SPAN, SPAN, True, False)


def bwd_kernel(
    steps_ref, p_ref, act_ref, slope_ref, dy_ref, dz_ref, h_ref, cw_ref, hp_ref, dsk_ref, seg_ref, bc_ref, sofar_ref, *refs
):
    dp_ref, acc_ref = refs[-17:-15]
    heads_at = slice(XBC, XCOLS)
    dt_s, parts_s, grow_s, ct_s, gt_s, dgt_s, kc_s, kr_s, fold_s, dbc_s, ds_s, da_s, dst_s, after_s, sums_s = refs[-15:]
    lane = lane_index()
    head_row = lax.broadcasted_iota(jnp.int32, (LOCAL_HEADS, 1), 0)

    @pl.when(pl.program_id(0) == 0)
    def _():
        acc_ref[...] = sofar_ref[...]

    rate = hp_ref[1:2]
    dt_s[...] = softplus(p_ref[:, XBC:] + hp_ref[0:1])

    def block(off, q, state_in, state_out):
        rows = pl.ds(off, q)
        dt = dt_s[rows, :]
        cum2 = running_sum(dt * rate, True) * LOG2E
        parts_s[:q, :] = three_parts(cum2 - jnp.log2(dt))
        turned = cum2.T
        for h in range(LOCAL_HEADS):
            ct_s[h, :, :q] = turned[h : h + 1]
        b = act_ref[rows, WIDTH : WIDTH + STATE]
        c = act_ref[rows, WIDTH + STATE :]
        gt_s[:q, :q] = nt(b, c)
        dgt_s[:q, :q] = jnp.zeros((q, q), F32)
        kc_s[:q, :] = jnp.zeros((q, 128), F32)
        kr_s[:, :q] = jnp.zeros((LOCAL_HEADS, q), F32)
        if state_in or state_out:
            fold_s[:q, :] = jnp.zeros((q, 128), F32)
            dbc_s[:q, :] = jnp.zeros((q, 128), F32)
        if state_in:
            grow_s[:q, :] = two_parts(jnp.exp2(cum2))
            c_turned = c.astype(F32).T.astype(BF)
        if state_out:
            decay = jnp.exp2(cum2[q - 1 : q] - cum2)
            grow_s[:q, :] = two_parts(decay * dt)
        diagonal = lax.broadcasted_iota(jnp.int32, (128, 128), 1) >= lax.broadcasted_iota(
            jnp.int32, (128, 128), 0
        )
        tiles = q // 128

        def pair(p, carry):
            lanes = pl.ds(pl.multiple_of(p * 128, 128), 128)
            x2 = act_ref[rows, lanes]
            dy2 = dy_ref[rows, lanes]
            zero = jnp.zeros_like(dy2)
            dy_heads = [jnp.where(lane < HEAD_DIM, dy2, zero), jnp.where(lane < HEAD_DIM, zero, dy2)]
            cols = nn(parts_s[:q, :], bc_ref[:, pl.ds(pl.multiple_of(p * 256, 256), 256)])
            if state_in:
                hb = h_ref[0, :, lanes].astype(BF)
                dyc = dy2.astype(F32) * nn(grow_s[:q, :], seg_ref[:, lanes])
                dyb = dyc.astype(BF)
                fold_s[:q, :] += nt((dyc * nn(c, hb)).astype(BF), seg_ref[:, lanes])
                dbc_s[:q, :] += nt(dyb, hb)
                ds_s[:, lanes] = nn(c_turned, dyb).astype(BF)
            if state_out:
                sb = ds_s[:, lanes]
                wide = nn(grow_s[:q, :], seg_ref[:, lanes])
                bd = nn(b, sb)
                xf = x2.astype(F32)
                fold_s[:q, :] += nt((xf * bd).astype(BF), seg_ref[:, lanes])
                dbc_s[:q, :] += nt((wide * xf).astype(BF), sb)
                late = wide * bd
            picks = [jnp.where(lane == p * 2 + j, 1.0, 0.0).astype(BF) for j in range(2)]
            marks = [jnp.where(head_row == p * 2 + j, 1.0, 0.0).astype(BF) for j in range(2)]
            for jt in range(tiles):
                lo = jt * 128
                span = q - lo
                xj = x2[lo : lo + 128]
                mixes = []
                terms = []
                dgs = [None] * tiles
                for j in range(2):
                    col = cols[lo : lo + 128, j * 128 : j * 128 + 128]
                    for it in range(jt, tiles):
                        at = it * 128
                        spread = ct_s[p * 2 + j, :, at : at + 128] - col
                        if it == jt:
                            spread = jnp.where(diagonal, spread, NEG)
                        e = jnp.exp2(spread)
                        score = gt_s[lo : lo + 128, at : at + 128]
                        dme = nt(xj, dy_heads[j][at : at + 128]) * e
                        dgs[it] = dme if dgs[it] is None else dgs[it] + dme
                        terms.append((dme * score).astype(BF))
                        mixes.append((score * e).astype(BF))
                for it in range(jt, tiles):
                    dgt_s[lo : lo + 128, it * 128 : it * 128 + 128] += dgs[it]
                half = len(terms) // 2
                kc_s[lo : lo + 128, :] += nn(
                    jnp.concatenate(terms, axis=1),
                    jnp.concatenate([jnp.broadcast_to(v, (span, 128)) for v in picks], axis=0),
                )
                kr_s[:, lo:q] += nn(
                    jnp.concatenate([jnp.broadcast_to(v, (LOCAL_HEADS, 128)) for v in marks], axis=1),
                    jnp.concatenate(
                        [jnp.concatenate(terms[:half], axis=1), jnp.concatenate(terms[half:], axis=1)], axis=0
                    ),
                )
                dy_both = jnp.concatenate([d[lo:] for d in dy_heads], axis=0)
                out = nn(jnp.concatenate(mixes, axis=1), dy_both)
                dyj = dy2[lo : lo + 128].astype(F32)
                acc_ref[5:6, lanes] += jnp.sum(dyj * xj.astype(F32), axis=0, keepdims=True)
                out = out + dsk_ref[0:1, lanes] * dyj
                if state_out:
                    out = out + late[lo : lo + 128]
                da_s[pl.ds(off + lo, 128), lanes] = out
            return carry

        lax.fori_loop(0, LOCAL_HEADS // 2, pair, 0, unroll=True)

        dgt = dgt_s[:q, :q].astype(BF)
        db = nn(dgt, c)
        dc = tn(dgt, b)
        kcol = kc_s[:q, :]
        row_terms = jnp.concatenate([kr_s[:, :q], jnp.zeros((128 - LOCAL_HEADS, q), F32)], axis=0)
        d_cum = row_terms.T - kcol
        inverse = jnp.where(dt > 1e-30, 1.0 / jnp.maximum(dt, 1e-30), 0.0)
        d_dt = kcol * inverse
        if state_in:
            d_cum = d_cum + fold_s[:q, :]
            dc = dc + dbc_s[:q, :]
        if state_out:
            db = db + dbc_s[:q, :]
            d_weights = fold_s[:q, :]
            d_dt = d_dt + d_weights * decay
            w_term = d_weights * decay * dt
            last = lax.broadcasted_iota(jnp.int32, (q, 1), 0) == q - 1
            d_cum = d_cum - w_term + jnp.where(last, jnp.sum(w_term, axis=0, keepdims=True), 0.0)
        da_s[rows, WIDTH : WIDTH + STATE] = db
        da_s[rows, WIDTH + STATE :] = dc
        d_rate = running_sum(d_cum, False)
        dst_s[rows, :] = d_dt + d_rate * rate
        acc_ref[1:2, heads_at] += jnp.sum(d_rate * dt, axis=0, keepdims=True)

    block(0, HEAD, False, False)
    block(HEAD + SPAN, SPAN, True, False)
    block(HEAD, SPAN, False, True)

    d_soft = dst_s[...] * jax.nn.sigmoid(p_ref[:, XBC:] + hp_ref[0:1])
    d_soft = jnp.where(lane < LOCAL_HEADS, d_soft, 0.0)
    acc_ref[0:1, heads_at] += jnp.sum(d_soft, axis=0, keepdims=True)
    dp_ref[:, XBC:XCOLS] = d_soft.astype(BF)
    dp_ref[:, XCOLS:] = dz_ref[...]
    sums_s[...] = jnp.zeros_like(sums_s)
    after_s[...] = jnp.zeros_like(after_s)

    def conv_step(i, carry):
        r0 = pl.multiple_of(TILE - ROWS - i * ROWS, ROWS)
        rows = pl.ds(r0, ROWS)
        ends = (r0 + ROWS == HEAD) | (r0 + ROWS == TILE)
        fold = lambda v: jnp.sum(v.reshape(ROWS // 8, 8, 128), axis=0)
        for c in range(XBC // 128):
            cols = slice(c * 128, c * 128 + 128)
            here = p_ref[rows, cols]
            d_conv = da_s[rows, cols] * slope_ref[rows, cols].astype(F32)
            both = jnp.concatenate([d_conv, jnp.where(ends, 0.0, after_s[:, cols])], axis=0)
            after_s[:, cols] = d_conv[:8]
            total = cw_ref[3:4, cols] * d_conv
            sums_s[3, :, cols] += fold(d_conv * here)
            sums_s[4, :, cols] += fold(d_conv)
            for m in (1, 2, 3):
                ahead = pltpu.roll(both, ROWS + 8 - m, 0)[:ROWS]
                total = total + cw_ref[3 - m : 4 - m, cols] * ahead
                sums_s[3 - m, :, cols] += fold(ahead * here)
            dp_ref[rows, cols] = total.astype(BF)
        return carry

    lax.fori_loop(0, TILE // ROWS, conv_step, 0)
    for k in range(KERNEL + 1):
        acc_ref[k : k + 1, :XBC] += jnp.sum(sums_s[k], axis=0, keepdims=True)


def stats_kernel(order_ref, y_ref, z_ref, dn_ref, gain_ref, st_ref, both_s):
    lane = lane_index()

    def step(i, carry):
        rows = pl.ds(pl.multiple_of(i * ROWS, ROWS), ROWS)
        p1 = jnp.zeros((ROWS, 128), F32)
        p2 = jnp.zeros((ROWS, 128), F32)
        for k in range(AHEADS):
            lanes = pl.ds(pl.multiple_of(order_ref[k] * 128, 128), 128)
            z = z_ref[rows, lanes].astype(F32)
            g = y_ref[rows, lanes].astype(F32) * (z * sigmoid(z))
            p1 = p1 + g * g
            p2 = p2 + g * (dn_ref[rows, k * 128 : k * 128 + 128].astype(F32) * gain_ref[0:1, lanes])
        both_s[rows, :] = jnp.where(
            lane == 0,
            jnp.sum(p1, axis=1, keepdims=True),
            jnp.where(lane == 1, jnp.sum(p2, axis=1, keepdims=True), 0.0),
        )
        return carry

    lax.fori_loop(0, y_ref.shape[0] // ROWS, step, 0)
    st_ref[...] = both_s[...].T[0:8]


def gate_kernel(order_ref, st_ref, y_ref, z_ref, dn_ref, gain_ref, n_ref, dy_ref, dz_ref, st_s):
    st_s[...] = jnp.concatenate([st_ref[...], jnp.zeros((120, y_ref.shape[0]), F32)], axis=0).T

    def step(i, carry):
        rows = pl.ds(pl.multiple_of(i * ROWS, ROWS), ROWS)
        st = st_s[rows, :]
        rg = lax.rsqrt(st[:, 0:1] * (1.0 / DI) + EPS)
        mean = rg * rg * st[:, 1:2] * (1.0 / DI)
        for k in range(AHEADS):
            lanes = pl.ds(pl.multiple_of(order_ref[k] * 128, 128), 128)
            fixed = slice(k * 128, k * 128 + 128)
            gain = gain_ref[0:1, lanes]
            z = z_ref[rows, lanes].astype(F32)
            y = y_ref[rows, lanes].astype(F32)
            sg = sigmoid(z)
            silu = z * sg
            ghat = y * silu * rg
            dg = rg * (dn_ref[rows, fixed].astype(F32) * gain) - ghat * mean
            n_ref[rows, fixed] = (ghat * gain).astype(BF)
            dy_ref[rows, lanes] = (dg * silu).astype(BF)
            dz_ref[rows, lanes] = (dg * y * (sg + silu * (1.0 - sg))).astype(BF)
        return carry

    lax.fori_loop(0, y_ref.shape[0] // ROWS, step, 0)


def norm_kernel(pieces, order_ref, *refs):
    gain_ref, u_ref = refs[pieces], refs[-1]
    at = 0
    for x_ref in refs[:pieces]:
        count = x_ref.shape[0] // ROWS

        def step(i, carry, x_ref=x_ref, at=at):
            rows = pl.ds(pl.multiple_of(i * ROWS, ROWS), ROWS)
            out = pl.ds(pl.multiple_of(at + i * ROWS, ROWS), ROWS)
            total = jnp.zeros((ROWS, 128), F32)
            for k in range(D // 128):
                v = x_ref[rows, k * 128 : k * 128 + 128].astype(F32)
                total = total + v * v
            scale = lax.rsqrt(jnp.sum(total, axis=1, keepdims=True) * (1.0 / D) + EPS)
            for k in range(AHEADS):
                lanes = pl.ds(pl.multiple_of(order_ref[k] * 256, 256), 256)
                u_ref[out, k * 256 : k * 256 + 256] = (
                    x_ref[rows, lanes].astype(F32) * scale * gain_ref[0:1, lanes]
                ).astype(BF)
            return carry

        lax.fori_loop(0, count, step, 0)
        at += x_ref.shape[0]


def whole(shape):
    return pl.BlockSpec(shape, lambda i, s: (0,) * len(shape))


def placed(cols):
    return pl.BlockSpec((TILE, cols), lambda i, s: (s[i], 0))


def params():
    return pltpu.CompilerParams(vmem_limit_bytes=56 * 1024 * 1024)


def onto(earlier, first_input):
    specs = [pl.BlockSpec(memory_space=pl.ANY)] * len(earlier)
    return list(earlier), specs, {first_input + i: i for i in range(len(earlier))}


STATES = pl.BlockSpec((1, STATE, WIDTH), lambda i, s: (s[i], 0, 0))


def ssd_forward(steps, proj, conv_w, conv_b, heads, skip, seg, spread, earlier=()):
    tokens = proj.shape[0]
    count = len(steps)
    more, more_specs, aliases = onto(earlier, 8)
    return pl.pallas_call(
        fwd_kernel,
        grid_spec=pltpu.PrefetchScalarGridSpec(
            num_scalar_prefetch=1,
            grid=(count,),
            in_specs=[
                placed(XCOLS), whole((8, XBC)), whole((8, XBC)), whole((8, 128)), whole((8, WIDTH)),
                whole((128, WIDTH)), whole((128, 128 * LOCAL_HEADS)), *more_specs,
            ],
            out_specs=[placed(WIDTH), placed(XBC), placed(XBC), STATES],
            scratch_shapes=[
                pltpu.VMEM((TILE, 128), F32),
                pltpu.VMEM((SPAN, 128), BF),
                pltpu.VMEM((SPAN, 128), BF),
                pltpu.VMEM((LOCAL_HEADS, 1, SPAN), F32),
                pltpu.VMEM((SPAN, SPAN), F32),
            ],
        ),
        out_shape=[
            jax.ShapeDtypeStruct((tokens, WIDTH), BF),
            jax.ShapeDtypeStruct((tokens, XBC), BF),
            jax.ShapeDtypeStruct((tokens, XBC), BF),
            jax.ShapeDtypeStruct((tokens // TILE, STATE, WIDTH), F32),
        ],
        input_output_aliases=aliases,
        compiler_params=params(),
        cost_estimate=pl.CostEstimate(
            flops=count * 4 * 10**9, bytes_accessed=count * 6 * 10**6, transcendentals=count * 2 * 10**6
        ),
        name="ssd_forward",
    )(jnp.stack(steps).astype(jnp.int32), proj, conv_w, conv_b, heads, skip, seg, spread, *more)


def ssd_backward(steps, proj, act, slope, dy, dz, states, conv_w, conv_b, heads, skip, seg, spread, sofar, earlier=()):
    tokens = proj.shape[0]
    count = len(steps)
    more, more_specs, aliases = onto(earlier, 13)
    return pl.pallas_call(
        bwd_kernel,
        grid_spec=pltpu.PrefetchScalarGridSpec(
            num_scalar_prefetch=1,
            grid=(count,),
            in_specs=[
                placed(XCOLS), placed(XBC), placed(XBC), placed(WIDTH), placed(WIDTH), STATES, whole((8, XBC)),
                whole((8, 128)), whole((8, WIDTH)), whole((128, WIDTH)), whole((128, 128 * LOCAL_HEADS)),
                whole((8, XCOLS)), *more_specs,
            ],
            out_specs=[placed(XCOLS + WIDTH), whole((8, XCOLS))],
            scratch_shapes=[
                pltpu.VMEM((TILE, 128), F32),
                pltpu.VMEM((SPAN, 128), BF),
                pltpu.VMEM((SPAN, 128), BF),
                pltpu.VMEM((LOCAL_HEADS, 1, SPAN), F32),
                pltpu.VMEM((SPAN, SPAN), F32),
                pltpu.VMEM((SPAN, SPAN), F32),
                pltpu.VMEM((SPAN, 128), F32),
                pltpu.VMEM((LOCAL_HEADS, SPAN), F32),
                pltpu.VMEM((SPAN, 128), F32),
                pltpu.VMEM((SPAN, 128), F32),
                pltpu.VMEM((STATE, WIDTH), BF),
                pltpu.VMEM((TILE, XBC), F32),
                pltpu.VMEM((TILE, 128), F32),
                pltpu.VMEM((8, XBC), F32),
                pltpu.VMEM((KERNEL + 1, 8, XBC), F32),
            ],
        ),
        out_shape=[
            jax.ShapeDtypeStruct((tokens, XCOLS + WIDTH), BF),
            jax.ShapeDtypeStruct((8, XCOLS), F32),
        ],
        input_output_aliases=aliases,
        compiler_params=params(),
        cost_estimate=pl.CostEstimate(
            flops=count * 10 * 10**9, bytes_accessed=count * 9 * 10**6, transcendentals=count * 4 * 10**6
        ),
        name="ssd_backward",
    )(jnp.stack(steps).astype(jnp.int32), proj, act, slope, dy, dz, states, conv_w, heads, skip, seg, spread, sofar, *more)


def gate_stats(order, y, z, dn, gain):
    steps = y.shape[0] // TILE
    block = pl.BlockSpec((TILE, WIDTH), lambda i, o: (i, 0))
    return pl.pallas_call(
        stats_kernel,
        grid_spec=pltpu.PrefetchScalarGridSpec(
            num_scalar_prefetch=1,
            grid=(steps,),
            in_specs=[block, block, block, whole((8, WIDTH))],
            out_specs=pl.BlockSpec((8, TILE), lambda i, o: (0, i)),
            scratch_shapes=[pltpu.VMEM((TILE, 128), F32)],
        ),
        out_shape=jax.ShapeDtypeStruct((8, y.shape[0]), F32),
        compiler_params=params(),
        cost_estimate=pl.CostEstimate(flops=3 * 10**9, bytes_accessed=16 * 10**6, transcendentals=3 * 10**6),
        name="gate_stats",
    )(order, y, z, dn, gain)


def gate_backward(order, st, y, z, dn, gain):
    steps = y.shape[0] // TILE
    block = pl.BlockSpec((TILE, WIDTH), lambda i, o: (i, 0))
    return pl.pallas_call(
        gate_kernel,
        grid_spec=pltpu.PrefetchScalarGridSpec(
            num_scalar_prefetch=1,
            grid=(steps,),
            in_specs=[pl.BlockSpec((8, TILE), lambda i, o: (0, i)), block, block, block, whole((8, WIDTH))],
            out_specs=[block, block, block],
            scratch_shapes=[pltpu.VMEM((TILE, 128), F32)],
        ),
        out_shape=[jax.ShapeDtypeStruct(y.shape, BF)] * 3,
        compiler_params=params(),
        cost_estimate=pl.CostEstimate(flops=6 * 10**9, bytes_accessed=32 * 10**6, transcendentals=3 * 10**6),
        name="gate_backward",
    )(order, st, y, z, dn, gain)


def norm_tokens(order, values, gain):
    rows = sum(v.shape[0] for v in values)
    return pl.pallas_call(
        functools.partial(norm_kernel, len(values)),
        grid_spec=pltpu.PrefetchScalarGridSpec(
            num_scalar_prefetch=1,
            grid=(1,),
            in_specs=[*(whole(v.shape) for v in values), whole((8, D))],
            out_specs=[whole((rows, D))],
        ),
        out_shape=[jax.ShapeDtypeStruct((rows, D), BF)],
        compiler_params=params(),
        cost_estimate=pl.CostEstimate(flops=rows * 10**6, bytes_accessed=rows * 8192, transcendentals=rows),
        name="norm_tokens",
    )(order, *values, gain)[0]


def pack_kernel(at_ref, in_ref, dt_ref, small_ref, send_ref, keep_ref, z_send_ref, z_keep_ref):
    rows = in_ref.shape[0]
    send_ref[:, rows:, :] = jnp.zeros((2, 8, XCOLS), BF)
    send_ref[0, rows:, :] = small_ref[...]
    source = lax.broadcasted_iota(jnp.int32, (HEADS, 128), 0)
    lane = lax.broadcasted_iota(jnp.int32, (HEADS, 128), 1)
    for x_ref, z_ref, x in ((send_ref, z_send_ref, 1 - at_ref[0]), (keep_ref, z_keep_ref, at_ref[0])):
        for core in range(2):
            slot = 2 * core + x
            for k in range(AHEADS):
                cols = slice(k * 128, k * 128 + 128)
                at = (k * SLOTS + slot) * 128
                z_ref[core, :, cols] = in_ref[:, pl.ds(pl.multiple_of(at, 128), 128)]
                x_ref[core, :rows, cols] = in_ref[:, pl.ds(pl.multiple_of(DI + at, 128), 128)]
            x_ref[core, :rows, WIDTH:XBC] = in_ref[:, 2 * DI :]
            wanted = jnp.where(lane < LOCAL_HEADS, (lane // 2) * 8 + slot * 2 + lane % 2, -1)
            x_ref[core, :rows, XBC:XCOLS] = nn(
                dt_ref[...], jnp.where(source == wanted, 1.0, 0.0).astype(BF)
            ).astype(BF)


def pack_weights(xi, in_w, dt_w, small):
    rows = in_w.shape[0]
    small = pad_rows(pad_cols(small[None], XCOLS))
    shapes = [(2, rows + 8, XCOLS), (2, rows, XCOLS), (2, rows, WIDTH), (2, rows, WIDTH)]
    return pl.pallas_call(
        pack_kernel,
        in_specs=[pl.BlockSpec(memory_space=pltpu.SMEM)] + [pl.BlockSpec(memory_space=pltpu.VMEM)] * 3,
        out_specs=[pl.BlockSpec(memory_space=pltpu.VMEM)] * 4,
        out_shape=[jax.ShapeDtypeStruct(shape, BF) for shape in shapes],
        cost_estimate=pl.CostEstimate(flops=10**8, bytes_accessed=3 * 10**6, transcendentals=0),
        name="pack_weights",
    )(xi[None].astype(jnp.int32), in_w, dt_w, small)


def pair_kernel(at_ref, keep_ref, got_ref, send_ref, stay_ref):
    rows = keep_ref.shape[1]
    mine = pl.ds(pl.multiple_of(at_ref[0] * rows, rows), rows)
    other = pl.ds(pl.multiple_of((1 - at_ref[0]) * rows, rows), rows)
    for out, core in ((send_ref, 1 - at_ref[1]), (stay_ref, at_ref[1])):
        out[mine, :] = keep_ref[core]
        out[other, :] = got_ref[core, :rows]


def pair_rows(xi, ci, keep, got):
    shape = (2 * keep.shape[1], keep.shape[2])
    return pl.pallas_call(
        pair_kernel,
        in_specs=[pl.BlockSpec(memory_space=pltpu.SMEM)] + [pl.BlockSpec(memory_space=pltpu.VMEM)] * 2,
        out_specs=[pl.BlockSpec(memory_space=pltpu.VMEM)] * 2,
        out_shape=[jax.ShapeDtypeStruct(shape, BF)] * 2,
        cost_estimate=pl.CostEstimate(flops=0, bytes_accessed=2 * 10**6, transcendentals=0),
        name="pair_rows",
    )(jnp.stack([xi, ci]).astype(jnp.int32), keep, got)


def place_kernel(at_ref, stay_ref, got_ref, out_ref):
    rows = stay_ref.shape[0]
    for index, ref in ((at_ref[0], stay_ref), (1 - at_ref[0], got_ref)):
        out_ref[pl.ds(pl.multiple_of(index * rows, rows), rows), :] = ref[...]


def place_rows(index, stay, got):
    return pl.pallas_call(
        place_kernel,
        in_specs=[pl.BlockSpec(memory_space=pltpu.SMEM)] + [pl.BlockSpec(memory_space=pltpu.VMEM)] * 2,
        out_specs=pl.BlockSpec(memory_space=pltpu.VMEM),
        out_shape=jax.ShapeDtypeStruct((2 * stay.shape[0], stay.shape[1]), BF),
        cost_estimate=pl.CostEstimate(flops=0, bytes_accessed=2 * 10**6, transcendentals=0),
        name="place_rows",
    )(index[None].astype(jnp.int32), stay, got)


def assemble_kernel(at_ref, pz_ref, gz_ref, px_ref, gx_ref, in_ref, dt_ref, out_ref, dt_out_ref, sum_ref):
    rows = in_ref.shape[0]
    total = jnp.zeros((rows, 128), F32)
    shared = [jnp.zeros((rows, 128), F32), jnp.zeros((rows, 128), F32)]
    dt_total = jnp.zeros((rows, HEADS), F32)
    lane = lax.broadcasted_iota(jnp.int32, (128, HEADS), 0)
    place = lax.broadcasted_iota(jnp.int32, (128, HEADS), 1)
    for core in range(2):
        for mine in (True, False):
            x = at_ref[0] if mine else 1 - at_ref[0]
            slot = 2 * core + x
            z_of = (lambda cols: pz_ref[core, x, :, cols]) if mine else (lambda cols: gz_ref[core, :, cols])
            x_of = (lambda cols: px_ref[core, x, :, cols]) if mine else (lambda cols: gx_ref[core, :, cols])
            for k in range(AHEADS):
                cols = slice(k * 128, k * 128 + 128)
                at = (k * SLOTS + slot) * 128
                for value, start in ((z_of(cols), at), (x_of(cols), DI + at)):
                    lanes = pl.ds(pl.multiple_of(start, 128), 128)
                    value = value.astype(F32)
                    out_ref[:, lanes] = value
                    total = total + value * in_ref[:, lanes].astype(F32)
            for k in range(2):
                shared[k] = shared[k] + x_of(slice(WIDTH + k * 128, WIDTH + k * 128 + 128)).astype(F32)
            wanted = jnp.where(lane < LOCAL_HEADS, (lane // 2) * 8 + slot * 2 + lane % 2, -1)
            dt_total = dt_total + nn(x_of(slice(XBC, XCOLS)), jnp.where(place == wanted, 1.0, 0.0).astype(BF))
    for k in range(2):
        cols = slice(2 * DI + k * 128, 2 * DI + k * 128 + 128)
        out_ref[:, cols] = shared[k]
        total = total + shared[k] * in_ref[:, cols].astype(F32)
    dt_out_ref[...] = dt_total
    rows_sum = jnp.sum(total, axis=1, keepdims=True) + jnp.sum(
        dt_total * dt_ref[...].astype(F32), axis=1, keepdims=True
    )
    sum_ref[...] = jnp.broadcast_to(rows_sum, (rows, 128))


def assemble_rows(xi, z_pair, z_got, x_pair, x_got, in_w, dt_w):
    rows = in_w.shape[0]
    return pl.pallas_call(
        assemble_kernel,
        in_specs=[pl.BlockSpec(memory_space=pltpu.SMEM)] + [pl.BlockSpec(memory_space=pltpu.VMEM)] * 6,
        out_specs=[pl.BlockSpec(memory_space=pltpu.VMEM)] * 3,
        out_shape=[
            jax.ShapeDtypeStruct(in_w.shape, F32),
            jax.ShapeDtypeStruct(dt_w.shape, F32),
            jax.ShapeDtypeStruct((rows, 128), F32),
        ],
        cost_estimate=pl.CostEstimate(flops=10**7, bytes_accessed=5 * 10**6, transcendentals=0),
        name="assemble_rows",
    )(xi[None].astype(jnp.int32), z_pair, z_got, x_pair, x_got, in_w, dt_w)


def small_kernel(at_ref, own_ref, x_ref, far_ref, taps_ref, heads_ref):
    xi, ci = at_ref[0], at_ref[1]
    terms = (
        (2 * ci + xi, own_ref), (2 * ci + 1 - xi, x_ref),
        (2 - 2 * ci + xi, far_ref.at[0]), (3 - 2 * ci - xi, far_ref.at[1]),
    )
    shared = jnp.zeros((8, 2 * STATE), F32)
    heads = jnp.zeros((8, HEADS), F32)
    source = lax.broadcasted_iota(jnp.int32, (128, HEADS), 0)
    place = lax.broadcasted_iota(jnp.int32, (128, HEADS), 1)
    row = lax.broadcasted_iota(jnp.int32, (8, 1), 0)
    exact = functools.partial(
        lax.dot_general,
        dimension_numbers=(((1,), (0,)), ((), ())),
        precision=lax.Precision.HIGHEST,
        preferred_element_type=F32,
    )
    for slot, ref in terms:
        for k in range(AHEADS):
            cols = ref[:, k * 128 : k * 128 + 128]
            taps_ref[:, pl.ds(pl.multiple_of((k * SLOTS + slot) * 128, 128), 128)] = cols
            wanted = jnp.where(place == k * 8 + slot * 2 + source // HEAD_DIM, 1.0, 0.0)
            heads = heads + exact(jnp.where(row == 5, cols, 0.0), wanted)
        shared = shared + ref[:, WIDTH:XBC]
        wanted = jnp.where(
            (source < LOCAL_HEADS) & (place == (source // 2) * 8 + slot * 2 + source % 2), 1.0, 0.0
        )
        heads = heads + exact(jnp.where(row < 2, ref[:, XBC:], 0.0), wanted)
    taps_ref[:, DI:] = shared
    heads_ref[...] = heads


def assemble_small(xi, ci, own, x, far):
    return pl.pallas_call(
        small_kernel,
        in_specs=[pl.BlockSpec(memory_space=pltpu.SMEM)] + [pl.BlockSpec(memory_space=pltpu.VMEM)] * 3,
        out_specs=[pl.BlockSpec(memory_space=pltpu.VMEM)] * 2,
        out_shape=[jax.ShapeDtypeStruct((8, DI + 2 * STATE), F32), jax.ShapeDtypeStruct((8, HEADS), F32)],
        cost_estimate=pl.CostEstimate(flops=10**7, bytes_accessed=10**6, transcendentals=0),
        name="assemble_small",
    )(jnp.stack([xi, ci]).astype(jnp.int32), own, x, far)


def rows_kernel(order_ref, *refs):
    rows = refs[0].shape[0]
    out_ref = refs[-1]
    for k, (ref, shift) in enumerate(zip(refs[:-1], (0, 0, 0, 0, 0, rows // 2, 0, 0, 0))):
        at = order_ref[k if k < 5 else k - 1] * rows + shift
        out_ref[pl.ds(pl.multiple_of(at, rows // 2), ref.shape[0]), :] = ref[...]


def ordered_rows(order, blocks):
    rows, cols = blocks[0].shape
    return pl.pallas_call(
        rows_kernel,
        in_specs=[pl.BlockSpec(memory_space=pltpu.SMEM)] + [pl.BlockSpec(memory_space=pltpu.VMEM)] * len(blocks),
        out_specs=pl.BlockSpec(memory_space=pltpu.VMEM),
        out_shape=jax.ShapeDtypeStruct((AHEADS * rows, cols), BF),
        compiler_params=params(),
        cost_estimate=pl.CostEstimate(flops=0, bytes_accessed=8 * 10**6, transcendentals=0),
        name="ordered_rows",
    )(order, *blocks)


def swap_x(v):
    return lax.ppermute(v, "x", SWAP)


def swap_core(v):
    return lax.ppermute(v, "core", SWAP)


def pick(v, index, axis=0):
    return lax.dynamic_index_in_dim(v, index, axis, keepdims=False)


def joined(index, mine, other, axis):
    return jnp.where(
        index == 0,
        jnp.concatenate([mine, other], axis=axis),
        jnp.concatenate([other, mine], axis=axis),
    )


def from_slots(v):
    slots, rows, cols = v.shape
    return (
        v.reshape(slots, rows, AHEADS, cols // AHEADS)
        .transpose(1, 2, 0, 3)
        .reshape(rows, slots * cols)
    )


class Return:
    def __init__(self, block):
        self.xi, self.ci = lax.axis_index("x"), lax.axis_index("core")
        self.rows = block.shape[0] // 4
        self.halves = block.astype(BF).reshape(2, 2 * self.rows, -1)
        self.flying = swap_core(pick(self.halves, 1 - self.ci))

    def turn(self, chain):
        got = chain.take(self.flying)
        pair = joined(self.ci, pick(self.halves, self.ci)[None], got[None], 0)
        self.pair = pair.reshape(2, 2, self.rows, -1)
        self.flying = swap_x(pick(self.pair, 1 - self.xi, 1))

    def land(self, chain):
        self.got = chain.take(self.flying)


class Chain:
    def __init__(self):
        self.last = ()

    def tie(self, value):
        return lax.optimization_barrier((value, self.last))[0]

    def mark(self, value):
        self.last = value
        return value

    def take(self, value):
        return self.mark(self.tie(value))


class Ring:
    def __init__(self):
        self.size = len(CYCLE)
        place = [CYCLE.index(i) for i in range(self.size)]
        position = jnp.asarray(place, jnp.int32)[lax.axis_index("ra")]
        cycle = jnp.asarray(CYCLE, jnp.int32)
        steps = jnp.arange(self.size, dtype=jnp.int32)
        self.order = cycle[(position + steps) % self.size]
        self.inverse = (jnp.asarray(place, jnp.int32) - position) % self.size

    def pairs(self, d):
        return [(CYCLE[i], CYCLE[(i + d) % self.size]) for i in range(self.size)]

    def right(self, v):
        return lax.ppermute(v, "ra", self.pairs(1))

    def left(self, v):
        return lax.ppermute(v, "ra", self.pairs(-1))


class Gather:
    def __init__(self, ring, block):
        self.ring = ring
        self.rights, self.lefts = [block], [block]

    def start(self):
        r, l = self.rights[-1], self.lefts[-1]
        if len(self.rights) == 4:
            half = r.shape[0] // 2
            r, l = r[:half], l[half:]
        self.flying = self.ring.right(r), self.ring.left(l)

    def land(self, chain):
        r, l = chain.take(self.flying)
        self.rights.append(r)
        self.lefts.append(l)

    def pieces(self):
        r, l = self.rights, self.lefts
        return [r[0], l[1], l[2], l[3], r[4], l[4], r[3], r[2], r[1]]


class Scatter:
    def __init__(self, ring, block, chain):
        self.ring, self.block, self.chain, self.count = ring, block, chain, 0

    def start(self):
        block, ring, k = self.block, self.ring, self.count
        self.count += 1
        if k == 0:
            far = block(4)
            half = far.shape[0] // 2
            sends = far[:half], far[half:]
        elif k == 1:
            up, down = block(3), block(5)
            half = up.shape[0] // 2
            r, l = self.right.astype(F32), self.left.astype(F32)
            sends = (
                jnp.concatenate([up[:half] + r, up[half:]], axis=0),
                jnp.concatenate([down[:half], down[half:] + l], axis=0),
            )
        else:
            sends = block(4 - k) + self.right.astype(F32), block(4 + k) + self.left.astype(F32)
        sends = self.chain.mark((sends[0].astype(BF), sends[1].astype(BF)))
        self.flying = ring.right(sends[0]), ring.left(sends[1])

    def land(self, chain):
        self.right, self.left = chain.take(self.flying)

    def total(self):
        return self.block(0) + self.right.astype(F32) + self.left.astype(F32)


def flat_index(sizes):
    index = 0
    for name, size in zip(ALL, sizes):
        index = index * size + lax.axis_index(name)
    return index


class SmallSum:
    def __init__(self, v):
        self.value = v
        self.bits = [1, 2, 4]

    def start(self):
        bit = self.bits.pop(0)
        self.flying = lax.ppermute(self.value, "ra", [(i, i ^ bit) for i in range(len(CYCLE))])

    def land(self, chain):
        self.value = chain.mark(self.value + chain.take(self.flying))


def permute_blocks(v, order, width):
    return jnp.concatenate(
        [
            lax.dynamic_slice(v, (0, order[k] * width), (v.shape[0], width))
            for k in range(v.shape[1] // width)
        ],
        axis=1,
    )


def pad_rows(v, rows=8):
    return jnp.concatenate([v, jnp.zeros((rows - v.shape[0], v.shape[1]), v.dtype)], axis=0)


def pad_cols(v, cols):
    return jnp.concatenate([v, jnp.zeros(v.shape[:-1] + (cols - v.shape[-1],), v.dtype)], axis=-1)


def per_device(
    sizes, tokens_short, tokens_long, cot_short, cot_long, seq_lengths,
    norm_gain, in_w, dt_w, conv_w, conv_b, dt_bias, a_log, d_skip, gate_gain, out_w,
):
    ringed = sizes == (8, 2, 1, 2)
    short, long = tokens_short.shape[0], tokens_long.shape[0]
    xi, ci = lax.axis_index("x"), lax.axis_index("core")
    slot = ci * 2 + xi
    feature = D // AHEADS
    mine_cols = lambda v: pick(v.reshape(v.shape[0], AHEADS, SLOTS, -1), slot, 2).reshape(v.shape[0], -1)
    chain = Chain()

    if ringed:
        ring = Ring()
        order, inverse = ring.order, ring.inverse
        from_ring = lambda v: permute_blocks(v, inverse, feature)
    else:
        order = jnp.arange(AHEADS, dtype=jnp.int32)
        from_ring = lambda v: v

    width = conv_w.shape[1]
    pieces = [conv_w.reshape(-1), conv_b, norm_gain, gate_gain]
    ends = np.cumsum([0] + [p.shape[0] for p in pieces])
    small = jnp.concatenate(pieces)
    group = ("core", "x")
    everyone = lambda v: lax.all_gather(v, group, axis=0, tiled=True)

    def stage(v, bit):
        count = int(np.prod(sizes))
        return lax.ppermute(v, ALL, [(i, i ^ bit) for i in range(count)])

    def widen(v, got, bit):
        return joined((flat_index(sizes) // bit) % 2, v, got, 0)

    if ringed:
        rows, n = in_w.shape[0], small.shape[0]
        x_send, x_keep, z_send, z_keep = chain.mark(pack_weights(xi, in_w, dt_w, small))
        x_got = chain.take(swap_x(x_send))
        small = widen(small[None], x_got[0, rows : rows + 1, :n], 1)
        passing = stage(small, 2)
        send, stay = chain.mark(pair_rows(xi, ci, x_keep, x_got))
        got = swap_core(send)
        small = widen(small, chain.take(passing), 2)
        passing = stage(small, 4)
        got = chain.take(got)
        small = widen(small, chain.take(passing), 4)
        passing = stage(small, 8)
        x_block = chain.mark(place_rows(ci, stay, got))
        small = widen(small, chain.take(passing), 8)
        small = widen(small, chain.take(stage(small, 16)), 16)
        gather_x = Gather(ring, chain.tie(x_block))
        gather_x.start()
        z_got = swap_x(chain.tie(z_send))
    else:
        small = lax.all_gather(small[None], ALL, axis=0, tiled=True)
    norm_full = pad_rows(small[:, ends[2] : ends[3]].reshape(1, -1).astype(F32))
    u_own = chain.mark(norm_tokens(order, [chain.tie(tokens_short), tokens_long], norm_full))
    xh = everyone(u_own)
    if ringed:
        gather_x.land(chain)
        gather_x.start()

    small, dt_bias, a_log, d_skip, cot_s, cot_l = chain.mark(
        chain.tie((small, dt_bias, a_log, d_skip, cot_short, cot_long))
    )
    live_s = (jnp.arange(short) < seq_lengths[0, 0]).astype(F32)[:, None]
    live_l = (jnp.arange(long) < seq_lengths[1, 0]).astype(F32)[:, None]
    dv_own = chain.mark(jnp.concatenate([(live_s * cot_s).astype(BF), (live_l * cot_l).astype(BF)], axis=0))
    taps = small[:, : ends[2]].reshape(-1, KERNEL + 1, width)
    taps = taps.transpose(1, 0, 2).reshape(KERNEL + 1, -1).astype(F32)
    taps = jnp.concatenate([mine_cols(taps[:, :DI]), taps[:, DI:]], axis=1)
    conv_taps, conv_bias = pad_rows(taps[:KERNEL]), pad_rows(taps[KERNEL:])
    gate_mine = pad_rows(mine_cols(small[:, ends[3] :].reshape(1, -1).astype(F32)))
    neg_rate = -jnp.exp(a_log.astype(F32))
    heads = pad_rows(pad_cols(mine_cols(jnp.stack([dt_bias.astype(F32), neg_rate])), 128))
    skip = pad_rows(jnp.repeat(mine_cols(d_skip.astype(F32)[None]), HEAD_DIM, axis=1))
    head_rows = np.arange(128)[:, None]
    seg = jnp.asarray(
        (head_rows < 2 * LOCAL_HEADS) & (head_rows % LOCAL_HEADS == np.arange(WIDTH)[None, :] // HEAD_DIM), BF
    )
    spread = jnp.asarray(
        (head_rows < 3 * LOCAL_HEADS)
        & (head_rows % LOCAL_HEADS == np.arange(128 * LOCAL_HEADS)[None, :] // 128),
        BF,
    )
    gate_mine, *seq_params = chain.mark((gate_mine, conv_taps, conv_bias, heads, skip, seg, spread))
    if ringed:
        send, stay = chain.mark(pair_rows(xi, ci, z_keep, chain.take(z_got)))
        z_block = chain.mark(place_rows(ci, stay, chain.take(swap_core(send))))
    slots = [jnp.int32(k) for k in range(SLOTS)]

    if ringed:
        gather_x.land(chain)
        gather_x.start()
        gather_x.land(chain)
        gather_x.start()
        gather_z = Gather(ring, z_block)
        gather_z.start()
        gather_z.land(chain)
        gather_x.land(chain)
        w_x = chain.mark(jnp.concatenate(gather_x.pieces(), axis=0))
        xh = chain.take(xh)
        dv = everyone(chain.tie(dv_own))
        gather_z.start()
        gather_o = Gather(ring, chain.tie(out_w))
        gather_o.start()
        both = gather_o, gather_z
        proj = chain.mark(nn(chain.tie(xh), w_x))
        for gather in both:
            gather.land(chain)
            gather.start()
        kept = chain.mark(ssd_forward(slots[:2], chain.tie(proj), *seq_params))
        for gather in both:
            gather.land(chain)
            gather.start()
        y, act, slope, states = chain.mark(ssd_forward(slots[2:], chain.tie(proj), *seq_params, earlier=kept))
        for gather in both:
            gather.land(chain)
        gather_o.start()
        w_all = chain.mark(jnp.concatenate([w_x, jnp.concatenate(gather_z.pieces(), axis=0)], axis=1))
        z = chain.mark(nn(chain.tie(xh), w_all[:, XCOLS:]).astype(BF))
        gather_o.land(chain)
        w_o = chain.mark(ordered_rows(order, chain.tie(gather_o.pieces())))
        dv = chain.take(dv)
        dn = chain.mark(nt(dv, w_o).astype(BF))
    else:
        full = lax.all_gather(in_w, ALL, axis=0, tiled=True)
        full_dt = lax.all_gather(dt_w, ALL, axis=0, tiled=True)
        full_out = lax.all_gather(out_w, ALL, axis=0, tiled=True)
        w_z = mine_cols(full[:, :DI])
        w_x = jnp.concatenate(
            [mine_cols(full[:, DI : 2 * DI]), full[:, 2 * DI :], pad_cols(mine_cols(full_dt), 128)], axis=-1
        )
        w_o = pick(full_out.reshape(AHEADS, SLOTS, 128, D), slot, 1).reshape(WIDTH, D)
        dv = everyone(dv_own)
        proj = nn(xh, w_x)
        y, act, slope, states = ssd_forward(slots, proj, *seq_params)
        dn = nt(dv, w_o).astype(BF)
        z = nn(xh, w_z).astype(BF)
        w_all = jnp.concatenate([w_x, w_z], axis=1)

    straight = jnp.arange(AHEADS, dtype=jnp.int32)
    st = chain.mark(gate_stats(straight, y, chain.tie(z), dn, gate_mine))
    st = st + swap_core(st)
    st = st + swap_x(st)
    n, dy, dz = chain.mark(gate_backward(straight, st, y, z, dn, gate_mine))

    own = short + long
    rows_of = lambda v, start, count: lax.dynamic_slice(v, (start * own, 0), (count * own, v.shape[1]))

    def unit_product(dx, start, count):
        dx = chain.tie(dx)
        return nt(rows_of(dx, start, count), w_all)

    def backward_call(steps, sofar, earlier):
        return chain.mark(
            ssd_backward(steps, chain.tie(proj), act, slope, dy, dz, states, *seq_params, sofar, earlier=earlier)
        )

    none_yet = jnp.zeros((8, XCOLS), F32)

    far, mid = 2 * (1 - ci), 2 * ci + 1 - xi
    g_out = chain.mark(tn(n, dv).astype(BF))
    reduced = lambda v, axes: lax.psum_scatter(v, axes, scatter_dimension=0, tiled=True)
    if ringed:
        own_out = reduced(g_out, "ra").astype(F32)
        g_z = chain.mark(tn(chain.tie(xh), dz))
        blocks_z = g_z.reshape(AHEADS, -1, WIDTH)
        scatter_z = Scatter(ring, lambda k: blocks_z[k], chain)
        scatter_z.start()
    else:
        g_z = tn(xh, dz)
    branch = chain.mark(nn(chain.tie(n), w_o).astype(BF))
    branch = reduced(branch, group)
    if ringed:
        scatter_z.land(chain)
        scatter_z.start()
        dx, acc = backward_call([far, far + 1], none_yet, ())
        scatter_z.land(chain)
        scatter_z.start()
        far_u = swap_core(chain.mark(unit_product(dx, far, 2).astype(BF)))
        dx, acc = backward_call([mid], acc, (chain.tie(dx),))
        scatter_z.land(chain)
        scatter_z.start()
        far_u = chain.take(far_u)
        mid_u = chain.mark(
            (unit_product(dx, mid, 1) + rows_of(far_u, 1 - xi, 1).astype(F32)).astype(BF)
        )
        mid_u = swap_x(mid_u)
        dx, acc = backward_call([slot], acc, (chain.tie(dx),))
        scatter_z.land(chain)
        back_z = Return(chain.mark(scatter_z.total()))

        def blocks_x(first, last):
            part = tn(xh[:, first * feature : last * feature], chain.tie(dx)[:, :XCOLS])
            return dict(enumerate(chain.mark(part).reshape(last - first, feature, XCOLS), first))

        made = blocks_x(4, 5)
        scatter_x = Scatter(ring, lambda k: made[k], chain)
        scatter_x.start()
        tally = SmallSum(chain.tie(acc))
        tally.start()
        made.update(blocks_x(3, 4))
        made.update(blocks_x(5, 6))
        scatter_x.land(chain)
        tally.land(chain)
        scatter_x.start()
        tally.start()
        made.update(blocks_x(0, 3))
        made.update(blocks_x(6, 8))
        scatter_x.land(chain)
        tally.land(chain)
        scatter_x.start()
        tally.start()
        back_z.turn(chain)
        du_own = unit_product(dx, slot, 1) + rows_of(far_u, xi, 1).astype(F32)
        du_own = chain.mark(lax.optimization_barrier(du_own))
        scatter_x.land(chain)
        tally.land(chain)
        scatter_x.start()
        mid_u = chain.take(mid_u)
        du = chain.mark(du_own + mid_u.astype(F32))
        scatter_x.land(chain)
        back_x = Return(chain.mark(scatter_x.total()))
        acc = tally.value
        acc_x = swap_x(acc)
        back_z.land(chain)
        back_x.turn(chain)
        acc_x = chain.take(acc_x)
        acc_far = chain.take(swap_core(jnp.stack([acc, acc_x])))
        taps_total, head_total = chain.mark(assemble_small(xi, ci, acc, acc_x, acc_far))
        own_conv = lax.dynamic_slice(taps_total, (0, flat_index(sizes) * width), (KERNEL + 1, width))
    else:
        dx, acc = backward_call(slots, none_yet, ())
        du = reduced(nt(dx, w_all), group)
        g_x = tn(xh, dx[:, :XCOLS])
        acc = lax.psum(acc, ("ra", "rb"))
        acc_x = swap_x(acc)
        acc_far = swap_core(jnp.stack([acc, acc_x]))
        taps_total, head_total = assemble_small(xi, ci, acc, acc_x, acc_far)
        own_conv = lax.dynamic_slice(taps_total, (0, flat_index(sizes) * width), (KERNEL + 1, width))
    v_s, v_l = branch[:short].astype(F32), branch[short:].astype(F32)
    du_s, du_l = du[:short], du[short:]

    out_short = (tokens_short.astype(F32) + live_s * v_s).astype(BF)
    out_long = (tokens_long.astype(F32) + live_l * v_l).astype(BF)

    def token_grad(token, cot, d_u):
        residual = token.astype(F32)
        row_scale = lax.rsqrt(jnp.mean(residual * residual, axis=-1, keepdims=True) + EPS)
        unit = residual * row_scale
        d_norm = from_ring(d_u) * norm_full[0:1]
        return cot.astype(F32) + row_scale * (d_norm - unit * jnp.mean(d_norm * unit, axis=-1, keepdims=True))

    grad_short, grad_long = chain.mark(
        (token_grad(tokens_short, cot_short, du_s), token_grad(tokens_long, cot_long, du_l))
    )

    if ringed:
        back_x.land(chain)
        grad_in_w, grad_dt_w, norm_sum = chain.mark(
            assemble_rows(xi, back_z.pair, back_z.got, back_x.pair, back_x.got, in_w, dt_w)
        )
        norm_sum = norm_sum[:, 0]
    else:
        here = (jnp.arange(SLOTS) == slot).astype(F32)
        wider = lambda v: (v.reshape(D, AHEADS, 1, -1) * here[:, None]).reshape(D, -1)
        reduce = lambda v: lax.psum_scatter(v, ALL, scatter_dimension=0, tiled=True)
        grad_in_w = reduce(
            jnp.concatenate([wider(g_z), wider(g_x[:, :WIDTH]), g_x[:, WIDTH:XBC]], axis=1)
        )
        grad_dt_w = reduce(wider(g_x[:, XBC : XBC + LOCAL_HEADS]))
        own_out = reduce(
            (g_out.astype(F32).reshape(AHEADS, 1, 128, D) * here[:, None, None]).reshape(DI, D)
        )

        norm_sum = jnp.sum(in_w.astype(F32) * grad_in_w, axis=1) + jnp.sum(dt_w.astype(F32) * grad_dt_w, axis=1)

    grad_norm_gain = norm_sum / norm_gain.astype(F32)
    grad_gate_gain = jnp.sum(out_w.astype(F32) * own_out, axis=1) / gate_gain.astype(F32)

    return (
        out_short,
        out_long,
        grad_short,
        grad_long,
        grad_norm_gain,
        grad_in_w,
        grad_dt_w,
        own_conv[:KERNEL],
        own_conv[KERNEL],
        head_total[0],
        head_total[1] * neg_rate,
        head_total[5],
        grad_gate_gain,
        own_out,
    )


def solution(mesh):
    wide, narrow = mesh.shape["wide"], mesh.shape["narrow"]
    sizes = (wide // 2, 2, narrow // 2, 2)
    split = Mesh(mesh.devices.reshape(sizes), ALL)
    rows, vector, columns = P(ALL, None), P(ALL), P(None, ALL)
    return jax.shard_map(
        functools.partial(per_device, sizes),
        mesh=split,
        in_specs=(
            rows, rows, rows, rows, columns, vector, rows, rows, columns, vector, P(), P(), P(), vector, rows,
        ),
        out_specs=(
            rows, rows, rows, rows, vector, rows, rows, columns, vector, P(), P(), P(), vector, rows,
        ),
        check_vma=False,
    )
```

```python
import functools

import jax
import jax.numpy as jnp
import numpy as np
from jax import lax
from jax.experimental import pallas as pl
from jax.experimental.pallas import tpu as pltpu
from jax.sharding import Mesh
from jax.sharding import PartitionSpec as P

D = 2048
DI = 4096
HEADS = 64
HEAD_DIM = 64
STATE = 128
KERNEL = 4
SPAN = 256
EPS = 1e-05
BF = jnp.bfloat16
F32 = jnp.float32

SLOTS = 4
AHEADS = 8
WIDTH = DI // SLOTS
LOCAL_HEADS = HEADS // SLOTS
XBC = WIDTH + 2 * STATE
XCOLS = XBC + 128
ALL = ("ra", "core", "rb", "x")
NEG = -1e30
TILE = 640
HEAD = 128

SWAP = [(0, 1), (1, 0)]
CYCLE = (0, 2, 4, 6, 7, 5, 3, 1)


def nt(a, b):
    return lax.dot_general(a, b, (((1,), (1,)), ((), ())), preferred_element_type=F32)


def nn(a, b):
    return lax.dot_general(a, b, (((1,), (0,)), ((), ())), preferred_element_type=F32)


def tn(a, b):
    return lax.dot_general(a, b, (((0,), (0,)), ((), ())), preferred_element_type=F32)


LOG2E = 1.4426950408889634
ROWS = 64


def sigmoid(v):
    return 0.5 * jnp.tanh(0.5 * v) + 0.5


def lane_index():
    return lax.broadcasted_iota(jnp.int32, (1, 128), 1)


def three_parts(values):
    values = jnp.where(lane_index() < LOCAL_HEADS, values, 0.0)
    high = values.astype(BF).astype(F32)
    rest = values - high
    mid = rest.astype(BF).astype(F32)
    low = rest - mid
    return (high + pltpu.roll(mid, LOCAL_HEADS, 1) + pltpu.roll(low, 2 * LOCAL_HEADS, 1)).astype(BF)


def add_parts(values):
    return values + pltpu.roll(values, 128 - LOCAL_HEADS, 1) + pltpu.roll(values, 128 - 2 * LOCAL_HEADS, 1)


def triangle(n, lower):
    i = lax.broadcasted_iota(jnp.int32, (n, n), 0)
    j = lax.broadcasted_iota(jnp.int32, (n, n), 1)
    return jnp.where(i >= j if lower else i <= j, 1.0, 0.0).astype(BF)


def running_sum(values, lower):
    return add_parts(nn(triangle(values.shape[0], lower), three_parts(values)))


def two_parts(values):
    values = jnp.where(lane_index() < LOCAL_HEADS, values, 0.0)
    high = values.astype(BF).astype(F32)
    return (high + pltpu.roll(values - high, LOCAL_HEADS, 1)).astype(BF)


def softplus(v):
    return jnp.maximum(v, 0.0) + jnp.log1p(jnp.exp(-jnp.abs(v)))


def conv_tile(p_ref, cw_ref, cb_ref, r0, cols):
    starts = (r0 == 0) | (r0 == HEAD)
    before = p_ref[pl.ds(pl.multiple_of(jnp.maximum(r0 - 8, 0), 8), 8), cols]
    before = jnp.where(starts, 0.0, before)
    here = p_ref[pl.ds(r0, ROWS), cols]
    both = jnp.concatenate([before, here], axis=0)
    back = [here] + [pltpu.roll(both, m, 0)[8:] for m in (1, 2, 3)]
    total = cb_ref[0:1, cols]
    for m in range(KERNEL):
        total = total + cw_ref[3 - m : 4 - m, cols] * back[m]
    return total, back


def fwd_kernel(
    steps_ref, p_ref, cw_ref, cb_ref, hp_ref, dsk_ref, seg_ref, bc_ref, *refs
):
    y_ref, act_ref, slope_ref, h_ref, dt_s, parts_s, grow_s, rt_s, g_s = refs[-9:]
    lane = lane_index()

    def conv_step(i, carry):
        r0 = pl.multiple_of(i * ROWS, ROWS)
        rows = pl.ds(r0, ROWS)
        for c in range(XBC // 128):
            cols = slice(c * 128, c * 128 + 128)
            conv, _ = conv_tile(p_ref, cw_ref, cb_ref, r0, cols)
            gate = sigmoid(conv)
            act = conv * gate
            act_ref[rows, cols] = act.astype(BF)
            slope_ref[rows, cols] = (gate + act * (1.0 - gate)).astype(BF)
        dt_s[rows, :] = softplus(p_ref[rows, XBC:] + hp_ref[0:1])
        return carry

    lax.fori_loop(0, TILE // ROWS, conv_step, 0, unroll=2)
    rate = hp_ref[1:2]

    def block(off, q, read_state, make_state):
        rows = pl.ds(off, q)
        dt = dt_s[rows, :]
        cum2 = running_sum(dt * rate, True) * LOG2E
        parts_s[:q, :] = three_parts(cum2)
        turned = (cum2 - jnp.log2(dt)).T
        for h in range(LOCAL_HEADS):
            rt_s[h, :, :q] = turned[h : h + 1]
        b = act_ref[rows, WIDTH : WIDTH + STATE]
        c = act_ref[rows, WIDTH + STATE :]
        g_s[:q, :q] = nt(c, b)
        if read_state:
            grow_s[:q, :] = two_parts(jnp.exp2(cum2))
        if make_state:
            grow_s[:q, :] = two_parts(jnp.exp2(cum2[q - 1 : q] - cum2) * dt)
            b_turned = b.astype(F32).T.astype(BF)
        diagonal = lax.broadcasted_iota(jnp.int32, (128, 128), 0) >= lax.broadcasted_iota(
            jnp.int32, (128, 128), 1
        )

        def pair(p, carry):
            lanes = pl.ds(pl.multiple_of(p * 128, 128), 128)
            x2 = act_ref[rows, lanes]
            zero = jnp.zeros_like(x2)
            x_heads = [jnp.where(lane < HEAD_DIM, x2, zero), jnp.where(lane < HEAD_DIM, zero, x2)]
            cols = nn(parts_s[:q, :], bc_ref[:, pl.ds(pl.multiple_of(p * 256, 256), 256)])
            if read_state:
                carried = nn(grow_s[:q, :], seg_ref[:, lanes]) * nn(c, h_ref[0, :, lanes].astype(BF))
            for rt in range(q // 128):
                top = rt * 128
                mixes = []
                for j in range(2):
                    col = cols[top : top + 128, j * 128 : j * 128 + 128]
                    for ct in range(rt + 1):
                        lo = ct * 128
                        spread = col - rt_s[p * 2 + j, :, lo : lo + 128]
                        if ct == rt:
                            spread = jnp.where(diagonal, spread, NEG)
                        mixes.append((g_s[top : top + 128, lo : lo + 128] * jnp.exp2(spread)).astype(BF))
                x_both = jnp.concatenate([x[: top + 128] for x in x_heads], axis=0)
                out = nn(jnp.concatenate(mixes, axis=1), x_both)
                out = out + dsk_ref[0:1, lanes] * x2[top : top + 128].astype(F32)
                if read_state:
                    out = out + carried[top : top + 128]
                y_ref[pl.ds(off + top, 128), lanes] = out.astype(y_ref.dtype)
            if make_state:
                wide = nn(grow_s[:q, :], seg_ref[:, lanes])
                h_ref[0, :, lanes] = nn(b_turned, (wide * x2.astype(F32)).astype(BF))
            return carry

        lax.fori_loop(0, LOCAL_HEADS // 2, pair, 0, unroll=True)

    block(0, HEAD, False, False)
    block(HEAD, SPAN, False, True)
    block(HEAD + SPAN, SPAN, True, False)


def bwd_kernel(
    steps_ref, p_ref, act_ref, slope_ref, dy_ref, dz_ref, h_ref, cw_ref, hp_ref, dsk_ref, seg_ref, bc_ref, sofar_ref, *refs
):
    dp_ref, acc_ref = refs[-17:-15]
    heads_at = slice(XBC, XCOLS)
    dt_s, parts_s, grow_s, ct_s, gt_s, dgt_s, kc_s, kr_s, fold_s, dbc_s, ds_s, da_s, dst_s, after_s, sums_s = refs[-15:]
    lane = lane_index()
    head_row = lax.broadcasted_iota(jnp.int32, (LOCAL_HEADS, 1), 0)

    @pl.when(pl.program_id(0) == 0)
    def _():
        acc_ref[...] = sofar_ref[...]

    rate = hp_ref[1:2]
    dt_s[...] = softplus(p_ref[:, XBC:] + hp_ref[0:1])

    def block(off, q, state_in, state_out):
        rows = pl.ds(off, q)
        dt = dt_s[rows, :]
        cum2 = running_sum(dt * rate, True) * LOG2E
        parts_s[:q, :] = three_parts(cum2 - jnp.log2(dt))
        turned = cum2.T
        for h in range(LOCAL_HEADS):
            ct_s[h, :, :q] = turned[h : h + 1]
        b = act_ref[rows, WIDTH : WIDTH + STATE]
        c = act_ref[rows, WIDTH + STATE :]
        gt_s[:q, :q] = nt(b, c)
        dgt_s[:q, :q] = jnp.zeros((q, q), F32)
        kc_s[:q, :] = jnp.zeros((q, 128), F32)
        kr_s[:, :q] = jnp.zeros((LOCAL_HEADS, q), F32)
        if state_in:
            grow_s[:q, :] = two_parts(jnp.exp2(cum2))
            c_turned = c.astype(F32).T.astype(BF)
        if state_out:
            decay = jnp.exp2(cum2[q - 1 : q] - cum2)
            grow_s[:q, :] = two_parts(decay * dt)
        diagonal = lax.broadcasted_iota(jnp.int32, (128, 128), 1) >= lax.broadcasted_iota(
            jnp.int32, (128, 128), 0
        )
        tiles = q // 128

        def pair(p, carry):
            lanes = pl.ds(pl.multiple_of(p * 128, 128), 128)
            x2 = act_ref[rows, lanes]
            dy2 = dy_ref[rows, lanes]
            zero = jnp.zeros_like(dy2)
            dy_heads = [jnp.where(lane < HEAD_DIM, dy2, zero), jnp.where(lane < HEAD_DIM, zero, dy2)]
            cols = nn(parts_s[:q, :], bc_ref[:, pl.ds(pl.multiple_of(p * 256, 256), 256)])
            if state_in:
                hb = h_ref[0, :, lanes].astype(BF)
                dyc = dy2.astype(F32) * nn(grow_s[:q, :], seg_ref[:, lanes])
                dyb = dyc.astype(BF)
                fold_s[:q, lanes] = (dyc * nn(c, hb)).astype(BF)
                dbc_s[:q, lanes] = dyb
                ds_s[:, lanes] = nn(c_turned, dyb).astype(BF)
            if state_out:
                sb = ds_s[:, lanes]
                wide = nn(grow_s[:q, :], seg_ref[:, lanes])
                bd = nn(b, sb)
                xf = x2.astype(F32)
                fold_s[:q, lanes] = (xf * bd).astype(BF)
                dbc_s[:q, lanes] = (wide * xf).astype(BF)
                late = wide * bd
            picks = [jnp.where(lane == p * 2 + j, 1.0, 0.0).astype(BF) for j in range(2)]
            marks = [jnp.where(head_row == p * 2 + j, 1.0, 0.0).astype(BF) for j in range(2)]
            for jt in range(tiles):
                lo = jt * 128
                span = q - lo
                xj = x2[lo : lo + 128]
                mixes = []
                terms = []
                dgs = [None] * tiles
                for j in range(2):
                    col = cols[lo : lo + 128, j * 128 : j * 128 + 128]
                    for it in range(jt, tiles):
                        at = it * 128
                        spread = ct_s[p * 2 + j, :, at : at + 128] - col
                        if it == jt:
                            spread = jnp.where(diagonal, spread, NEG)
                        e = jnp.exp2(spread)
                        score = gt_s[lo : lo + 128, at : at + 128]
                        dme = nt(xj, dy_heads[j][at : at + 128]) * e
                        dgs[it] = dme if dgs[it] is None else dgs[it] + dme
                        terms.append((dme * score).astype(BF))
                        mixes.append((score * e).astype(BF))
                for it in range(jt, tiles):
                    dgt_s[lo : lo + 128, it * 128 : it * 128 + 128] += dgs[it]
                half = len(terms) // 2
                kc_s[lo : lo + 128, :] += nn(
                    jnp.concatenate(terms, axis=1),
                    jnp.concatenate([jnp.broadcast_to(v, (span, 128)) for v in picks], axis=0),
                )
                kr_s[:, lo:q] += nn(
                    jnp.concatenate([jnp.broadcast_to(v, (LOCAL_HEADS, 128)) for v in marks], axis=1),
                    jnp.concatenate(
                        [jnp.concatenate(terms[:half], axis=1), jnp.concatenate(terms[half:], axis=1)], axis=0
                    ),
                )
                dy_both = jnp.concatenate([d[lo:] for d in dy_heads], axis=0)
                out = nn(jnp.concatenate(mixes, axis=1), dy_both)
                dyj = dy2[lo : lo + 128].astype(F32)
                acc_ref[5:6, lanes] += jnp.sum(dyj * xj.astype(F32), axis=0, keepdims=True)
                out = out + dsk_ref[0:1, lanes] * dyj
                if state_out:
                    out = out + late[lo : lo + 128]
                da_s[pl.ds(off + lo, 128), lanes] = out
            return carry

        lax.fori_loop(0, LOCAL_HEADS // 2, pair, 0, unroll=True)

        dgt = dgt_s[:q, :q].astype(BF)
        db = nn(dgt, c)
        dc = tn(dgt, b)
        kcol = kc_s[:q, :]
        row_terms = jnp.concatenate([kr_s[:, :q], jnp.zeros((128 - LOCAL_HEADS, q), F32)], axis=0)
        d_cum = row_terms.T - kcol
        inverse = jnp.where(dt > 1e-30, 1.0 / jnp.maximum(dt, 1e-30), 0.0)
        d_dt = kcol * inverse
        if state_in:
            d_cum = d_cum + nt(fold_s[:q, :], seg_ref[...])
            dc = dc + nt(dbc_s[:q, :], h_ref[0].astype(BF))
        if state_out:
            db = db + nt(dbc_s[:q, :], ds_s[...])
            d_weights = nt(fold_s[:q, :], seg_ref[...])
            d_dt = d_dt + d_weights * decay
            w_term = d_weights * decay * dt
            last = lax.broadcasted_iota(jnp.int32, (q, 1), 0) == q - 1
            d_cum = d_cum - w_term + jnp.where(last, jnp.sum(w_term, axis=0, keepdims=True), 0.0)
        da_s[rows, WIDTH : WIDTH + STATE] = db
        da_s[rows, WIDTH + STATE :] = dc
        d_rate = running_sum(d_cum, False)
        dst_s[rows, :] = d_dt + d_rate * rate
        acc_ref[1:2, heads_at] += jnp.sum(d_rate * dt, axis=0, keepdims=True)

    block(0, HEAD, False, False)
    block(HEAD + SPAN, SPAN, True, False)
    block(HEAD, SPAN, False, True)

    d_soft = dst_s[...] * jax.nn.sigmoid(p_ref[:, XBC:] + hp_ref[0:1])
    d_soft = jnp.where(lane < LOCAL_HEADS, d_soft, 0.0)
    acc_ref[0:1, heads_at] += jnp.sum(d_soft, axis=0, keepdims=True)
    dp_ref[:, XBC:XCOLS] = d_soft.astype(BF)
    dp_ref[:, XCOLS:] = dz_ref[...]
    sums_s[...] = jnp.zeros_like(sums_s)
    after_s[...] = jnp.zeros_like(after_s)

    def conv_step(i, carry):
        r0 = pl.multiple_of(TILE - ROWS - i * ROWS, ROWS)
        rows = pl.ds(r0, ROWS)
        ends = (r0 + ROWS == HEAD) | (r0 + ROWS == TILE)
        fold = lambda v: jnp.sum(v.reshape(ROWS // 8, 8, 128), axis=0)
        for c in range(XBC // 128):
            cols = slice(c * 128, c * 128 + 128)
            here = p_ref[rows, cols]
            d_conv = da_s[rows, cols] * slope_ref[rows, cols].astype(F32)
            both = jnp.concatenate([d_conv, jnp.where(ends, 0.0, after_s[:, cols])], axis=0)
            after_s[:, cols] = d_conv[:8]
            total = cw_ref[3:4, cols] * d_conv
            sums_s[3, :, cols] += fold(d_conv * here)
            sums_s[4, :, cols] += fold(d_conv)
            for m in (1, 2, 3):
                ahead = pltpu.roll(both, ROWS + 8 - m, 0)[:ROWS]
                total = total + cw_ref[3 - m : 4 - m, cols] * ahead
                sums_s[3 - m, :, cols] += fold(ahead * here)
            dp_ref[rows, cols] = total.astype(BF)
        return carry

    lax.fori_loop(0, TILE // ROWS, conv_step, 0, unroll=2)
    for k in range(KERNEL + 1):
        acc_ref[k : k + 1, :XBC] += jnp.sum(sums_s[k], axis=0, keepdims=True)


def stats_kernel(order_ref, y_ref, z_ref, dn_ref, gain_ref, st_ref, both_s):
    lane = lane_index()

    def step(i, carry):
        rows = pl.ds(pl.multiple_of(i * ROWS, ROWS), ROWS)
        p1 = jnp.zeros((ROWS, 128), F32)
        p2 = jnp.zeros((ROWS, 128), F32)
        for k in range(AHEADS):
            lanes = pl.ds(pl.multiple_of(order_ref[k] * 128, 128), 128)
            z = z_ref[rows, lanes].astype(F32)
            g = y_ref[rows, lanes].astype(F32) * (z * sigmoid(z))
            p1 = p1 + g * g
            p2 = p2 + g * (dn_ref[rows, k * 128 : k * 128 + 128].astype(F32) * gain_ref[0:1, lanes])
        both_s[rows, :] = jnp.where(
            lane == 0,
            jnp.sum(p1, axis=1, keepdims=True),
            jnp.where(lane == 1, jnp.sum(p2, axis=1, keepdims=True), 0.0),
        )
        return carry

    lax.fori_loop(0, y_ref.shape[0] // ROWS, step, 0, unroll=2)
    st_ref[...] = both_s[...].T[0:8]


def gate_kernel(order_ref, st_ref, y_ref, z_ref, dn_ref, gain_ref, n_ref, dy_ref, dz_ref, st_s):
    st_s[...] = jnp.concatenate([st_ref[...], jnp.zeros((120, y_ref.shape[0]), F32)], axis=0).T

    def step(i, carry):
        rows = pl.ds(pl.multiple_of(i * ROWS, ROWS), ROWS)
        st = st_s[rows, :]
        rg = lax.rsqrt(st[:, 0:1] * (1.0 / DI) + EPS)
        mean = rg * rg * st[:, 1:2] * (1.0 / DI)
        for k in range(AHEADS):
            lanes = pl.ds(pl.multiple_of(order_ref[k] * 128, 128), 128)
            fixed = slice(k * 128, k * 128 + 128)
            gain = gain_ref[0:1, lanes]
            z = z_ref[rows, lanes].astype(F32)
            y = y_ref[rows, lanes].astype(F32)
            sg = sigmoid(z)
            silu = z * sg
            ghat = y * silu * rg
            dg = rg * (dn_ref[rows, fixed].astype(F32) * gain) - ghat * mean
            n_ref[rows, fixed] = (ghat * gain).astype(BF)
            dy_ref[rows, lanes] = (dg * silu).astype(BF)
            dz_ref[rows, lanes] = (dg * y * (sg + silu * (1.0 - sg))).astype(BF)
        return carry

    lax.fori_loop(0, y_ref.shape[0] // ROWS, step, 0, unroll=2)


def norm_kernel(pieces, order_ref, *refs):
    gain_ref, u_ref = refs[pieces], refs[-1]
    at = 0
    for x_ref in refs[:pieces]:
        count = x_ref.shape[0] // ROWS

        def step(i, carry, x_ref=x_ref, at=at):
            rows = pl.ds(pl.multiple_of(i * ROWS, ROWS), ROWS)
            out = pl.ds(pl.multiple_of(at + i * ROWS, ROWS), ROWS)
            total = jnp.zeros((ROWS, 128), F32)
            for k in range(D // 128):
                v = x_ref[rows, k * 128 : k * 128 + 128].astype(F32)
                total = total + v * v
            scale = lax.rsqrt(jnp.sum(total, axis=1, keepdims=True) * (1.0 / D) + EPS)
            for k in range(AHEADS):
                lanes = pl.ds(pl.multiple_of(order_ref[k] * 256, 256), 256)
                u_ref[out, k * 256 : k * 256 + 256] = (
                    x_ref[rows, lanes].astype(F32) * scale * gain_ref[0:1, lanes]
                ).astype(BF)
            return carry

        lax.fori_loop(0, count, step, 0)
        at += x_ref.shape[0]


def whole(shape):
    return pl.BlockSpec(shape, lambda i, s: (0,) * len(shape))


def placed(cols):
    return pl.BlockSpec((TILE, cols), lambda i, s: (s[i], 0))


def params():
    return pltpu.CompilerParams(vmem_limit_bytes=56 * 1024 * 1024)


def onto(earlier, first_input):
    specs = [pl.BlockSpec(memory_space=pl.ANY)] * len(earlier)
    return list(earlier), specs, {first_input + i: i for i in range(len(earlier))}


STATES = pl.BlockSpec((1, STATE, WIDTH), lambda i, s: (s[i], 0, 0))


def ssd_forward(steps, proj, conv_w, conv_b, heads, skip, seg, spread, earlier=()):
    tokens = proj.shape[0]
    count = len(steps)
    more, more_specs, aliases = onto(earlier, 8)
    return pl.pallas_call(
        fwd_kernel,
        grid_spec=pltpu.PrefetchScalarGridSpec(
            num_scalar_prefetch=1,
            grid=(count,),
            in_specs=[
                placed(XCOLS), whole((8, XBC)), whole((8, XBC)), whole((8, 128)), whole((8, WIDTH)),
                whole((128, WIDTH)), whole((128, 128 * LOCAL_HEADS)), *more_specs,
            ],
            out_specs=[placed(WIDTH), placed(XBC), placed(XBC), STATES],
            scratch_shapes=[
                pltpu.VMEM((TILE, 128), F32),
                pltpu.VMEM((SPAN, 128), BF),
                pltpu.VMEM((SPAN, 128), BF),
                pltpu.VMEM((LOCAL_HEADS, 1, SPAN), F32),
                pltpu.VMEM((SPAN, SPAN), F32),
            ],
        ),
        out_shape=[
            jax.ShapeDtypeStruct((tokens, WIDTH), BF),
            jax.ShapeDtypeStruct((tokens, XBC), BF),
            jax.ShapeDtypeStruct((tokens, XBC), BF),
            jax.ShapeDtypeStruct((tokens // TILE, STATE, WIDTH), F32),
        ],
        input_output_aliases=aliases,
        compiler_params=params(),
        cost_estimate=pl.CostEstimate(
            flops=count * 4 * 10**9, bytes_accessed=count * 6 * 10**6, transcendentals=count * 2 * 10**6
        ),
        name="ssd_forward",
    )(jnp.stack(steps).astype(jnp.int32), proj, conv_w, conv_b, heads, skip, seg, spread, *more)


def ssd_backward(steps, proj, act, slope, dy, dz, states, conv_w, conv_b, heads, skip, seg, spread, sofar, earlier=()):
    tokens = proj.shape[0]
    count = len(steps)
    more, more_specs, aliases = onto(earlier, 13)
    return pl.pallas_call(
        bwd_kernel,
        grid_spec=pltpu.PrefetchScalarGridSpec(
            num_scalar_prefetch=1,
            grid=(count,),
            in_specs=[
                placed(XCOLS), placed(XBC), placed(XBC), placed(WIDTH), placed(WIDTH), STATES, whole((8, XBC)),
                whole((8, 128)), whole((8, WIDTH)), whole((128, WIDTH)), whole((128, 128 * LOCAL_HEADS)),
                whole((8, XCOLS)), *more_specs,
            ],
            out_specs=[placed(XCOLS + WIDTH), whole((8, XCOLS))],
            scratch_shapes=[
                pltpu.VMEM((TILE, 128), F32),
                pltpu.VMEM((SPAN, 128), BF),
                pltpu.VMEM((SPAN, 128), BF),
                pltpu.VMEM((LOCAL_HEADS, 1, SPAN), F32),
                pltpu.VMEM((SPAN, SPAN), F32),
                pltpu.VMEM((SPAN, SPAN), F32),
                pltpu.VMEM((SPAN, 128), F32),
                pltpu.VMEM((LOCAL_HEADS, SPAN), F32),
                pltpu.VMEM((SPAN, WIDTH), BF),
                pltpu.VMEM((SPAN, WIDTH), BF),
                pltpu.VMEM((STATE, WIDTH), BF),
                pltpu.VMEM((TILE, XBC), F32),
                pltpu.VMEM((TILE, 128), F32),
                pltpu.VMEM((8, XBC), F32),
                pltpu.VMEM((KERNEL + 1, 8, XBC), F32),
            ],
        ),
        out_shape=[
            jax.ShapeDtypeStruct((tokens, XCOLS + WIDTH), BF),
            jax.ShapeDtypeStruct((8, XCOLS), F32),
        ],
        input_output_aliases=aliases,
        compiler_params=params(),
        cost_estimate=pl.CostEstimate(
            flops=count * 10 * 10**9, bytes_accessed=count * 9 * 10**6, transcendentals=count * 4 * 10**6
        ),
        name="ssd_backward",
    )(jnp.stack(steps).astype(jnp.int32), proj, act, slope, dy, dz, states, conv_w, heads, skip, seg, spread, sofar, *more)


def gate_stats(order, y, z, dn, gain):
    steps = y.shape[0] // TILE
    block = pl.BlockSpec((TILE, WIDTH), lambda i, o: (i, 0))
    return pl.pallas_call(
        stats_kernel,
        grid_spec=pltpu.PrefetchScalarGridSpec(
            num_scalar_prefetch=1,
            grid=(steps,),
            in_specs=[block, block, block, whole((8, WIDTH))],
            out_specs=pl.BlockSpec((8, TILE), lambda i, o: (0, i)),
            scratch_shapes=[pltpu.VMEM((TILE, 128), F32)],
        ),
        out_shape=jax.ShapeDtypeStruct((8, y.shape[0]), F32),
        compiler_params=params(),
        cost_estimate=pl.CostEstimate(flops=3 * 10**9, bytes_accessed=16 * 10**6, transcendentals=3 * 10**6),
        name="gate_stats",
    )(order, y, z, dn, gain)


def gate_backward(order, st, y, z, dn, gain):
    steps = y.shape[0] // TILE
    block = pl.BlockSpec((TILE, WIDTH), lambda i, o: (i, 0))
    return pl.pallas_call(
        gate_kernel,
        grid_spec=pltpu.PrefetchScalarGridSpec(
            num_scalar_prefetch=1,
            grid=(steps,),
            in_specs=[pl.BlockSpec((8, TILE), lambda i, o: (0, i)), block, block, block, whole((8, WIDTH))],
            out_specs=[block, block, block],
            scratch_shapes=[pltpu.VMEM((TILE, 128), F32)],
        ),
        out_shape=[jax.ShapeDtypeStruct(y.shape, BF)] * 3,
        compiler_params=params(),
        cost_estimate=pl.CostEstimate(flops=6 * 10**9, bytes_accessed=32 * 10**6, transcendentals=3 * 10**6),
        name="gate_backward",
    )(order, st, y, z, dn, gain)


def norm_tokens(order, values, gain):
    rows = sum(v.shape[0] for v in values)
    return pl.pallas_call(
        functools.partial(norm_kernel, len(values)),
        grid_spec=pltpu.PrefetchScalarGridSpec(
            num_scalar_prefetch=1,
            grid=(1,),
            in_specs=[*(whole(v.shape) for v in values), whole((8, D))],
            out_specs=[whole((rows, D))],
        ),
        out_shape=[jax.ShapeDtypeStruct((rows, D), BF)],
        compiler_params=params(),
        cost_estimate=pl.CostEstimate(flops=rows * 10**6, bytes_accessed=rows * 8192, transcendentals=rows),
        name="norm_tokens",
    )(order, *values, gain)[0]


def pack_kernel(at_ref, in_ref, dt_ref, small_ref, send_ref, keep_ref, z_send_ref, z_keep_ref):
    rows = in_ref.shape[0]
    send_ref[:, rows:, :] = jnp.zeros((2, 8, XCOLS), BF)
    send_ref[0, rows:, :] = small_ref[...]
    source = lax.broadcasted_iota(jnp.int32, (HEADS, 128), 0)
    lane = lax.broadcasted_iota(jnp.int32, (HEADS, 128), 1)
    for x_ref, z_ref, x in ((send_ref, z_send_ref, 1 - at_ref[0]), (keep_ref, z_keep_ref, at_ref[0])):
        for core in range(2):
            slot = 2 * core + x
            for k in range(AHEADS):
                cols = slice(k * 128, k * 128 + 128)
                at = (k * SLOTS + slot) * 128
                z_ref[core, :, cols] = in_ref[:, pl.ds(pl.multiple_of(at, 128), 128)]
                x_ref[core, :rows, cols] = in_ref[:, pl.ds(pl.multiple_of(DI + at, 128), 128)]
            x_ref[core, :rows, WIDTH:XBC] = in_ref[:, 2 * DI :]
            wanted = jnp.where(lane < LOCAL_HEADS, (lane // 2) * 8 + slot * 2 + lane % 2, -1)
            x_ref[core, :rows, XBC:XCOLS] = nn(
                dt_ref[...], jnp.where(source == wanted, 1.0, 0.0).astype(BF)
            ).astype(BF)


def pack_weights(xi, in_w, dt_w, small):
    rows = in_w.shape[0]
    small = pad_rows(pad_cols(small[None], XCOLS))
    shapes = [(2, rows + 8, XCOLS), (2, rows, XCOLS), (2, rows, WIDTH), (2, rows, WIDTH)]
    return pl.pallas_call(
        pack_kernel,
        in_specs=[pl.BlockSpec(memory_space=pltpu.SMEM)] + [pl.BlockSpec(memory_space=pltpu.VMEM)] * 3,
        out_specs=[pl.BlockSpec(memory_space=pltpu.VMEM)] * 4,
        out_shape=[jax.ShapeDtypeStruct(shape, BF) for shape in shapes],
        cost_estimate=pl.CostEstimate(flops=10**8, bytes_accessed=3 * 10**6, transcendentals=0),
        name="pack_weights",
    )(xi[None].astype(jnp.int32), in_w, dt_w, small)


def pair_kernel(at_ref, keep_ref, got_ref, send_ref, stay_ref):
    rows = keep_ref.shape[1]
    mine = pl.ds(pl.multiple_of(at_ref[0] * rows, rows), rows)
    other = pl.ds(pl.multiple_of((1 - at_ref[0]) * rows, rows), rows)
    for out, core in ((send_ref, 1 - at_ref[1]), (stay_ref, at_ref[1])):
        out[mine, :] = keep_ref[core]
        out[other, :] = got_ref[core, :rows]


def pair_rows(xi, ci, keep, got):
    shape = (2 * keep.shape[1], keep.shape[2])
    return pl.pallas_call(
        pair_kernel,
        in_specs=[pl.BlockSpec(memory_space=pltpu.SMEM)] + [pl.BlockSpec(memory_space=pltpu.VMEM)] * 2,
        out_specs=[pl.BlockSpec(memory_space=pltpu.VMEM)] * 2,
        out_shape=[jax.ShapeDtypeStruct(shape, BF)] * 2,
        cost_estimate=pl.CostEstimate(flops=0, bytes_accessed=2 * 10**6, transcendentals=0),
        name="pair_rows",
    )(jnp.stack([xi, ci]).astype(jnp.int32), keep, got)


def place_kernel(at_ref, stay_ref, got_ref, out_ref):
    rows = stay_ref.shape[0]
    for index, ref in ((at_ref[0], stay_ref), (1 - at_ref[0], got_ref)):
        out_ref[pl.ds(pl.multiple_of(index * rows, rows), rows), :] = ref[...]


def place_rows(index, stay, got):
    return pl.pallas_call(
        place_kernel,
        in_specs=[pl.BlockSpec(memory_space=pltpu.SMEM)] + [pl.BlockSpec(memory_space=pltpu.VMEM)] * 2,
        out_specs=pl.BlockSpec(memory_space=pltpu.VMEM),
        out_shape=jax.ShapeDtypeStruct((2 * stay.shape[0], stay.shape[1]), BF),
        cost_estimate=pl.CostEstimate(flops=0, bytes_accessed=2 * 10**6, transcendentals=0),
        name="place_rows",
    )(index[None].astype(jnp.int32), stay, got)


def assemble_kernel(at_ref, pz_ref, gz_ref, px_ref, gx_ref, in_ref, dt_ref, out_ref, dt_out_ref, sum_ref):
    rows = in_ref.shape[0]
    total = jnp.zeros((rows, 128), F32)
    shared = [jnp.zeros((rows, 128), F32), jnp.zeros((rows, 128), F32)]
    dt_total = jnp.zeros((rows, HEADS), F32)
    lane = lax.broadcasted_iota(jnp.int32, (128, HEADS), 0)
    place = lax.broadcasted_iota(jnp.int32, (128, HEADS), 1)
    for core in range(2):
        for mine in (True, False):
            x = at_ref[0] if mine else 1 - at_ref[0]
            slot = 2 * core + x
            z_of = (lambda cols: pz_ref[core, x, :, cols]) if mine else (lambda cols: gz_ref[core, :, cols])
            x_of = (lambda cols: px_ref[core, x, :, cols]) if mine else (lambda cols: gx_ref[core, :, cols])
            for k in range(AHEADS):
                cols = slice(k * 128, k * 128 + 128)
                at = (k * SLOTS + slot) * 128
                for value, start in ((z_of(cols), at), (x_of(cols), DI + at)):
                    lanes = pl.ds(pl.multiple_of(start, 128), 128)
                    value = value.astype(F32)
                    out_ref[:, lanes] = value
                    total = total + value * in_ref[:, lanes].astype(F32)
            for k in range(2):
                shared[k] = shared[k] + x_of(slice(WIDTH + k * 128, WIDTH + k * 128 + 128)).astype(F32)
            wanted = jnp.where(lane < LOCAL_HEADS, (lane // 2) * 8 + slot * 2 + lane % 2, -1)
            dt_total = dt_total + nn(x_of(slice(XBC, XCOLS)), jnp.where(place == wanted, 1.0, 0.0).astype(BF))
    for k in range(2):
        cols = slice(2 * DI + k * 128, 2 * DI + k * 128 + 128)
        out_ref[:, cols] = shared[k]
        total = total + shared[k] * in_ref[:, cols].astype(F32)
    dt_out_ref[...] = dt_total
    rows_sum = jnp.sum(total, axis=1, keepdims=True) + jnp.sum(
        dt_total * dt_ref[...].astype(F32), axis=1, keepdims=True
    )
    sum_ref[...] = jnp.broadcast_to(rows_sum, (rows, 128))


def assemble_rows(xi, z_pair, z_got, x_pair, x_got, in_w, dt_w):
    rows = in_w.shape[0]
    return pl.pallas_call(
        assemble_kernel,
        in_specs=[pl.BlockSpec(memory_space=pltpu.SMEM)] + [pl.BlockSpec(memory_space=pltpu.VMEM)] * 6,
        out_specs=[pl.BlockSpec(memory_space=pltpu.VMEM)] * 3,
        out_shape=[
            jax.ShapeDtypeStruct(in_w.shape, F32),
            jax.ShapeDtypeStruct(dt_w.shape, F32),
            jax.ShapeDtypeStruct((rows, 128), F32),
        ],
        cost_estimate=pl.CostEstimate(flops=10**7, bytes_accessed=5 * 10**6, transcendentals=0),
        name="assemble_rows",
    )(xi[None].astype(jnp.int32), z_pair, z_got, x_pair, x_got, in_w, dt_w)


def small_kernel(at_ref, own_ref, x_ref, far_ref, taps_ref, heads_ref):
    xi, ci = at_ref[0], at_ref[1]
    terms = (
        (2 * ci + xi, own_ref), (2 * ci + 1 - xi, x_ref),
        (2 - 2 * ci + xi, far_ref.at[0]), (3 - 2 * ci - xi, far_ref.at[1]),
    )
    shared = jnp.zeros((8, 2 * STATE), F32)
    heads = jnp.zeros((8, HEADS), F32)
    source = lax.broadcasted_iota(jnp.int32, (128, HEADS), 0)
    place = lax.broadcasted_iota(jnp.int32, (128, HEADS), 1)
    row = lax.broadcasted_iota(jnp.int32, (8, 1), 0)
    exact = functools.partial(
        lax.dot_general,
        dimension_numbers=(((1,), (0,)), ((), ())),
        precision=lax.Precision.HIGHEST,
        preferred_element_type=F32,
    )
    for slot, ref in terms:
        for k in range(AHEADS):
            cols = ref[:, k * 128 : k * 128 + 128]
            taps_ref[:, pl.ds(pl.multiple_of((k * SLOTS + slot) * 128, 128), 128)] = cols
            wanted = jnp.where(place == k * 8 + slot * 2 + source // HEAD_DIM, 1.0, 0.0)
            heads = heads + exact(jnp.where(row == 5, cols, 0.0), wanted)
        shared = shared + ref[:, WIDTH:XBC]
        wanted = jnp.where(
            (source < LOCAL_HEADS) & (place == (source // 2) * 8 + slot * 2 + source % 2), 1.0, 0.0
        )
        heads = heads + exact(jnp.where(row < 2, ref[:, XBC:], 0.0), wanted)
    taps_ref[:, DI:] = shared
    heads_ref[...] = heads


def assemble_small(xi, ci, own, x, far):
    return pl.pallas_call(
        small_kernel,
        in_specs=[pl.BlockSpec(memory_space=pltpu.SMEM)] + [pl.BlockSpec(memory_space=pltpu.VMEM)] * 3,
        out_specs=[pl.BlockSpec(memory_space=pltpu.VMEM)] * 2,
        out_shape=[jax.ShapeDtypeStruct((8, DI + 2 * STATE), F32), jax.ShapeDtypeStruct((8, HEADS), F32)],
        cost_estimate=pl.CostEstimate(flops=10**7, bytes_accessed=10**6, transcendentals=0),
        name="assemble_small",
    )(jnp.stack([xi, ci]).astype(jnp.int32), own, x, far)


def rows_kernel(order_ref, *refs):
    rows = refs[0].shape[0]
    out_ref = refs[-1]
    for k, (ref, shift) in enumerate(zip(refs[:-1], (0, 0, 0, 0, 0, rows // 2, 0, 0, 0))):
        at = order_ref[k if k < 5 else k - 1] * rows + shift
        out_ref[pl.ds(pl.multiple_of(at, rows // 2), ref.shape[0]), :] = ref[...]


def ordered_rows(order, blocks):
    rows, cols = blocks[0].shape
    return pl.pallas_call(
        rows_kernel,
        in_specs=[pl.BlockSpec(memory_space=pltpu.SMEM)] + [pl.BlockSpec(memory_space=pltpu.VMEM)] * len(blocks),
        out_specs=pl.BlockSpec(memory_space=pltpu.VMEM),
        out_shape=jax.ShapeDtypeStruct((AHEADS * rows, cols), BF),
        compiler_params=params(),
        cost_estimate=pl.CostEstimate(flops=0, bytes_accessed=8 * 10**6, transcendentals=0),
        name="ordered_rows",
    )(order, *blocks)


def swap_x(v):
    return lax.ppermute(v, "x", SWAP)


def swap_core(v):
    return lax.ppermute(v, "core", SWAP)


def pick(v, index, axis=0):
    return lax.dynamic_index_in_dim(v, index, axis, keepdims=False)


def joined(index, mine, other, axis):
    return jnp.where(
        index == 0,
        jnp.concatenate([mine, other], axis=axis),
        jnp.concatenate([other, mine], axis=axis),
    )


def from_slots(v):
    slots, rows, cols = v.shape
    return (
        v.reshape(slots, rows, AHEADS, cols // AHEADS)
        .transpose(1, 2, 0, 3)
        .reshape(rows, slots * cols)
    )


class Return:
    def __init__(self, block):
        self.xi, self.ci = lax.axis_index("x"), lax.axis_index("core")
        self.rows = block.shape[0] // 4
        self.halves = block.astype(BF).reshape(2, 2 * self.rows, -1)
        self.flying = swap_core(pick(self.halves, 1 - self.ci))

    def turn(self, chain):
        got = chain.take(self.flying)
        pair = joined(self.ci, pick(self.halves, self.ci)[None], got[None], 0)
        self.pair = pair.reshape(2, 2, self.rows, -1)
        self.flying = swap_x(pick(self.pair, 1 - self.xi, 1))

    def land(self, chain):
        self.got = chain.take(self.flying)


class Chain:
    def __init__(self):
        self.last = ()

    def tie(self, value):
        return lax.optimization_barrier((value, self.last))[0]

    def mark(self, value):
        self.last = value
        return value

    def take(self, value):
        return self.mark(self.tie(value))


class Ring:
    def __init__(self):
        self.size = len(CYCLE)
        place = [CYCLE.index(i) for i in range(self.size)]
        position = jnp.asarray(place, jnp.int32)[lax.axis_index("ra")]
        cycle = jnp.asarray(CYCLE, jnp.int32)
        steps = jnp.arange(self.size, dtype=jnp.int32)
        self.order = cycle[(position + steps) % self.size]
        self.inverse = (jnp.asarray(place, jnp.int32) - position) % self.size

    def pairs(self, d):
        return [(CYCLE[i], CYCLE[(i + d) % self.size]) for i in range(self.size)]

    def right(self, v):
        return lax.ppermute(v, "ra", self.pairs(1))

    def left(self, v):
        return lax.ppermute(v, "ra", self.pairs(-1))


class Gather:
    def __init__(self, ring, block):
        self.ring = ring
        self.rights, self.lefts = [block], [block]

    def start(self):
        r, l = self.rights[-1], self.lefts[-1]
        if len(self.rights) == 4:
            half = r.shape[0] // 2
            r, l = r[:half], l[half:]
        self.flying = self.ring.right(r), self.ring.left(l)

    def land(self, chain):
        r, l = chain.take(self.flying)
        self.rights.append(r)
        self.lefts.append(l)

    def pieces(self):
        r, l = self.rights, self.lefts
        return [r[0], l[1], l[2], l[3], r[4], l[4], r[3], r[2], r[1]]


class Scatter:
    def __init__(self, ring, block, chain):
        self.ring, self.block, self.chain, self.count = ring, block, chain, 0

    def start(self):
        block, ring, k = self.block, self.ring, self.count
        self.count += 1
        if k == 0:
            far = block(4)
            half = far.shape[0] // 2
            sends = far[:half], far[half:]
        elif k == 1:
            up, down = block(3), block(5)
            half = up.shape[0] // 2
            r, l = self.right.astype(F32), self.left.astype(F32)
            sends = (
                jnp.concatenate([up[:half] + r, up[half:]], axis=0),
                jnp.concatenate([down[:half], down[half:] + l], axis=0),
            )
        else:
            sends = block(4 - k) + self.right.astype(F32), block(4 + k) + self.left.astype(F32)
        sends = self.chain.mark((sends[0].astype(BF), sends[1].astype(BF)))
        self.flying = ring.right(sends[0]), ring.left(sends[1])

    def land(self, chain):
        self.right, self.left = chain.take(self.flying)

    def total(self):
        return self.block(0) + self.right.astype(F32) + self.left.astype(F32)


def flat_index(sizes):
    index = 0
    for name, size in zip(ALL, sizes):
        index = index * size + lax.axis_index(name)
    return index


class SmallSum:
    def __init__(self, v):
        self.value = v
        self.bits = [1, 2, 4]

    def start(self):
        bit = self.bits.pop(0)
        self.flying = lax.ppermute(self.value, "ra", [(i, i ^ bit) for i in range(len(CYCLE))])

    def land(self, chain):
        self.value = chain.mark(self.value + chain.take(self.flying))


def permute_blocks(v, order, width):
    return jnp.concatenate(
        [
            lax.dynamic_slice(v, (0, order[k] * width), (v.shape[0], width))
            for k in range(v.shape[1] // width)
        ],
        axis=1,
    )


def pad_rows(v, rows=8):
    return jnp.concatenate([v, jnp.zeros((rows - v.shape[0], v.shape[1]), v.dtype)], axis=0)


def pad_cols(v, cols):
    return jnp.concatenate([v, jnp.zeros(v.shape[:-1] + (cols - v.shape[-1],), v.dtype)], axis=-1)


def per_device(
    sizes, tokens_short, tokens_long, cot_short, cot_long, seq_lengths,
    norm_gain, in_w, dt_w, conv_w, conv_b, dt_bias, a_log, d_skip, gate_gain, out_w,
):
    ringed = sizes == (8, 2, 1, 2)
    short, long = tokens_short.shape[0], tokens_long.shape[0]
    xi, ci = lax.axis_index("x"), lax.axis_index("core")
    slot = ci * 2 + xi
    feature = D // AHEADS
    mine_cols = lambda v: pick(v.reshape(v.shape[0], AHEADS, SLOTS, -1), slot, 2).reshape(v.shape[0], -1)
    chain = Chain()

    if ringed:
        ring = Ring()
        order, inverse = ring.order, ring.inverse
        from_ring = lambda v: permute_blocks(v, inverse, feature)
    else:
        order = jnp.arange(AHEADS, dtype=jnp.int32)
        from_ring = lambda v: v

    width = conv_w.shape[1]
    pieces = [conv_w.reshape(-1), conv_b, norm_gain, gate_gain]
    ends = np.cumsum([0] + [p.shape[0] for p in pieces])
    small = jnp.concatenate(pieces)
    group = ("core", "x")
    everyone = lambda v: lax.all_gather(v, group, axis=0, tiled=True)

    def stage(v, bit):
        count = int(np.prod(sizes))
        return lax.ppermute(v, ALL, [(i, i ^ bit) for i in range(count)])

    def widen(v, got, bit):
        return joined((flat_index(sizes) // bit) % 2, v, got, 0)

    if ringed:
        rows, n = in_w.shape[0], small.shape[0]
        x_send, x_keep, z_send, z_keep = chain.mark(pack_weights(xi, in_w, dt_w, small))
        x_got = chain.take(swap_x(x_send))
        small = widen(small[None], x_got[0, rows : rows + 1, :n], 1)
        passing = stage(small, 2)
        send, stay = chain.mark(pair_rows(xi, ci, x_keep, x_got))
        got = swap_core(send)
        small = widen(small, chain.take(passing), 2)
        passing = stage(small, 4)
        got = chain.take(got)
        small = widen(small, chain.take(passing), 4)
        passing = stage(small, 8)
        x_block = chain.mark(place_rows(ci, stay, got))
        small = widen(small, chain.take(passing), 8)
        small = widen(small, chain.take(stage(small, 16)), 16)
        gather_x = Gather(ring, chain.tie(x_block))
        gather_x.start()
        z_got = swap_x(chain.tie(z_send))
    else:
        small = lax.all_gather(small[None], ALL, axis=0, tiled=True)
    norm_full = pad_rows(small[:, ends[2] : ends[3]].reshape(1, -1).astype(F32))
    u_own = chain.mark(norm_tokens(order, [chain.tie(tokens_short), tokens_long], norm_full))
    xh = everyone(u_own)
    if ringed:
        gather_x.land(chain)
        gather_x.start()

    small, dt_bias, a_log, d_skip, cot_s, cot_l = chain.mark(
        chain.tie((small, dt_bias, a_log, d_skip, cot_short, cot_long))
    )
    live_s = (jnp.arange(short) < seq_lengths[0, 0]).astype(F32)[:, None]
    live_l = (jnp.arange(long) < seq_lengths[1, 0]).astype(F32)[:, None]
    dv_own = chain.mark(jnp.concatenate([(live_s * cot_s).astype(BF), (live_l * cot_l).astype(BF)], axis=0))
    taps = small[:, : ends[2]].reshape(-1, KERNEL + 1, width)
    taps = taps.transpose(1, 0, 2).reshape(KERNEL + 1, -1).astype(F32)
    taps = jnp.concatenate([mine_cols(taps[:, :DI]), taps[:, DI:]], axis=1)
    conv_taps, conv_bias = pad_rows(taps[:KERNEL]), pad_rows(taps[KERNEL:])
    gate_mine = pad_rows(mine_cols(small[:, ends[3] :].reshape(1, -1).astype(F32)))
    neg_rate = -jnp.exp(a_log.astype(F32))
    heads = pad_rows(pad_cols(mine_cols(jnp.stack([dt_bias.astype(F32), neg_rate])), 128))
    skip = pad_rows(jnp.repeat(mine_cols(d_skip.astype(F32)[None]), HEAD_DIM, axis=1))
    head_rows = np.arange(128)[:, None]
    seg = jnp.asarray(
        (head_rows < 2 * LOCAL_HEADS) & (head_rows % LOCAL_HEADS == np.arange(WIDTH)[None, :] // HEAD_DIM), BF
    )
    spread = jnp.asarray(
        (head_rows < 3 * LOCAL_HEADS)
        & (head_rows % LOCAL_HEADS == np.arange(128 * LOCAL_HEADS)[None, :] // 128),
        BF,
    )
    gate_mine, *seq_params = chain.mark((gate_mine, conv_taps, conv_bias, heads, skip, seg, spread))
    if ringed:
        send, stay = chain.mark(pair_rows(xi, ci, z_keep, chain.take(z_got)))
        z_block = chain.mark(place_rows(ci, stay, chain.take(swap_core(send))))
    slots = [jnp.int32(k) for k in range(SLOTS)]

    if ringed:
        gather_x.land(chain)
        gather_x.start()
        gather_x.land(chain)
        gather_x.start()
        gather_z = Gather(ring, z_block)
        gather_z.start()
        gather_z.land(chain)
        gather_x.land(chain)
        w_x = chain.mark(jnp.concatenate(gather_x.pieces(), axis=0))
        xh = chain.take(xh)
        dv = everyone(chain.tie(dv_own))
        gather_z.start()
        gather_o = Gather(ring, chain.tie(out_w))
        gather_o.start()
        both = gather_o, gather_z
        proj = chain.mark(nn(chain.tie(xh), w_x))
        for gather in both:
            gather.land(chain)
            gather.start()
        kept = chain.mark(ssd_forward(slots[:2], chain.tie(proj), *seq_params))
        for gather in both:
            gather.land(chain)
            gather.start()
        y, act, slope, states = chain.mark(ssd_forward(slots[2:], chain.tie(proj), *seq_params, earlier=kept))
        for gather in both:
            gather.land(chain)
        gather_o.start()
        w_all = chain.mark(jnp.concatenate([w_x, jnp.concatenate(gather_z.pieces(), axis=0)], axis=1))
        z = chain.mark(nn(chain.tie(xh), w_all[:, XCOLS:]).astype(BF))
        gather_o.land(chain)
        w_o = chain.mark(ordered_rows(order, chain.tie(gather_o.pieces())))
        dv = chain.take(dv)
        dn = chain.mark(nt(dv, w_o).astype(BF))
    else:
        full = lax.all_gather(in_w, ALL, axis=0, tiled=True)
        full_dt = lax.all_gather(dt_w, ALL, axis=0, tiled=True)
        full_out = lax.all_gather(out_w, ALL, axis=0, tiled=True)
        w_z = mine_cols(full[:, :DI])
        w_x = jnp.concatenate(
            [mine_cols(full[:, DI : 2 * DI]), full[:, 2 * DI :], pad_cols(mine_cols(full_dt), 128)], axis=-1
        )
        w_o = pick(full_out.reshape(AHEADS, SLOTS, 128, D), slot, 1).reshape(WIDTH, D)
        dv = everyone(dv_own)
        proj = nn(xh, w_x)
        y, act, slope, states = ssd_forward(slots, proj, *seq_params)
        dn = nt(dv, w_o).astype(BF)
        z = nn(xh, w_z).astype(BF)
        w_all = jnp.concatenate([w_x, w_z], axis=1)

    straight = jnp.arange(AHEADS, dtype=jnp.int32)
    st = chain.mark(gate_stats(straight, y, chain.tie(z), dn, gate_mine))
    st = st + swap_core(st)
    st = st + swap_x(st)
    n, dy, dz = chain.mark(gate_backward(straight, st, y, z, dn, gate_mine))

    own = short + long
    rows_of = lambda v, start, count: lax.dynamic_slice(v, (start * own, 0), (count * own, v.shape[1]))

    def unit_product(dx, start, count):
        dx = chain.tie(dx)
        return nt(rows_of(dx, start, count), w_all)

    def backward_call(steps, sofar, earlier):
        return chain.mark(
            ssd_backward(steps, chain.tie(proj), act, slope, dy, dz, states, *seq_params, sofar, earlier=earlier)
        )

    none_yet = jnp.zeros((8, XCOLS), F32)

    far, mid = 2 * (1 - ci), 2 * ci + 1 - xi
    g_out = chain.mark(tn(n, dv).astype(BF))
    reduced = lambda v, axes: lax.psum_scatter(v, axes, scatter_dimension=0, tiled=True)
    if ringed:
        own_out = reduced(g_out, "ra").astype(F32)
        g_z = chain.mark(tn(chain.tie(xh), dz))
        blocks_z = g_z.reshape(AHEADS, -1, WIDTH)
        scatter_z = Scatter(ring, lambda k: blocks_z[k], chain)
        scatter_z.start()
    else:
        g_z = tn(xh, dz)
    branch = chain.mark(nn(chain.tie(n), w_o).astype(BF))
    branch = reduced(branch, group)
    if ringed:
        scatter_z.land(chain)
        scatter_z.start()
        dx, acc = backward_call([far, far + 1], none_yet, ())
        scatter_z.land(chain)
        scatter_z.start()
        far_u = swap_core(chain.mark(unit_product(dx, far, 2).astype(BF)))
        dx, acc = backward_call([mid], acc, (chain.tie(dx),))
        scatter_z.land(chain)
        scatter_z.start()
        far_u = chain.take(far_u)
        mid_u = chain.mark(
            (unit_product(dx, mid, 1) + rows_of(far_u, 1 - xi, 1).astype(F32)).astype(BF)
        )
        mid_u = swap_x(mid_u)
        dx, acc = backward_call([slot], acc, (chain.tie(dx),))
        scatter_z.land(chain)
        back_z = Return(chain.mark(scatter_z.total()))

        def blocks_x(first, last):
            part = tn(xh[:, first * feature : last * feature], chain.tie(dx)[:, :XCOLS])
            return dict(enumerate(chain.mark(part).reshape(last - first, feature, XCOLS), first))

        made = blocks_x(4, 5)
        scatter_x = Scatter(ring, lambda k: made[k], chain)
        scatter_x.start()
        tally = SmallSum(chain.tie(acc))
        tally.start()
        made.update(blocks_x(3, 4))
        made.update(blocks_x(5, 6))
        scatter_x.land(chain)
        tally.land(chain)
        scatter_x.start()
        tally.start()
        made.update(blocks_x(0, 3))
        made.update(blocks_x(6, 8))
        scatter_x.land(chain)
        tally.land(chain)
        scatter_x.start()
        tally.start()
        back_z.turn(chain)
        du_own = unit_product(dx, slot, 1) + rows_of(far_u, xi, 1).astype(F32)
        du_own = chain.mark(lax.optimization_barrier(du_own))
        scatter_x.land(chain)
        tally.land(chain)
        scatter_x.start()
        mid_u = chain.take(mid_u)
        du = chain.mark(du_own + mid_u.astype(F32))
        scatter_x.land(chain)
        back_x = Return(chain.mark(scatter_x.total()))
        acc = tally.value
        acc_x = swap_x(acc)
        back_z.land(chain)
        back_x.turn(chain)
        acc_x = chain.take(acc_x)
        acc_far = chain.take(swap_core(jnp.stack([acc, acc_x])))
        taps_total, head_total = chain.mark(assemble_small(xi, ci, acc, acc_x, acc_far))
        own_conv = lax.dynamic_slice(taps_total, (0, flat_index(sizes) * width), (KERNEL + 1, width))
    else:
        dx, acc = backward_call(slots, none_yet, ())
        du = reduced(nt(dx, w_all), group)
        g_x = tn(xh, dx[:, :XCOLS])
        acc = lax.psum(acc, ("ra", "rb"))
        acc_x = swap_x(acc)
        acc_far = swap_core(jnp.stack([acc, acc_x]))
        taps_total, head_total = assemble_small(xi, ci, acc, acc_x, acc_far)
        own_conv = lax.dynamic_slice(taps_total, (0, flat_index(sizes) * width), (KERNEL + 1, width))
    v_s, v_l = branch[:short].astype(F32), branch[short:].astype(F32)
    du_s, du_l = du[:short], du[short:]

    out_short = (tokens_short.astype(F32) + live_s * v_s).astype(BF)
    out_long = (tokens_long.astype(F32) + live_l * v_l).astype(BF)

    def token_grad(token, cot, d_u):
        residual = token.astype(F32)
        row_scale = lax.rsqrt(jnp.mean(residual * residual, axis=-1, keepdims=True) + EPS)
        unit = residual * row_scale
        d_norm = from_ring(d_u) * norm_full[0:1]
        return cot.astype(F32) + row_scale * (d_norm - unit * jnp.mean(d_norm * unit, axis=-1, keepdims=True))

    grad_short, grad_long = chain.mark(
        (token_grad(tokens_short, cot_short, du_s), token_grad(tokens_long, cot_long, du_l))
    )

    if ringed:
        back_x.land(chain)
        grad_in_w, grad_dt_w, norm_sum = chain.mark(
            assemble_rows(xi, back_z.pair, back_z.got, back_x.pair, back_x.got, in_w, dt_w)
        )
        norm_sum = norm_sum[:, 0]
    else:
        here = (jnp.arange(SLOTS) == slot).astype(F32)
        wider = lambda v: (v.reshape(D, AHEADS, 1, -1) * here[:, None]).reshape(D, -1)
        reduce = lambda v: lax.psum_scatter(v, ALL, scatter_dimension=0, tiled=True)
        grad_in_w = reduce(
            jnp.concatenate([wider(g_z), wider(g_x[:, :WIDTH]), g_x[:, WIDTH:XBC]], axis=1)
        )
        grad_dt_w = reduce(wider(g_x[:, XBC : XBC + LOCAL_HEADS]))
        own_out = reduce(
            (g_out.astype(F32).reshape(AHEADS, 1, 128, D) * here[:, None, None]).reshape(DI, D)
        )

        norm_sum = jnp.sum(in_w.astype(F32) * grad_in_w, axis=1) + jnp.sum(dt_w.astype(F32) * grad_dt_w, axis=1)

    grad_norm_gain = norm_sum / norm_gain.astype(F32)
    grad_gate_gain = jnp.sum(out_w.astype(F32) * own_out, axis=1) / gate_gain.astype(F32)

    return (
        out_short,
        out_long,
        grad_short,
        grad_long,
        grad_norm_gain,
        grad_in_w,
        grad_dt_w,
        own_conv[:KERNEL],
        own_conv[KERNEL],
        head_total[0],
        head_total[1] * neg_rate,
        head_total[5],
        grad_gate_gain,
        own_out,
    )


def solution(mesh):
    wide, narrow = mesh.shape["wide"], mesh.shape["narrow"]
    sizes = (wide // 2, 2, narrow // 2, 2)
    split = Mesh(mesh.devices.reshape(sizes), ALL)
    rows, vector, columns = P(ALL, None), P(ALL), P(None, ALL)
    return jax.shard_map(
        functools.partial(per_device, sizes),
        mesh=split,
        in_specs=(
            rows, rows, rows, rows, columns, vector, rows, rows, columns, vector, P(), P(), P(), vector, rows,
        ),
        out_specs=(
            rows, rows, rows, rows, vector, rows, rows, columns, vector, P(), P(), P(), vector, rows,
        ),
        check_vma=False,
    )
```

```python
import functools

import jax
import jax.numpy as jnp
import numpy as np
from jax import lax
from jax.experimental import pallas as pl
from jax.experimental.pallas import tpu as pltpu
from jax.sharding import Mesh
from jax.sharding import PartitionSpec as P

D = 2048
DI = 4096
HEADS = 64
HEAD_DIM = 64
STATE = 128
KERNEL = 4
SPAN = 256
EPS = 1e-05
BF = jnp.bfloat16
F32 = jnp.float32

SLOTS = 4
AHEADS = 8
WIDTH = DI // SLOTS
LOCAL_HEADS = HEADS // SLOTS
XBC = WIDTH + 2 * STATE
XCOLS = XBC + 128
ALL = ("ra", "core", "rb", "x")
NEG = -1e30
TILE = 640
HEAD = 128

SWAP = [(0, 1), (1, 0)]
CYCLE = (0, 2, 4, 6, 7, 5, 3, 1)


def nt(a, b):
    return lax.dot_general(a, b, (((1,), (1,)), ((), ())), preferred_element_type=F32)


def nn(a, b):
    return lax.dot_general(a, b, (((1,), (0,)), ((), ())), preferred_element_type=F32)


def tn(a, b):
    return lax.dot_general(a, b, (((0,), (0,)), ((), ())), preferred_element_type=F32)


LOG2E = 1.4426950408889634
ROWS = 64


def sigmoid(v):
    return 0.5 * jnp.tanh(0.5 * v) + 0.5


def lane_index():
    return lax.broadcasted_iota(jnp.int32, (1, 128), 1)


def three_parts(values):
    values = jnp.where(lane_index() < LOCAL_HEADS, values, 0.0)
    high = values.astype(BF).astype(F32)
    rest = values - high
    mid = rest.astype(BF).astype(F32)
    low = rest - mid
    return (high + pltpu.roll(mid, LOCAL_HEADS, 1) + pltpu.roll(low, 2 * LOCAL_HEADS, 1)).astype(BF)


def add_parts(values):
    return values + pltpu.roll(values, 128 - LOCAL_HEADS, 1) + pltpu.roll(values, 128 - 2 * LOCAL_HEADS, 1)


def triangle(n, lower):
    i = lax.broadcasted_iota(jnp.int32, (n, n), 0)
    j = lax.broadcasted_iota(jnp.int32, (n, n), 1)
    return jnp.where(i >= j if lower else i <= j, 1.0, 0.0).astype(BF)


def running_sum(values, lower):
    return add_parts(nn(triangle(values.shape[0], lower), three_parts(values)))


def two_parts(values):
    values = jnp.where(lane_index() < LOCAL_HEADS, values, 0.0)
    high = values.astype(BF).astype(F32)
    return (high + pltpu.roll(values - high, LOCAL_HEADS, 1)).astype(BF)


def softplus(v):
    return jnp.maximum(v, 0.0) + jnp.log1p(jnp.exp(-jnp.abs(v)))


def conv_tile(p_ref, cw_ref, cb_ref, r0, cols):
    starts = (r0 == 0) | (r0 == HEAD)
    before = p_ref[pl.ds(pl.multiple_of(jnp.maximum(r0 - 8, 0), 8), 8), cols]
    before = jnp.where(starts, 0.0, before)
    here = p_ref[pl.ds(r0, ROWS), cols]
    both = jnp.concatenate([before, here], axis=0)
    back = [here] + [pltpu.roll(both, m, 0)[8:] for m in (1, 2, 3)]
    total = cb_ref[0:1, cols]
    for m in range(KERNEL):
        total = total + cw_ref[3 - m : 4 - m, cols] * back[m]
    return total, back


def fwd_kernel(
    steps_ref, p_ref, cw_ref, cb_ref, hp_ref, dsk_ref, seg_ref, bc_ref, *refs
):
    y_ref, act_ref, slope_ref, h_ref, dt_s, parts_s, grow_s, rt_s, g_s = refs[-9:]
    lane = lane_index()

    def conv_step(i, carry):
        r0 = pl.multiple_of(i * ROWS, ROWS)
        rows = pl.ds(r0, ROWS)
        for c in range(XBC // 128):
            cols = slice(c * 128, c * 128 + 128)
            conv, _ = conv_tile(p_ref, cw_ref, cb_ref, r0, cols)
            gate = sigmoid(conv)
            act = conv * gate
            act_ref[rows, cols] = act.astype(BF)
            slope_ref[rows, cols] = (gate + act * (1.0 - gate)).astype(BF)
        dt_s[rows, :] = softplus(p_ref[rows, XBC:] + hp_ref[0:1])
        return carry

    lax.fori_loop(0, TILE // ROWS, conv_step, 0, unroll=2)
    rate = hp_ref[1:2]

    def block(off, q, read_state, make_state):
        rows = pl.ds(off, q)
        dt = dt_s[rows, :]
        cum2 = running_sum(dt * rate, True) * LOG2E
        parts_s[:q, :] = three_parts(cum2)
        turned = (cum2 - jnp.log2(dt)).T
        for h in range(LOCAL_HEADS):
            rt_s[h, :, :q] = turned[h : h + 1]
        b = act_ref[rows, WIDTH : WIDTH + STATE]
        c = act_ref[rows, WIDTH + STATE :]
        g_s[:q, :q] = nt(c, b)
        if read_state:
            grow_s[:q, :] = two_parts(jnp.exp2(cum2))
        if make_state:
            grow_s[:q, :] = two_parts(jnp.exp2(cum2[q - 1 : q] - cum2) * dt)
            b_turned = b.astype(F32).T.astype(BF)
        diagonal = lax.broadcasted_iota(jnp.int32, (128, 128), 0) >= lax.broadcasted_iota(
            jnp.int32, (128, 128), 1
        )

        def pair(p, carry):
            lanes = pl.ds(pl.multiple_of(p * 128, 128), 128)
            x2 = act_ref[rows, lanes]
            zero = jnp.zeros_like(x2)
            x_heads = [jnp.where(lane < HEAD_DIM, x2, zero), jnp.where(lane < HEAD_DIM, zero, x2)]
            cols = nn(parts_s[:q, :], bc_ref[:, pl.ds(pl.multiple_of(p * 256, 256), 256)])
            if read_state:
                carried = nn(grow_s[:q, :], seg_ref[:, lanes]) * nn(c, h_ref[0, :, lanes].astype(BF))
            for rt in range(q // 128):
                top = rt * 128
                mixes = []
                for j in range(2):
                    col = cols[top : top + 128, j * 128 : j * 128 + 128]
                    for ct in range(rt + 1):
                        lo = ct * 128
                        spread = col - rt_s[p * 2 + j, :, lo : lo + 128]
                        if ct == rt:
                            spread = jnp.where(diagonal, spread, NEG)
                        mixes.append((g_s[top : top + 128, lo : lo + 128] * jnp.exp2(spread)).astype(BF))
                x_both = jnp.concatenate([x[: top + 128] for x in x_heads], axis=0)
                out = nn(jnp.concatenate(mixes, axis=1), x_both)
                out = out + dsk_ref[0:1, lanes] * x2[top : top + 128].astype(F32)
                if read_state:
                    out = out + carried[top : top + 128]
                y_ref[pl.ds(off + top, 128), lanes] = out.astype(y_ref.dtype)
            if make_state:
                wide = nn(grow_s[:q, :], seg_ref[:, lanes])
                h_ref[0, :, lanes] = nn(b_turned, (wide * x2.astype(F32)).astype(BF))
            return carry

        lax.fori_loop(0, LOCAL_HEADS // 2, pair, 0, unroll=True)

    block(0, HEAD, False, False)
    block(HEAD, SPAN, False, True)
    block(HEAD + SPAN, SPAN, True, False)


def bwd_kernel(
    steps_ref, p_ref, act_ref, slope_ref, dy_ref, dz_ref, h_ref, cw_ref, hp_ref, dsk_ref, seg_ref, bc_ref, sofar_ref, *refs
):
    dp_ref, acc_ref = refs[-17:-15]
    heads_at = slice(XBC, XCOLS)
    dt_s, parts_s, grow_s, ct_s, gt_s, dgt_s, kc_s, kr_s, fold_s, dbc_s, ds_s, da_s, dst_s, after_s, sums_s = refs[-15:]
    lane = lane_index()
    head_row = lax.broadcasted_iota(jnp.int32, (LOCAL_HEADS, 1), 0)

    @pl.when(pl.program_id(0) == 0)
    def _():
        acc_ref[...] = sofar_ref[...]

    rate = hp_ref[1:2]
    dt_s[...] = softplus(p_ref[:, XBC:] + hp_ref[0:1])

    def block(off, q, state_in, state_out):
        rows = pl.ds(off, q)
        dt = dt_s[rows, :]
        cum2 = running_sum(dt * rate, True) * LOG2E
        parts_s[:q, :] = three_parts(cum2 - jnp.log2(dt))
        turned = cum2.T
        for h in range(LOCAL_HEADS):
            ct_s[h, :, :q] = turned[h : h + 1]
        b = act_ref[rows, WIDTH : WIDTH + STATE]
        c = act_ref[rows, WIDTH + STATE :]
        gt_s[:q, :q] = nt(b, c)
        dgt_s[:q, :q] = jnp.zeros((q, q), F32)
        kc_s[:q, :] = jnp.zeros((q, 128), F32)
        kr_s[:, :q] = jnp.zeros((LOCAL_HEADS, q), F32)
        if state_in:
            grow_s[:q, :] = two_parts(jnp.exp2(cum2))
            c_turned = c.astype(F32).T.astype(BF)
        if state_out:
            decay = jnp.exp2(cum2[q - 1 : q] - cum2)
            grow_s[:q, :] = two_parts(decay * dt)
        diagonal = lax.broadcasted_iota(jnp.int32, (128, 128), 1) >= lax.broadcasted_iota(
            jnp.int32, (128, 128), 0
        )
        tiles = q // 128

        def pair(p, carry):
            lanes = pl.ds(pl.multiple_of(p * 128, 128), 128)
            x2 = act_ref[rows, lanes]
            dy2 = dy_ref[rows, lanes]
            zero = jnp.zeros_like(dy2)
            dy_heads = [jnp.where(lane < HEAD_DIM, dy2, zero), jnp.where(lane < HEAD_DIM, zero, dy2)]
            cols = nn(parts_s[:q, :], bc_ref[:, pl.ds(pl.multiple_of(p * 256, 256), 256)])
            if state_in:
                hb = h_ref[0, :, lanes].astype(BF)
                dyc = dy2.astype(F32) * nn(grow_s[:q, :], seg_ref[:, lanes])
                dyb = dyc.astype(BF)
                fold_s[:q, lanes] = (dyc * nn(c, hb)).astype(BF)
                dbc_s[:q, lanes] = dyb
                ds_s[:, lanes] = nn(c_turned, dyb).astype(BF)
            if state_out:
                sb = ds_s[:, lanes]
                wide = nn(grow_s[:q, :], seg_ref[:, lanes])
                bd = nn(b, sb)
                xf = x2.astype(F32)
                fold_s[:q, lanes] = (xf * bd).astype(BF)
                dbc_s[:q, lanes] = (wide * xf).astype(BF)
                late = wide * bd
            picks = [jnp.where(lane == p * 2 + j, 1.0, 0.0).astype(BF) for j in range(2)]
            marks = [jnp.where(head_row == p * 2 + j, 1.0, 0.0).astype(BF) for j in range(2)]
            for jt in range(tiles):
                lo = jt * 128
                span = q - lo
                xj = x2[lo : lo + 128]
                mixes = []
                terms = []
                dgs = [None] * tiles
                for j in range(2):
                    col = cols[lo : lo + 128, j * 128 : j * 128 + 128]
                    for it in range(jt, tiles):
                        at = it * 128
                        spread = ct_s[p * 2 + j, :, at : at + 128] - col
                        if it == jt:
                            spread = jnp.where(diagonal, spread, NEG)
                        e = jnp.exp2(spread)
                        score = gt_s[lo : lo + 128, at : at + 128]
                        dme = nt(xj, dy_heads[j][at : at + 128]) * e
                        dgs[it] = dme if dgs[it] is None else dgs[it] + dme
                        terms.append((dme * score).astype(BF))
                        mixes.append((score * e).astype(BF))
                for it in range(jt, tiles):
                    dgt_s[lo : lo + 128, it * 128 : it * 128 + 128] += dgs[it]
                half = len(terms) // 2
                kc_s[lo : lo + 128, :] += nn(
                    jnp.concatenate(terms, axis=1),
                    jnp.concatenate([jnp.broadcast_to(v, (span, 128)) for v in picks], axis=0),
                )
                kr_s[:, lo:q] += nn(
                    jnp.concatenate([jnp.broadcast_to(v, (LOCAL_HEADS, 128)) for v in marks], axis=1),
                    jnp.concatenate(
                        [jnp.concatenate(terms[:half], axis=1), jnp.concatenate(terms[half:], axis=1)], axis=0
                    ),
                )
                dy_both = jnp.concatenate([d[lo:] for d in dy_heads], axis=0)
                out = nn(jnp.concatenate(mixes, axis=1), dy_both)
                dyj = dy2[lo : lo + 128].astype(F32)
                acc_ref[5:6, lanes] += jnp.sum(dyj * xj.astype(F32), axis=0, keepdims=True)
                out = out + dsk_ref[0:1, lanes] * dyj
                if state_out:
                    out = out + late[lo : lo + 128]
                da_s[pl.ds(off + lo, 128), lanes] = out
            return carry

        lax.fori_loop(0, LOCAL_HEADS // 2, pair, 0, unroll=True)

        dgt = dgt_s[:q, :q].astype(BF)
        db = nn(dgt, c)
        dc = tn(dgt, b)
        kcol = kc_s[:q, :]
        row_terms = jnp.concatenate([kr_s[:, :q], jnp.zeros((128 - LOCAL_HEADS, q), F32)], axis=0)
        d_cum = row_terms.T - kcol
        inverse = jnp.where(dt > 1e-30, 1.0 / jnp.maximum(dt, 1e-30), 0.0)
        d_dt = kcol * inverse
        if state_in:
            d_cum = d_cum + nt(fold_s[:q, :], seg_ref[...])
            dc = dc + nt(dbc_s[:q, :], h_ref[0].astype(BF))
        if state_out:
            db = db + nt(dbc_s[:q, :], ds_s[...])
            d_weights = nt(fold_s[:q, :], seg_ref[...])
            d_dt = d_dt + d_weights * decay
            w_term = d_weights * decay * dt
            last = lax.broadcasted_iota(jnp.int32, (q, 1), 0) == q - 1
            d_cum = d_cum - w_term + jnp.where(last, jnp.sum(w_term, axis=0, keepdims=True), 0.0)
        da_s[rows, WIDTH : WIDTH + STATE] = db
        da_s[rows, WIDTH + STATE :] = dc
        d_rate = running_sum(d_cum, False)
        dst_s[rows, :] = d_dt + d_rate * rate
        acc_ref[1:2, heads_at] += jnp.sum(d_rate * dt, axis=0, keepdims=True)

    block(0, HEAD, False, False)
    block(HEAD + SPAN, SPAN, True, False)
    block(HEAD, SPAN, False, True)

    d_soft = dst_s[...] * jax.nn.sigmoid(p_ref[:, XBC:] + hp_ref[0:1])
    d_soft = jnp.where(lane < LOCAL_HEADS, d_soft, 0.0)
    acc_ref[0:1, heads_at] += jnp.sum(d_soft, axis=0, keepdims=True)
    dp_ref[:, XBC:XCOLS] = d_soft.astype(BF)
    dp_ref[:, XCOLS:] = dz_ref[...]
    sums_s[...] = jnp.zeros_like(sums_s)
    after_s[...] = jnp.zeros_like(after_s)

    def conv_step(i, carry):
        r0 = pl.multiple_of(TILE - ROWS - i * ROWS, ROWS)
        rows = pl.ds(r0, ROWS)
        ends = (r0 + ROWS == HEAD) | (r0 + ROWS == TILE)
        fold = lambda v: jnp.sum(v.reshape(ROWS // 8, 8, 128), axis=0)
        for c in range(XBC // 128):
            cols = slice(c * 128, c * 128 + 128)
            here = p_ref[rows, cols]
            d_conv = da_s[rows, cols] * slope_ref[rows, cols].astype(F32)
            both = jnp.concatenate([d_conv, jnp.where(ends, 0.0, after_s[:, cols])], axis=0)
            after_s[:, cols] = d_conv[:8]
            total = cw_ref[3:4, cols] * d_conv
            sums_s[3, :, cols] += fold(d_conv * here)
            sums_s[4, :, cols] += fold(d_conv)
            for m in (1, 2, 3):
                ahead = pltpu.roll(both, ROWS + 8 - m, 0)[:ROWS]
                total = total + cw_ref[3 - m : 4 - m, cols] * ahead
                sums_s[3 - m, :, cols] += fold(ahead * here)
            dp_ref[rows, cols] = total.astype(BF)
        return carry

    lax.fori_loop(0, TILE // ROWS, conv_step, 0, unroll=2)
    for k in range(KERNEL + 1):
        acc_ref[k : k + 1, :XBC] += jnp.sum(sums_s[k], axis=0, keepdims=True)


def stats_kernel(order_ref, y_ref, z_ref, dn_ref, gain_ref, st_ref, both_s):
    lane = lane_index()

    def step(i, carry):
        rows = pl.ds(pl.multiple_of(i * ROWS, ROWS), ROWS)
        p1 = jnp.zeros((ROWS, 128), F32)
        p2 = jnp.zeros((ROWS, 128), F32)
        for k in range(AHEADS):
            lanes = pl.ds(pl.multiple_of(order_ref[k] * 128, 128), 128)
            z = z_ref[rows, lanes].astype(F32)
            g = y_ref[rows, lanes].astype(F32) * (z * sigmoid(z))
            p1 = p1 + g * g
            p2 = p2 + g * (dn_ref[rows, k * 128 : k * 128 + 128].astype(F32) * gain_ref[0:1, lanes])
        both_s[rows, :] = jnp.where(
            lane == 0,
            jnp.sum(p1, axis=1, keepdims=True),
            jnp.where(lane == 1, jnp.sum(p2, axis=1, keepdims=True), 0.0),
        )
        return carry

    lax.fori_loop(0, y_ref.shape[0] // ROWS, step, 0, unroll=2)
    st_ref[...] = both_s[...].T[0:8]


def gate_kernel(order_ref, st_ref, y_ref, z_ref, dn_ref, gain_ref, n_ref, dy_ref, dz_ref, st_s):
    st_s[...] = jnp.concatenate([st_ref[...], jnp.zeros((120, y_ref.shape[0]), F32)], axis=0).T

    def step(i, carry):
        rows = pl.ds(pl.multiple_of(i * ROWS, ROWS), ROWS)
        st = st_s[rows, :]
        rg = lax.rsqrt(st[:, 0:1] * (1.0 / DI) + EPS)
        mean = rg * rg * st[:, 1:2] * (1.0 / DI)
        for k in range(AHEADS):
            lanes = pl.ds(pl.multiple_of(order_ref[k] * 128, 128), 128)
            fixed = slice(k * 128, k * 128 + 128)
            gain = gain_ref[0:1, lanes]
            z = z_ref[rows, lanes].astype(F32)
            y = y_ref[rows, lanes].astype(F32)
            sg = sigmoid(z)
            silu = z * sg
            ghat = y * silu * rg
            dg = rg * (dn_ref[rows, fixed].astype(F32) * gain) - ghat * mean
            n_ref[rows, fixed] = (ghat * gain).astype(BF)
            dy_ref[rows, lanes] = (dg * silu).astype(BF)
            dz_ref[rows, lanes] = (dg * y * (sg + silu * (1.0 - sg))).astype(BF)
        return carry

    lax.fori_loop(0, y_ref.shape[0] // ROWS, step, 0, unroll=2)


def norm_kernel(pieces, order_ref, *refs):
    gain_ref, u_ref = refs[pieces], refs[-1]
    at = 0
    for x_ref in refs[:pieces]:
        count = x_ref.shape[0] // ROWS

        def step(i, carry, x_ref=x_ref, at=at):
            rows = pl.ds(pl.multiple_of(i * ROWS, ROWS), ROWS)
            out = pl.ds(pl.multiple_of(at + i * ROWS, ROWS), ROWS)
            total = jnp.zeros((ROWS, 128), F32)
            for k in range(D // 128):
                v = x_ref[rows, k * 128 : k * 128 + 128].astype(F32)
                total = total + v * v
            scale = lax.rsqrt(jnp.sum(total, axis=1, keepdims=True) * (1.0 / D) + EPS)
            for k in range(AHEADS):
                lanes = pl.ds(pl.multiple_of(order_ref[k] * 256, 256), 256)
                u_ref[out, k * 256 : k * 256 + 256] = (
                    x_ref[rows, lanes].astype(F32) * scale * gain_ref[0:1, lanes]
                ).astype(BF)
            return carry

        lax.fori_loop(0, count, step, 0)
        at += x_ref.shape[0]


def whole(shape):
    return pl.BlockSpec(shape, lambda i, s: (0,) * len(shape))


def placed(cols):
    return pl.BlockSpec((TILE, cols), lambda i, s: (s[i], 0))


def params():
    return pltpu.CompilerParams(vmem_limit_bytes=56 * 1024 * 1024)


def onto(earlier, first_input):
    specs = [pl.BlockSpec(memory_space=pl.ANY)] * len(earlier)
    return list(earlier), specs, {first_input + i: i for i in range(len(earlier))}


STATES = pl.BlockSpec((1, STATE, WIDTH), lambda i, s: (s[i], 0, 0))


def ssd_forward(steps, proj, conv_w, conv_b, heads, skip, seg, spread, earlier=()):
    tokens = proj.shape[0]
    count = len(steps)
    more, more_specs, aliases = onto(earlier, 8)
    return pl.pallas_call(
        fwd_kernel,
        grid_spec=pltpu.PrefetchScalarGridSpec(
            num_scalar_prefetch=1,
            grid=(count,),
            in_specs=[
                placed(XCOLS), whole((8, XBC)), whole((8, XBC)), whole((8, 128)), whole((8, WIDTH)),
                whole((128, WIDTH)), whole((128, 128 * LOCAL_HEADS)), *more_specs,
            ],
            out_specs=[placed(WIDTH), placed(XBC), placed(XBC), STATES],
            scratch_shapes=[
                pltpu.VMEM((TILE, 128), F32),
                pltpu.VMEM((SPAN, 128), BF),
                pltpu.VMEM((SPAN, 128), BF),
                pltpu.VMEM((LOCAL_HEADS, 1, SPAN), F32),
                pltpu.VMEM((SPAN, SPAN), F32),
            ],
        ),
        out_shape=[
            jax.ShapeDtypeStruct((tokens, WIDTH), BF),
            jax.ShapeDtypeStruct((tokens, XBC), BF),
            jax.ShapeDtypeStruct((tokens, XBC), BF),
            jax.ShapeDtypeStruct((tokens // TILE, STATE, WIDTH), F32),
        ],
        input_output_aliases=aliases,
        compiler_params=params(),
        cost_estimate=pl.CostEstimate(
            flops=count * 4 * 10**9, bytes_accessed=count * 6 * 10**6, transcendentals=count * 2 * 10**6
        ),
        name="ssd_forward",
    )(jnp.stack(steps).astype(jnp.int32), proj, conv_w, conv_b, heads, skip, seg, spread, *more)


def ssd_backward(steps, proj, act, slope, dy, dz, states, conv_w, conv_b, heads, skip, seg, spread, sofar, earlier=()):
    tokens = proj.shape[0]
    count = len(steps)
    more, more_specs, aliases = onto(earlier, 13)
    return pl.pallas_call(
        bwd_kernel,
        grid_spec=pltpu.PrefetchScalarGridSpec(
            num_scalar_prefetch=1,
            grid=(count,),
            in_specs=[
                placed(XCOLS), placed(XBC), placed(XBC), placed(WIDTH), placed(WIDTH), STATES, whole((8, XBC)),
                whole((8, 128)), whole((8, WIDTH)), whole((128, WIDTH)), whole((128, 128 * LOCAL_HEADS)),
                whole((8, XCOLS)), *more_specs,
            ],
            out_specs=[placed(XCOLS + WIDTH), whole((8, XCOLS))],
            scratch_shapes=[
                pltpu.VMEM((TILE, 128), F32),
                pltpu.VMEM((SPAN, 128), BF),
                pltpu.VMEM((SPAN, 128), BF),
                pltpu.VMEM((LOCAL_HEADS, 1, SPAN), F32),
                pltpu.VMEM((SPAN, SPAN), F32),
                pltpu.VMEM((SPAN, SPAN), F32),
                pltpu.VMEM((SPAN, 128), F32),
                pltpu.VMEM((LOCAL_HEADS, SPAN), F32),
                pltpu.VMEM((SPAN, WIDTH), BF),
                pltpu.VMEM((SPAN, WIDTH), BF),
                pltpu.VMEM((STATE, WIDTH), BF),
                pltpu.VMEM((TILE, XBC), F32),
                pltpu.VMEM((TILE, 128), F32),
                pltpu.VMEM((8, XBC), F32),
                pltpu.VMEM((KERNEL + 1, 8, XBC), F32),
            ],
        ),
        out_shape=[
            jax.ShapeDtypeStruct((tokens, XCOLS + WIDTH), BF),
            jax.ShapeDtypeStruct((8, XCOLS), F32),
        ],
        input_output_aliases=aliases,
        compiler_params=params(),
        cost_estimate=pl.CostEstimate(
            flops=count * 10 * 10**9, bytes_accessed=count * 9 * 10**6, transcendentals=count * 4 * 10**6
        ),
        name="ssd_backward",
    )(jnp.stack(steps).astype(jnp.int32), proj, act, slope, dy, dz, states, conv_w, heads, skip, seg, spread, sofar, *more)


def gate_stats(order, y, z, dn, gain):
    steps = y.shape[0] // TILE
    block = pl.BlockSpec((TILE, WIDTH), lambda i, o: (i, 0))
    return pl.pallas_call(
        stats_kernel,
        grid_spec=pltpu.PrefetchScalarGridSpec(
            num_scalar_prefetch=1,
            grid=(steps,),
            in_specs=[block, block, block, whole((8, WIDTH))],
            out_specs=pl.BlockSpec((8, TILE), lambda i, o: (0, i)),
            scratch_shapes=[pltpu.VMEM((TILE, 128), F32)],
        ),
        out_shape=jax.ShapeDtypeStruct((8, y.shape[0]), F32),
        compiler_params=params(),
        cost_estimate=pl.CostEstimate(flops=3 * 10**9, bytes_accessed=16 * 10**6, transcendentals=3 * 10**6),
        name="gate_stats",
    )(order, y, z, dn, gain)


def gate_backward(order, st, y, z, dn, gain):
    steps = y.shape[0] // TILE
    block = pl.BlockSpec((TILE, WIDTH), lambda i, o: (i, 0))
    return pl.pallas_call(
        gate_kernel,
        grid_spec=pltpu.PrefetchScalarGridSpec(
            num_scalar_prefetch=1,
            grid=(steps,),
            in_specs=[pl.BlockSpec((8, TILE), lambda i, o: (0, i)), block, block, block, whole((8, WIDTH))],
            out_specs=[block, block, block],
            scratch_shapes=[pltpu.VMEM((TILE, 128), F32)],
        ),
        out_shape=[jax.ShapeDtypeStruct(y.shape, BF)] * 3,
        compiler_params=params(),
        cost_estimate=pl.CostEstimate(flops=6 * 10**9, bytes_accessed=32 * 10**6, transcendentals=3 * 10**6),
        name="gate_backward",
    )(order, st, y, z, dn, gain)


def norm_tokens(order, values, gain):
    rows = sum(v.shape[0] for v in values)
    return pl.pallas_call(
        functools.partial(norm_kernel, len(values)),
        grid_spec=pltpu.PrefetchScalarGridSpec(
            num_scalar_prefetch=1,
            grid=(1,),
            in_specs=[*(whole(v.shape) for v in values), whole((8, D))],
            out_specs=[whole((rows, D))],
        ),
        out_shape=[jax.ShapeDtypeStruct((rows, D), BF)],
        compiler_params=params(),
        cost_estimate=pl.CostEstimate(flops=rows * 10**6, bytes_accessed=rows * 8192, transcendentals=rows),
        name="norm_tokens",
    )(order, *values, gain)[0]


def pack_kernel(at_ref, in_ref, dt_ref, small_ref, send_ref, keep_ref, z_send_ref, z_keep_ref):
    rows = in_ref.shape[0]
    send_ref[:, rows:, :] = jnp.zeros((2, 8, XCOLS), BF)
    send_ref[0, rows:, :] = small_ref[...]
    source = lax.broadcasted_iota(jnp.int32, (HEADS, 128), 0)
    lane = lax.broadcasted_iota(jnp.int32, (HEADS, 128), 1)
    for x_ref, z_ref, x in ((send_ref, z_send_ref, 1 - at_ref[0]), (keep_ref, z_keep_ref, at_ref[0])):
        for core in range(2):
            slot = 2 * core + x
            for k in range(AHEADS):
                cols = slice(k * 128, k * 128 + 128)
                at = (k * SLOTS + slot) * 128
                z_ref[core, :, cols] = in_ref[:, pl.ds(pl.multiple_of(at, 128), 128)]
                x_ref[core, :rows, cols] = in_ref[:, pl.ds(pl.multiple_of(DI + at, 128), 128)]
            x_ref[core, :rows, WIDTH:XBC] = in_ref[:, 2 * DI :]
            wanted = jnp.where(lane < LOCAL_HEADS, (lane // 2) * 8 + slot * 2 + lane % 2, -1)
            x_ref[core, :rows, XBC:XCOLS] = nn(
                dt_ref[...], jnp.where(source == wanted, 1.0, 0.0).astype(BF)
            ).astype(BF)


def pack_weights(xi, in_w, dt_w, small):
    rows = in_w.shape[0]
    small = pad_rows(pad_cols(small[None], XCOLS))
    shapes = [(2, rows + 8, XCOLS), (2, rows, XCOLS), (2, rows, WIDTH), (2, rows, WIDTH)]
    return pl.pallas_call(
        pack_kernel,
        in_specs=[pl.BlockSpec(memory_space=pltpu.SMEM)] + [pl.BlockSpec(memory_space=pltpu.VMEM)] * 3,
        out_specs=[pl.BlockSpec(memory_space=pltpu.VMEM)] * 4,
        out_shape=[jax.ShapeDtypeStruct(shape, BF) for shape in shapes],
        cost_estimate=pl.CostEstimate(flops=10**8, bytes_accessed=3 * 10**6, transcendentals=0),
        name="pack_weights",
    )(xi[None].astype(jnp.int32), in_w, dt_w, small)


def pair_kernel(at_ref, keep_ref, got_ref, send_ref, stay_ref):
    rows = keep_ref.shape[1]
    mine = pl.ds(pl.multiple_of(at_ref[0] * rows, rows), rows)
    other = pl.ds(pl.multiple_of((1 - at_ref[0]) * rows, rows), rows)
    for out, core in ((send_ref, 1 - at_ref[1]), (stay_ref, at_ref[1])):
        out[mine, :] = keep_ref[core]
        out[other, :] = got_ref[core, :rows]


def pair_rows(xi, ci, keep, got):
    shape = (2 * keep.shape[1], keep.shape[2])
    return pl.pallas_call(
        pair_kernel,
        in_specs=[pl.BlockSpec(memory_space=pltpu.SMEM)] + [pl.BlockSpec(memory_space=pltpu.VMEM)] * 2,
        out_specs=[pl.BlockSpec(memory_space=pltpu.VMEM)] * 2,
        out_shape=[jax.ShapeDtypeStruct(shape, BF)] * 2,
        cost_estimate=pl.CostEstimate(flops=0, bytes_accessed=2 * 10**6, transcendentals=0),
        name="pair_rows",
    )(jnp.stack([xi, ci]).astype(jnp.int32), keep, got)


def place_kernel(at_ref, stay_ref, got_ref, out_ref):
    rows = stay_ref.shape[0]
    for index, ref in ((at_ref[0], stay_ref), (1 - at_ref[0], got_ref)):
        out_ref[pl.ds(pl.multiple_of(index * rows, rows), rows), :] = ref[...]


def place_rows(index, stay, got):
    return pl.pallas_call(
        place_kernel,
        in_specs=[pl.BlockSpec(memory_space=pltpu.SMEM)] + [pl.BlockSpec(memory_space=pltpu.VMEM)] * 2,
        out_specs=pl.BlockSpec(memory_space=pltpu.VMEM),
        out_shape=jax.ShapeDtypeStruct((2 * stay.shape[0], stay.shape[1]), BF),
        cost_estimate=pl.CostEstimate(flops=0, bytes_accessed=2 * 10**6, transcendentals=0),
        name="place_rows",
    )(index[None].astype(jnp.int32), stay, got)


def assemble_kernel(at_ref, pz_ref, gz_ref, px_ref, gx_ref, in_ref, dt_ref, out_ref, dt_out_ref, sum_ref):
    rows = in_ref.shape[0]
    total = jnp.zeros((rows, 128), F32)
    shared = [jnp.zeros((rows, 128), F32), jnp.zeros((rows, 128), F32)]
    dt_total = jnp.zeros((rows, HEADS), F32)
    lane = lax.broadcasted_iota(jnp.int32, (128, HEADS), 0)
    place = lax.broadcasted_iota(jnp.int32, (128, HEADS), 1)
    for core in range(2):
        for mine in (True, False):
            x = at_ref[0] if mine else 1 - at_ref[0]
            slot = 2 * core + x
            z_of = (lambda cols: pz_ref[core, x, :, cols]) if mine else (lambda cols: gz_ref[core, :, cols])
            x_of = (lambda cols: px_ref[core, x, :, cols]) if mine else (lambda cols: gx_ref[core, :, cols])
            for k in range(AHEADS):
                cols = slice(k * 128, k * 128 + 128)
                at = (k * SLOTS + slot) * 128
                for value, start in ((z_of(cols), at), (x_of(cols), DI + at)):
                    lanes = pl.ds(pl.multiple_of(start, 128), 128)
                    value = value.astype(F32)
                    out_ref[:, lanes] = value
                    total = total + value * in_ref[:, lanes].astype(F32)
            for k in range(2):
                shared[k] = shared[k] + x_of(slice(WIDTH + k * 128, WIDTH + k * 128 + 128)).astype(F32)
            wanted = jnp.where(lane < LOCAL_HEADS, (lane // 2) * 8 + slot * 2 + lane % 2, -1)
            dt_total = dt_total + nn(x_of(slice(XBC, XCOLS)), jnp.where(place == wanted, 1.0, 0.0).astype(BF))
    for k in range(2):
        cols = slice(2 * DI + k * 128, 2 * DI + k * 128 + 128)
        out_ref[:, cols] = shared[k]
        total = total + shared[k] * in_ref[:, cols].astype(F32)
    dt_out_ref[...] = dt_total
    rows_sum = jnp.sum(total, axis=1, keepdims=True) + jnp.sum(
        dt_total * dt_ref[...].astype(F32), axis=1, keepdims=True
    )
    sum_ref[...] = jnp.broadcast_to(rows_sum, (rows, 128))


def assemble_rows(xi, z_pair, z_got, x_pair, x_got, in_w, dt_w):
    rows = in_w.shape[0]
    return pl.pallas_call(
        assemble_kernel,
        in_specs=[pl.BlockSpec(memory_space=pltpu.SMEM)] + [pl.BlockSpec(memory_space=pltpu.VMEM)] * 6,
        out_specs=[pl.BlockSpec(memory_space=pltpu.VMEM)] * 3,
        out_shape=[
            jax.ShapeDtypeStruct(in_w.shape, F32),
            jax.ShapeDtypeStruct(dt_w.shape, F32),
            jax.ShapeDtypeStruct((rows, 128), F32),
        ],
        cost_estimate=pl.CostEstimate(flops=10**7, bytes_accessed=5 * 10**6, transcendentals=0),
        name="assemble_rows",
    )(xi[None].astype(jnp.int32), z_pair, z_got, x_pair, x_got, in_w, dt_w)


def small_kernel(at_ref, own_ref, x_ref, far_ref, taps_ref, heads_ref):
    xi, ci = at_ref[0], at_ref[1]
    terms = (
        (2 * ci + xi, own_ref), (2 * ci + 1 - xi, x_ref),
        (2 - 2 * ci + xi, far_ref.at[0]), (3 - 2 * ci - xi, far_ref.at[1]),
    )
    shared = jnp.zeros((8, 2 * STATE), F32)
    heads = jnp.zeros((8, HEADS), F32)
    source = lax.broadcasted_iota(jnp.int32, (128, HEADS), 0)
    place = lax.broadcasted_iota(jnp.int32, (128, HEADS), 1)
    row = lax.broadcasted_iota(jnp.int32, (8, 1), 0)
    exact = functools.partial(
        lax.dot_general,
        dimension_numbers=(((1,), (0,)), ((), ())),
        precision=lax.Precision.HIGHEST,
        preferred_element_type=F32,
    )
    for slot, ref in terms:
        for k in range(AHEADS):
            cols = ref[:, k * 128 : k * 128 + 128]
            taps_ref[:, pl.ds(pl.multiple_of((k * SLOTS + slot) * 128, 128), 128)] = cols
            wanted = jnp.where(place == k * 8 + slot * 2 + source // HEAD_DIM, 1.0, 0.0)
            heads = heads + exact(jnp.where(row == 5, cols, 0.0), wanted)
        shared = shared + ref[:, WIDTH:XBC]
        wanted = jnp.where(
            (source < LOCAL_HEADS) & (place == (source // 2) * 8 + slot * 2 + source % 2), 1.0, 0.0
        )
        heads = heads + exact(jnp.where(row < 2, ref[:, XBC:], 0.0), wanted)
    taps_ref[:, DI:] = shared
    heads_ref[...] = heads


def assemble_small(xi, ci, own, x, far):
    return pl.pallas_call(
        small_kernel,
        in_specs=[pl.BlockSpec(memory_space=pltpu.SMEM)] + [pl.BlockSpec(memory_space=pltpu.VMEM)] * 3,
        out_specs=[pl.BlockSpec(memory_space=pltpu.VMEM)] * 2,
        out_shape=[jax.ShapeDtypeStruct((8, DI + 2 * STATE), F32), jax.ShapeDtypeStruct((8, HEADS), F32)],
        cost_estimate=pl.CostEstimate(flops=10**7, bytes_accessed=10**6, transcendentals=0),
        name="assemble_small",
    )(jnp.stack([xi, ci]).astype(jnp.int32), own, x, far)


def rows_kernel(order_ref, *refs):
    rows = refs[0].shape[0]
    out_ref = refs[-1]
    for k, (ref, shift) in enumerate(zip(refs[:-1], (0, 0, 0, 0, 0, rows // 2, 0, 0, 0))):
        at = order_ref[k if k < 5 else k - 1] * rows + shift
        out_ref[pl.ds(pl.multiple_of(at, rows // 2), ref.shape[0]), :] = ref[...]


def ordered_rows(order, blocks):
    rows, cols = blocks[0].shape
    return pl.pallas_call(
        rows_kernel,
        in_specs=[pl.BlockSpec(memory_space=pltpu.SMEM)] + [pl.BlockSpec(memory_space=pltpu.VMEM)] * len(blocks),
        out_specs=pl.BlockSpec(memory_space=pltpu.VMEM),
        out_shape=jax.ShapeDtypeStruct((AHEADS * rows, cols), BF),
        compiler_params=params(),
        cost_estimate=pl.CostEstimate(flops=0, bytes_accessed=8 * 10**6, transcendentals=0),
        name="ordered_rows",
    )(order, *blocks)


def swap_x(v):
    return lax.ppermute(v, "x", SWAP)


def swap_core(v):
    return lax.ppermute(v, "core", SWAP)


def pick(v, index, axis=0):
    return lax.dynamic_index_in_dim(v, index, axis, keepdims=False)


def joined(index, mine, other, axis):
    return jnp.where(
        index == 0,
        jnp.concatenate([mine, other], axis=axis),
        jnp.concatenate([other, mine], axis=axis),
    )


def from_slots(v):
    slots, rows, cols = v.shape
    return (
        v.reshape(slots, rows, AHEADS, cols // AHEADS)
        .transpose(1, 2, 0, 3)
        .reshape(rows, slots * cols)
    )


class Return:
    def __init__(self, block):
        self.xi, self.ci = lax.axis_index("x"), lax.axis_index("core")
        self.rows = block.shape[0] // 4
        self.halves = block.astype(BF).reshape(2, 2 * self.rows, -1)
        self.flying = swap_core(pick(self.halves, 1 - self.ci))

    def turn(self, chain):
        got = chain.take(self.flying)
        pair = joined(self.ci, pick(self.halves, self.ci)[None], got[None], 0)
        self.pair = pair.reshape(2, 2, self.rows, -1)
        self.flying = swap_x(pick(self.pair, 1 - self.xi, 1))

    def land(self, chain):
        self.got = chain.take(self.flying)


class Chain:
    def __init__(self):
        self.last = ()

    def tie(self, value):
        return lax.optimization_barrier((value, self.last))[0]

    def mark(self, value):
        self.last = value
        return value

    def take(self, value):
        return self.mark(self.tie(value))


class Ring:
    def __init__(self):
        self.size = len(CYCLE)
        place = [CYCLE.index(i) for i in range(self.size)]
        position = jnp.asarray(place, jnp.int32)[lax.axis_index("ra")]
        cycle = jnp.asarray(CYCLE, jnp.int32)
        steps = jnp.arange(self.size, dtype=jnp.int32)
        self.order = cycle[(position + steps) % self.size]
        self.inverse = (jnp.asarray(place, jnp.int32) - position) % self.size

    def pairs(self, d):
        return [(CYCLE[i], CYCLE[(i + d) % self.size]) for i in range(self.size)]

    def right(self, v):
        return lax.ppermute(v, "ra", self.pairs(1))

    def left(self, v):
        return lax.ppermute(v, "ra", self.pairs(-1))


class Gather:
    def __init__(self, ring, block):
        self.ring = ring
        self.rights, self.lefts = [block], [block]

    def start(self):
        r, l = self.rights[-1], self.lefts[-1]
        if len(self.rights) == 4:
            half = r.shape[0] // 2
            r, l = r[:half], l[half:]
        self.flying = self.ring.right(r), self.ring.left(l)

    def land(self, chain):
        r, l = chain.take(self.flying)
        self.rights.append(r)
        self.lefts.append(l)

    def pieces(self):
        r, l = self.rights, self.lefts
        return [r[0], l[1], l[2], l[3], r[4], l[4], r[3], r[2], r[1]]


class Scatter:
    def __init__(self, ring, block, chain):
        self.ring, self.block, self.chain, self.count = ring, block, chain, 0

    def start(self):
        block, ring, k = self.block, self.ring, self.count
        self.count += 1
        if k == 0:
            far = block(4)
            half = far.shape[0] // 2
            sends = far[:half], far[half:]
        elif k == 1:
            up, down = block(3), block(5)
            half = up.shape[0] // 2
            r, l = self.right.astype(F32), self.left.astype(F32)
            sends = (
                jnp.concatenate([up[:half] + r, up[half:]], axis=0),
                jnp.concatenate([down[:half], down[half:] + l], axis=0),
            )
        else:
            sends = block(4 - k) + self.right.astype(F32), block(4 + k) + self.left.astype(F32)
        sends = self.chain.mark((sends[0].astype(BF), sends[1].astype(BF)))
        self.flying = ring.right(sends[0]), ring.left(sends[1])

    def land(self, chain):
        self.right, self.left = chain.take(self.flying)

    def total(self):
        return self.block(0) + self.right.astype(F32) + self.left.astype(F32)


def flat_index(sizes):
    index = 0
    for name, size in zip(ALL, sizes):
        index = index * size + lax.axis_index(name)
    return index


class SmallSum:
    def __init__(self, v):
        self.value = v
        self.bits = [1, 2, 4]

    def start(self):
        bit = self.bits.pop(0)
        self.flying = lax.ppermute(self.value, "ra", [(i, i ^ bit) for i in range(len(CYCLE))])

    def land(self, chain):
        self.value = chain.mark(self.value + chain.take(self.flying))


def permute_blocks(v, order, width):
    return jnp.concatenate(
        [
            lax.dynamic_slice(v, (0, order[k] * width), (v.shape[0], width))
            for k in range(v.shape[1] // width)
        ],
        axis=1,
    )


def pad_rows(v, rows=8):
    return jnp.concatenate([v, jnp.zeros((rows - v.shape[0], v.shape[1]), v.dtype)], axis=0)


def pad_cols(v, cols):
    return jnp.concatenate([v, jnp.zeros(v.shape[:-1] + (cols - v.shape[-1],), v.dtype)], axis=-1)


def per_device(
    sizes, tokens_short, tokens_long, cot_short, cot_long, seq_lengths,
    norm_gain, in_w, dt_w, conv_w, conv_b, dt_bias, a_log, d_skip, gate_gain, out_w,
):
    ringed = sizes == (8, 2, 1, 2)
    short, long = tokens_short.shape[0], tokens_long.shape[0]
    xi, ci = lax.axis_index("x"), lax.axis_index("core")
    slot = ci * 2 + xi
    feature = D // AHEADS
    mine_cols = lambda v: pick(v.reshape(v.shape[0], AHEADS, SLOTS, -1), slot, 2).reshape(v.shape[0], -1)
    chain = Chain()

    if ringed:
        ring = Ring()
        order, inverse = ring.order, ring.inverse
        from_ring = lambda v: permute_blocks(v, inverse, feature)
    else:
        order = jnp.arange(AHEADS, dtype=jnp.int32)
        from_ring = lambda v: v

    width = conv_w.shape[1]
    pieces = [conv_w.reshape(-1), conv_b, norm_gain, gate_gain]
    ends = np.cumsum([0] + [p.shape[0] for p in pieces])
    small = jnp.concatenate(pieces)
    group = ("core", "x")
    everyone = lambda v: lax.all_gather(v, group, axis=0, tiled=True)

    def stage(v, bit):
        count = int(np.prod(sizes))
        return lax.ppermute(v, ALL, [(i, i ^ bit) for i in range(count)])

    def widen(v, got, bit):
        return joined((flat_index(sizes) // bit) % 2, v, got, 0)

    if ringed:
        rows, n = in_w.shape[0], small.shape[0]
        x_send, x_keep, z_send, z_keep = chain.mark(pack_weights(xi, in_w, dt_w, small))
        x_got = chain.take(swap_x(x_send))
        small = widen(small[None], x_got[0, rows : rows + 1, :n], 1)
        passing = stage(small, 2)
        send, stay = chain.mark(pair_rows(xi, ci, x_keep, x_got))
        got = swap_core(send)
        small = widen(small, chain.take(passing), 2)
        passing = stage(small, 4)
        got = chain.take(got)
        small = widen(small, chain.take(passing), 4)
        passing = stage(small, 8)
        x_block = chain.mark(place_rows(ci, stay, got))
        small = widen(small, chain.take(passing), 8)
        small = widen(small, chain.take(stage(small, 16)), 16)
        gather_x = Gather(ring, chain.tie(x_block))
        gather_x.start()
        z_got = swap_x(chain.tie(z_send))
    else:
        small = lax.all_gather(small[None], ALL, axis=0, tiled=True)
    norm_full = pad_rows(small[:, ends[2] : ends[3]].reshape(1, -1).astype(F32))
    u_own = chain.mark(norm_tokens(order, [chain.tie(tokens_short), tokens_long], norm_full))
    xh = everyone(u_own)
    if ringed:
        gather_x.land(chain)
        gather_x.start()

    small, dt_bias, a_log, d_skip, cot_s, cot_l = chain.mark(
        chain.tie((small, dt_bias, a_log, d_skip, cot_short, cot_long))
    )
    live_s = (jnp.arange(short) < seq_lengths[0, 0]).astype(F32)[:, None]
    live_l = (jnp.arange(long) < seq_lengths[1, 0]).astype(F32)[:, None]
    dv_own = chain.mark(jnp.concatenate([(live_s * cot_s).astype(BF), (live_l * cot_l).astype(BF)], axis=0))
    taps = small[:, : ends[2]].reshape(-1, KERNEL + 1, width)
    taps = taps.transpose(1, 0, 2).reshape(KERNEL + 1, -1).astype(F32)
    taps = jnp.concatenate([mine_cols(taps[:, :DI]), taps[:, DI:]], axis=1)
    conv_taps, conv_bias = pad_rows(taps[:KERNEL]), pad_rows(taps[KERNEL:])
    gate_mine = pad_rows(mine_cols(small[:, ends[3] :].reshape(1, -1).astype(F32)))
    neg_rate = -jnp.exp(a_log.astype(F32))
    heads = pad_rows(pad_cols(mine_cols(jnp.stack([dt_bias.astype(F32), neg_rate])), 128))
    skip = pad_rows(jnp.repeat(mine_cols(d_skip.astype(F32)[None]), HEAD_DIM, axis=1))
    head_rows = np.arange(128)[:, None]
    seg = jnp.asarray(
        (head_rows < 2 * LOCAL_HEADS) & (head_rows % LOCAL_HEADS == np.arange(WIDTH)[None, :] // HEAD_DIM), BF
    )
    spread = jnp.asarray(
        (head_rows < 3 * LOCAL_HEADS)
        & (head_rows % LOCAL_HEADS == np.arange(128 * LOCAL_HEADS)[None, :] // 128),
        BF,
    )
    gate_mine, *seq_params = chain.mark((gate_mine, conv_taps, conv_bias, heads, skip, seg, spread))
    if ringed:
        send, stay = chain.mark(pair_rows(xi, ci, z_keep, chain.take(z_got)))
        z_block = chain.mark(place_rows(ci, stay, chain.take(swap_core(send))))
    slots = [jnp.int32(k) for k in range(SLOTS)]

    if ringed:
        gather_x.land(chain)
        gather_x.start()
        gather_x.land(chain)
        gather_x.start()
        gather_z = Gather(ring, z_block)
        gather_z.start()
        gather_z.land(chain)
        gather_x.land(chain)
        w_x = chain.mark(jnp.concatenate(gather_x.pieces(), axis=0))
        xh = chain.take(xh)
        dv = everyone(chain.tie(dv_own))
        gather_z.start()
        gather_o = Gather(ring, chain.tie(out_w))
        gather_o.start()
        both = gather_o, gather_z
        proj = chain.mark(nn(chain.tie(xh), w_x))
        for gather in both:
            gather.land(chain)
            gather.start()
        kept = chain.mark(ssd_forward(slots[:2], chain.tie(proj), *seq_params))
        for gather in both:
            gather.land(chain)
            gather.start()
        y, act, slope, states = chain.mark(ssd_forward(slots[2:], chain.tie(proj), *seq_params, earlier=kept))
        for gather in both:
            gather.land(chain)
        gather_o.start()
        w_all = chain.mark(jnp.concatenate([w_x, jnp.concatenate(gather_z.pieces(), axis=0)], axis=1))
        z = chain.mark(nn(chain.tie(xh), w_all[:, XCOLS:]).astype(BF))
        gather_o.land(chain)
        w_o = chain.mark(ordered_rows(order, chain.tie(gather_o.pieces())))
        dv = chain.take(dv)
        dn = chain.mark(nt(dv, w_o).astype(BF))
    else:
        full = lax.all_gather(in_w, ALL, axis=0, tiled=True)
        full_dt = lax.all_gather(dt_w, ALL, axis=0, tiled=True)
        full_out = lax.all_gather(out_w, ALL, axis=0, tiled=True)
        w_z = mine_cols(full[:, :DI])
        w_x = jnp.concatenate(
            [mine_cols(full[:, DI : 2 * DI]), full[:, 2 * DI :], pad_cols(mine_cols(full_dt), 128)], axis=-1
        )
        w_o = pick(full_out.reshape(AHEADS, SLOTS, 128, D), slot, 1).reshape(WIDTH, D)
        dv = everyone(dv_own)
        proj = nn(xh, w_x)
        y, act, slope, states = ssd_forward(slots, proj, *seq_params)
        dn = nt(dv, w_o).astype(BF)
        z = nn(xh, w_z).astype(BF)
        w_all = jnp.concatenate([w_x, w_z], axis=1)

    straight = jnp.arange(AHEADS, dtype=jnp.int32)
    st = chain.mark(gate_stats(straight, y, chain.tie(z), dn, gate_mine))
    st = st + swap_core(st)
    st = st + swap_x(st)
    n, dy, dz = chain.mark(gate_backward(straight, st, y, z, dn, gate_mine))

    own = short + long
    rows_of = lambda v, start, count: lax.dynamic_slice(v, (start * own, 0), (count * own, v.shape[1]))

    def unit_product(dx, start, count):
        dx = chain.tie(dx)
        return nt(rows_of(dx, start, count), w_all)

    def backward_call(steps, sofar, earlier):
        return chain.mark(
            ssd_backward(steps, chain.tie(proj), act, slope, dy, dz, states, *seq_params, sofar, earlier=earlier)
        )

    none_yet = jnp.zeros((8, XCOLS), F32)

    far, mid = 2 * (1 - ci), 2 * ci + 1 - xi
    g_out = chain.mark(tn(n, dv).astype(BF))
    reduced = lambda v, axes: lax.psum_scatter(v, axes, scatter_dimension=0, tiled=True)
    if ringed:
        own_out = reduced(g_out, "ra").astype(F32)
        g_z = chain.mark(tn(chain.tie(xh), dz).astype(BF))
        blocks_z = g_z.reshape(AHEADS, -1, WIDTH)
        scatter_z = Scatter(ring, lambda k: blocks_z[k], chain)
        scatter_z.start()
    else:
        g_z = tn(xh, dz)
    branch = chain.mark(nn(chain.tie(n), w_o).astype(BF))
    branch = reduced(branch, group)
    if ringed:
        scatter_z.land(chain)
        scatter_z.start()
        dx, acc = backward_call([far, far + 1], none_yet, ())
        scatter_z.land(chain)
        scatter_z.start()
        far_u = swap_core(chain.mark(unit_product(dx, far, 2).astype(BF)))
        dx, acc = backward_call([mid], acc, (chain.tie(dx),))
        scatter_z.land(chain)
        scatter_z.start()
        far_u = chain.take(far_u)
        mid_u = chain.mark(
            (unit_product(dx, mid, 1) + rows_of(far_u, 1 - xi, 1).astype(F32)).astype(BF)
        )
        mid_u = swap_x(mid_u)
        dx, acc = backward_call([slot], acc, (chain.tie(dx),))
        scatter_z.land(chain)
        back_z = Return(chain.mark(scatter_z.total()))

        def blocks_x(first, last):
            part = tn(xh[:, first * feature : last * feature], chain.tie(dx)[:, :XCOLS]).astype(BF)
            return dict(enumerate(chain.mark(part).reshape(last - first, feature, XCOLS), first))

        made = blocks_x(4, 5)
        scatter_x = Scatter(ring, lambda k: made[k], chain)
        scatter_x.start()
        tally = SmallSum(chain.tie(acc))
        tally.start()
        made.update(blocks_x(3, 4))
        made.update(blocks_x(5, 6))
        scatter_x.land(chain)
        tally.land(chain)
        scatter_x.start()
        tally.start()
        made.update(blocks_x(0, 3))
        made.update(blocks_x(6, 8))
        scatter_x.land(chain)
        tally.land(chain)
        scatter_x.start()
        tally.start()
        back_z.turn(chain)
        du_own = unit_product(dx, slot, 1) + rows_of(far_u, xi, 1).astype(F32)
        du_own = chain.mark(lax.optimization_barrier(du_own))
        scatter_x.land(chain)
        tally.land(chain)
        scatter_x.start()
        mid_u = chain.take(mid_u)
        du = chain.mark(du_own + mid_u.astype(F32))
        scatter_x.land(chain)
        back_x = Return(chain.mark(scatter_x.total()))
        acc = tally.value
        acc_x = swap_x(acc)
        back_z.land(chain)
        back_x.turn(chain)
        acc_x = chain.take(acc_x)
        acc_far = chain.take(swap_core(jnp.stack([acc, acc_x])))
        taps_total, head_total = chain.mark(assemble_small(xi, ci, acc, acc_x, acc_far))
        own_conv = lax.dynamic_slice(taps_total, (0, flat_index(sizes) * width), (KERNEL + 1, width))
    else:
        dx, acc = backward_call(slots, none_yet, ())
        du = reduced(nt(dx, w_all), group)
        g_x = tn(xh, dx[:, :XCOLS])
        acc = lax.psum(acc, ("ra", "rb"))
        acc_x = swap_x(acc)
        acc_far = swap_core(jnp.stack([acc, acc_x]))
        taps_total, head_total = assemble_small(xi, ci, acc, acc_x, acc_far)
        own_conv = lax.dynamic_slice(taps_total, (0, flat_index(sizes) * width), (KERNEL + 1, width))
    v_s, v_l = branch[:short].astype(F32), branch[short:].astype(F32)
    du_s, du_l = du[:short], du[short:]

    out_short = (tokens_short.astype(F32) + live_s * v_s).astype(BF)
    out_long = (tokens_long.astype(F32) + live_l * v_l).astype(BF)

    def token_grad(token, cot, d_u):
        residual = token.astype(F32)
        row_scale = lax.rsqrt(jnp.mean(residual * residual, axis=-1, keepdims=True) + EPS)
        unit = residual * row_scale
        d_norm = from_ring(d_u) * norm_full[0:1]
        return cot.astype(F32) + row_scale * (d_norm - unit * jnp.mean(d_norm * unit, axis=-1, keepdims=True))

    grad_short, grad_long = chain.mark(
        (token_grad(tokens_short, cot_short, du_s), token_grad(tokens_long, cot_long, du_l))
    )

    if ringed:
        back_x.land(chain)
        grad_in_w, grad_dt_w, norm_sum = chain.mark(
            assemble_rows(xi, back_z.pair, back_z.got, back_x.pair, back_x.got, in_w, dt_w)
        )
        norm_sum = norm_sum[:, 0]
    else:
        here = (jnp.arange(SLOTS) == slot).astype(F32)
        wider = lambda v: (v.reshape(D, AHEADS, 1, -1) * here[:, None]).reshape(D, -1)
        reduce = lambda v: lax.psum_scatter(v, ALL, scatter_dimension=0, tiled=True)
        grad_in_w = reduce(
            jnp.concatenate([wider(g_z), wider(g_x[:, :WIDTH]), g_x[:, WIDTH:XBC]], axis=1)
        )
        grad_dt_w = reduce(wider(g_x[:, XBC : XBC + LOCAL_HEADS]))
        own_out = reduce(
            (g_out.astype(F32).reshape(AHEADS, 1, 128, D) * here[:, None, None]).reshape(DI, D)
        )

        norm_sum = jnp.sum(in_w.astype(F32) * grad_in_w, axis=1) + jnp.sum(dt_w.astype(F32) * grad_dt_w, axis=1)

    grad_norm_gain = norm_sum / norm_gain.astype(F32)
    grad_gate_gain = jnp.sum(out_w.astype(F32) * own_out, axis=1) / gate_gain.astype(F32)

    return (
        out_short,
        out_long,
        grad_short,
        grad_long,
        grad_norm_gain,
        grad_in_w,
        grad_dt_w,
        own_conv[:KERNEL],
        own_conv[KERNEL],
        head_total[0],
        head_total[1] * neg_rate,
        head_total[5],
        grad_gate_gain,
        own_out,
    )


def solution(mesh):
    wide, narrow = mesh.shape["wide"], mesh.shape["narrow"]
    sizes = (wide // 2, 2, narrow // 2, 2)
    split = Mesh(mesh.devices.reshape(sizes), ALL)
    rows, vector, columns = P(ALL, None), P(ALL), P(None, ALL)
    return jax.shard_map(
        functools.partial(per_device, sizes),
        mesh=split,
        in_specs=(
            rows, rows, rows, rows, columns, vector, rows, rows, columns, vector, P(), P(), P(), vector, rows,
        ),
        out_specs=(
            rows, rows, rows, rows, vector, rows, rows, columns, vector, P(), P(), P(), vector, rows,
        ),
        check_vma=False,
    )
```
